32 devices in a mesh: tower: 2 (over core), blk: 8 (over z, x), seq: 2 (over y).
Axes of the slice: x: 2, y: 2, z: 4, core: 2. Of those that a mesh axis runs over, the one named last changes fastest.
Arguments:
- queries: bfloat16 [2, 2048, 1024], P('tower', ('blk', 'seq')), may hold values from -6 to 6
- key_rows: bfloat16 [2, 2048, 1024], P('tower', ('blk', 'seq')), may hold values from -6 to 6
- value_rows: bfloat16 [2, 2048, 1024], P('tower', ('blk', 'seq')), may hold values from -6 to 6
- cross_queries: bfloat16 [2, 2048, 1024], P('tower', ('blk', 'seq')), may hold values from -6 to 6
- cross_keys: bfloat16 [2, 2048, 1024], P('tower', ('blk', 'seq')), may hold values from -6 to 6
- cross_values: bfloat16 [2, 2048, 1024], P('tower', ('blk', 'seq')), may hold values from -6 to 6
- grad_out: bfloat16 [2, 2048, 1024], P('tower', ('blk', 'seq')), may hold values from -6 to 6
- offsets: int32 [2, 8], replicated, may hold values from -127 to 127, as said below
- key_valid: int32 [2, 2048], P(None, ('blk', 'seq')), may hold values from 0 to 1, as said below
Outputs:
- attended: bfloat16 [2, 2048, 1024], P('tower', ('blk', 'seq'))
- grad_queries: bfloat16 [2, 2048, 1024], P('tower', ('blk', 'seq'))
- grad_keys: bfloat16 [2, 2048, 1024], P('tower', ('blk', 'seq'))
- grad_values: bfloat16 [2, 2048, 1024], P('tower', ('blk', 'seq'))
- grad_cross_queries: bfloat16 [2, 2048, 1024], P('tower', ('blk', 'seq'))
- grad_cross_keys: bfloat16 [2, 2048, 1024], P('tower', ('blk', 'seq'))
- grad_cross_values: bfloat16 [2, 2048, 1024], P('tower', ('blk', 'seq'))
The draws below stay inside these ranges and needn't reach their ends.
Inputs may be any that keep to these rules, and one draw needn't show every extreme that they name: Both ends of the range occur in every draw; for every block b, offsets[0, b] and offsets[1, b] have opposite signs, and every magnitude is at least 64. `key_valid`: positions k * 256 + 256 // 2 - 1 and k * 256 + 256 // 2 are always 1.
All inputs are finite; a program needn't handle non-finite values.
Results may differ from the reference program's by a relative error of at most 0.019.
Values may be sent and summed in bfloat16 or wider, within the bound.
A program may use at most 128 MiB of HBM per device.

```python
import jax
import jax.numpy as jnp
from jax import lax

HEADS = 16
HEAD = 64
D = 1024
LEN = 2048
BLOCK = 256
NBLOCKS = 8
HALF = 128
QT = 256


def background(key, salt):
    sub_key = jax.random.fold_in(key, salt)
    return jnp.clip(jax.random.normal(sub_key, (2, LEN, HEADS * HEAD), jnp.float32), -4.0, 4.0)


def draw_queries(key, part):
    field = background(key, 1)
    return field.astype(jnp.bfloat16)


def draw_key_rows(key, part):
    field = background(key, 2)
    return field.astype(jnp.bfloat16)


def draw_cross_queries(key, part):
    field = background(key, 3)
    return field.astype(jnp.bfloat16)


def draw_cross_keys(key, part):
    field = background(key, 4)
    return field.astype(jnp.bfloat16)


def draw_offsets(key, part):
    low_mag = max(HALF // 2, 1)
    magnitude = jax.random.randint(key, (2, NBLOCKS), low_mag, HALF)
    sign_first = 2 * jax.random.randint(jax.random.fold_in(key, 7), (NBLOCKS,), 0, 2) - 1
    spots = jax.random.randint(jax.random.fold_in(key, 5), (2,), 0, NBLOCKS)
    sign_first = sign_first.at[spots[0]].set(1).at[spots[1]].set(1)
    magnitude = magnitude.at[0, spots[0]].set(HALF - 1).at[1, spots[1]].set(HALF - 1)
    signs = jnp.stack((sign_first, -sign_first))
    return (signs * magnitude).astype(jnp.int32)


def draw_key_valid(key, part):
    coins = jax.random.randint(key, (2, LEN), 0, 8)
    phase = jnp.arange(LEN) % BLOCK
    keep = (phase == BLOCK // 2 - 1) | (phase == BLOCK // 2)
    return jnp.where(keep[None, :] | (coins > 0), 1, 0).astype(jnp.int32)


def level_of(key, extent, pieces, smallest, high):
    gain, own = 1.0, jax.random.fold_in(key, 6)
    for axis_at, blocks in pieces:
        draws = jnp.exp(jax.random.uniform(jax.random.fold_in(own, axis_at), (blocks,), jnp.float32, smallest / len(pieces), high / len(pieces)))
        gain = gain * jnp.repeat(draws, extent[axis_at] // blocks).reshape([-1 if axis == axis_at else 1 for axis in range(len(extent))])
    return gain


def gaussian(key, extent, width, bound, pieces=(), kind=jnp.bfloat16):
    factor_of = level_of(key, extent, pieces, -0.22, 0.18) if pieces else 1.0
    entries = jax.random.normal(key, extent, jnp.float32) * width * factor_of
    return jnp.minimum(jnp.maximum(entries, -bound), bound).astype(kind)


def setup_inputs(seed: int = 0) -> dict:
    splits = jax.random.split(jax.random.key(seed), 10)
    return {
        "queries": draw_queries(jax.random.fold_in(splits[9], 71), 0),
        "key_rows": draw_key_rows(jax.random.fold_in(splits[9], 71), 0),
        "value_rows": gaussian(splits[2], (2, LEN, D), 1.0, 6.0, ((0, 2), (1, 16))),
        "cross_queries": draw_cross_queries(jax.random.fold_in(splits[9], 71), 0),
        "cross_keys": draw_cross_keys(jax.random.fold_in(splits[9], 71), 0),
        "cross_values": gaussian(splits[5], (2, LEN, D), 1.0, 6.0, ((0, 2), (1, 16))),
        "grad_out": gaussian(splits[6], (2, LEN, D), 1.0, 6.0, ((0, 2), (1, 16))),
        "offsets": draw_offsets(jax.random.fold_in(splits[9], 71), 0),
        "key_valid": draw_key_valid(jax.random.fold_in(splits[9], 71), 0),
    }


def attend(query_tile, grad_tile, key_block, value_block, allowed, heads_here):
    score_scale = HEAD ** -0.5
    rows_count = query_tile.shape[0]
    keys_count = key_block.shape[0]
    q_heads = query_tile.reshape(rows_count, heads_here, HEAD).astype(jnp.float32)
    g_heads = grad_tile.reshape(rows_count, heads_here, HEAD).astype(jnp.float32)
    k_heads = key_block.reshape(keys_count, heads_here, HEAD).astype(jnp.float32)
    v_heads = value_block.reshape(keys_count, heads_here, HEAD).astype(jnp.float32)
    scores = jnp.einsum("qhe,khe->hqk", q_heads, k_heads) * score_scale
    scores = jnp.where(allowed[None], scores, -1e30)
    row_max = jnp.max(scores, axis=2)
    unnormed = jnp.exp(scores - row_max[:, :, None])
    row_sum = jnp.sum(unnormed, axis=2)
    weights = unnormed / row_sum[:, :, None]
    prob_bf = weights.astype(jnp.bfloat16).astype(jnp.float32)
    result = jnp.einsum("hqk,khe->qhe", prob_bf, v_heads).reshape(rows_count, -1)
    grad_probs = jnp.einsum("qhe,khe->hqk", g_heads, v_heads)
    row_dot = jnp.sum(weights * grad_probs, axis=2)
    grad_scores = (weights * (grad_probs - row_dot[:, :, None]) * score_scale).astype(jnp.bfloat16).astype(jnp.float32)
    grad_query = jnp.einsum("hqk,khe->qhe", grad_scores, k_heads).reshape(rows_count, -1)
    grad_key = jnp.einsum("hqk,qhe->khe", grad_scores, q_heads).reshape(keys_count, -1)
    grad_value = jnp.einsum("hqk,qhe->khe", prob_bf, g_heads).reshape(keys_count, -1)
    return result, grad_query, grad_key, grad_value


def reference(queries, key_rows, value_rows, cross_queries, cross_keys, cross_values, grad_out, offsets, key_valid):
    pad_rows = ((HALF, HALF), (0, 0))
    window_span = QT + 2 * HALF
    rows_local = jnp.arange(QT)
    keys_local = jnp.arange(window_span)
    near = jnp.abs(rows_local[:, None] + HALF - keys_local[None, :]) <= HALF
    tiles = jnp.arange(LEN // QT, dtype=jnp.int32)
    zeros_pad = jnp.zeros((LEN + 2 * HALF, HEADS * HEAD), jnp.float32)
    results = []
    cross_key_grads = [None, None]
    cross_value_grads = [None, None]
    for chain in range(2):
        other = 1 - chain
        key_pad = jnp.pad(key_rows[chain], pad_rows)
        value_pad = jnp.pad(value_rows[chain], pad_rows)
        valid_pad = jnp.pad(key_valid[chain], HALF)
        cross_key_pad = jnp.pad(cross_keys[other], pad_rows)
        cross_value_pad = jnp.pad(cross_values[other], pad_rows)
        other_valid = jnp.pad(key_valid[other], HALF)

        def self_step(carry, tile_index):
            grad_key_acc, grad_value_acc = carry
            tile_start = (tile_index * QT).astype(jnp.int32)
            query_tile = lax.dynamic_slice_in_dim(queries[chain], tile_start, QT, 0)
            grad_tile = lax.dynamic_slice_in_dim(grad_out[chain], tile_start, QT, 0)
            key_window = lax.dynamic_slice_in_dim(key_pad, tile_start, window_span, 0)
            value_window = lax.dynamic_slice_in_dim(value_pad, tile_start, window_span, 0)
            allowed = near & (lax.dynamic_slice_in_dim(valid_pad, tile_start, window_span) > 0)[None, :]
            result, grad_query, grad_key, grad_value = attend(query_tile, grad_tile, key_window, value_window, allowed, HEADS)
            grad_key_acc = lax.dynamic_update_slice_in_dim(grad_key_acc, lax.dynamic_slice_in_dim(grad_key_acc, tile_start, window_span, 0) + grad_key, tile_start, 0)
            grad_value_acc = lax.dynamic_update_slice_in_dim(grad_value_acc, lax.dynamic_slice_in_dim(grad_value_acc, tile_start, window_span, 0) + grad_value, tile_start, 0)
            return (grad_key_acc, grad_value_acc), (result, grad_query)

        def cross_step(carry, tile_index):
            grad_key_acc, grad_value_acc = carry
            tile_start = (tile_index * QT).astype(jnp.int32)
            block_index = (tile_start // BLOCK).astype(jnp.int32)
            band_start = (block_index * BLOCK + offsets[chain, block_index] + HALF).astype(jnp.int32)
            query_tile = lax.dynamic_slice_in_dim(cross_queries[chain], tile_start, QT, 0)
            grad_tile = lax.dynamic_slice_in_dim(grad_out[chain], tile_start, QT, 0)
            key_band = lax.dynamic_slice_in_dim(cross_key_pad, band_start, BLOCK, 0)
            value_band = lax.dynamic_slice_in_dim(cross_value_pad, band_start, BLOCK, 0)
            allowed = (lax.dynamic_slice_in_dim(other_valid, band_start, BLOCK) > 0)[None, :]
            result, grad_query, grad_key, grad_value = attend(query_tile, grad_tile, key_band, value_band, allowed, HEADS)
            grad_key_acc = lax.dynamic_update_slice_in_dim(grad_key_acc, lax.dynamic_slice_in_dim(grad_key_acc, band_start, BLOCK, 0) + grad_key, band_start, 0)
            grad_value_acc = lax.dynamic_update_slice_in_dim(grad_value_acc, lax.dynamic_slice_in_dim(grad_value_acc, band_start, BLOCK, 0) + grad_value, band_start, 0)
            return (grad_key_acc, grad_value_acc), (result, grad_query)

        (self_gk, self_gv), (self_out, self_gq) = lax.scan(self_step, (zeros_pad, zeros_pad), tiles)
        (cross_gk, cross_gv), (cross_out, cross_gq) = lax.scan(cross_step, (zeros_pad, zeros_pad), tiles)
        self_out = self_out.reshape(LEN, -1)
        cross_out = cross_out.reshape(LEN, -1)
        attended = (self_out + cross_out).astype(jnp.bfloat16)
        results.append((attended, self_gq.reshape(LEN, -1).astype(jnp.bfloat16), self_gk[HALF:HALF + LEN].astype(jnp.bfloat16), self_gv[HALF:HALF + LEN].astype(jnp.bfloat16), cross_gq.reshape(LEN, -1).astype(jnp.bfloat16)))
        cross_key_grads[other] = cross_gk[HALF:HALF + LEN].astype(jnp.bfloat16)
        cross_value_grads[other] = cross_gv[HALF:HALF + LEN].astype(jnp.bfloat16)
    stacked = [jnp.stack((results[0][slot], results[1][slot])) for slot in range(5)]
    return (stacked[0], stacked[1], stacked[2], stacked[3], stacked[4], jnp.stack(cross_key_grads), jnp.stack(cross_value_grads))
```

```python
import functools

import jax
import jax.numpy as jnp
from jax import lax
from jax.experimental import pallas as pl
from jax.experimental.pallas import tpu as pltpu
from jax.sharding import PartitionSpec as P

HEADS = 16
HEAD = 64
WINDOW = 2048
TILE = 512
LAG = 2
MESH = pl.DeviceIdType.MESH
F32, BF16 = jnp.float32, jnp.bfloat16


def places():
    tower, blk, seq = lax.axis_index("tower"), lax.axis_index("blk"), lax.axis_index("seq")
    peers = dict(
        y=(tower, blk, 1 - seq),
        tower=(1 - tower, blk, seq),
        diag=(1 - tower, blk, 1 - seq),
        low=(tower, blk - 1, seq),
        high=(tower, blk + 1, seq),
    )
    return tower, blk, seq, peers


def greet(blk, blks, peers):
    barrier = pltpu.get_barrier_semaphore()
    for name in ("y", "tower", "diag"):
        pl.semaphore_signal(barrier, inc=1, device_id=peers[name], device_id_type=MESH)

    @pl.when(blk > 0)
    def _():
        pl.semaphore_signal(barrier, inc=1, device_id=peers["low"], device_id_type=MESH)

    @pl.when(blk < blks - 1)
    def _():
        pl.semaphore_signal(barrier, inc=1, device_id=peers["high"], device_id_type=MESH)

    count = 3 + jnp.where(blk > 0, 1, 0) + jnp.where(blk < blks - 1, 1, 0)
    pl.semaphore_wait(barrier, count)


def remote(src, dst, send, recv, device):
    return pltpu.make_async_remote_copy(
        src_ref=src, dst_ref=dst, send_sem=send, recv_sem=recv,
        device_id=device, device_id_type=MESH,
    )


def fused_kernel(
    blks, rows, cols,
    off_ref, q_ref, k_ref, v_ref, cq_ref, ck_ref, cv_ref, g_ref, m_ref,
    o_out, gq_out, gk_out, gv_out, gcq_out, gck_out, gcv_out,
    side, ext, cext, mate, pick, far, mask_ext, bias,
    y_stage, t_stage, low_stage, high_stage, core, recv, part, mate_part, gpick, gfar,
    local_sem, mask_send, mask_recv, in_send, in_recv,
    low_send, low_recv, high_send, high_recv, mate_send, mate_recv, far_send, far_recv,
    out_send, out_recv, glow_send, glow_recv, ghigh_send, ghigh_recv,
    part_send, part_recv, gfar_send, gfar_recv,
):
    tower, blk, seq, peers = places()
    half, wide = rows, 2 * HEAD
    keys, groups = 3 * rows, cols // (2 * HEAD)
    scale = HEAD ** (-0.5)
    has_low, has_high = blk > 0, blk < blks - 1
    here = pl.ds(pl.multiple_of(seq * half, half), half)
    ext_here = pl.ds(pl.multiple_of((1 + seq) * half, half), half)
    mine = pl.ds(pl.multiple_of(seq * cols, cols), cols)
    inner_low, inner_high = pl.ds(half, half), pl.ds(2 * half, half)
    outer_low, outer_high = pl.ds(0, half), pl.ds(3 * half, half)
    direct = [o_out, gq_out, gcq_out]
    grads = [gk_out, gv_out, gck_out, gcv_out]

    off = off_ref[tower, blk]
    off_below = off_ref[tower, jnp.maximum(blk - 1, 0)]
    off_above = off_ref[tower, jnp.minimum(blk + 1, blks - 1)]
    below = off < 0

    def strip(g, base=0):
        return pl.ds(pl.multiple_of(base + g * wide, wide), wide)

    def incoming(g):
        at = strip(g)
        keep, give = strip(g, seq * cols), strip(g, (1 - seq) * cols)
        moves = [
            (k_ref.at[:, give], ext.at[0, ext_here, at], "y"),
            (v_ref.at[:, give], ext.at[1, ext_here, at], "y"),
            (ck_ref.at[:, give], cext.at[0, here, at], "diag"),
            (cv_ref.at[:, give], cext.at[1, here, at], "diag"),
            (ck_ref.at[:, keep], cext.at[0, here, at], "tower"),
            (cv_ref.at[:, keep], cext.at[1, here, at], "tower"),
            (q_ref.at[:, give], side.at[0, here, at], "y"),
            (g_ref.at[:, give], side.at[2, here, at], "y"),
            (cq_ref.at[:, give], side.at[1, here, at], "y"),
        ]
        return [
            remote(src, dst, in_send.at[g, i], in_recv.at[g, i], peers[to])
            for i, (src, dst, to) in enumerate(moves)
        ]

    def up(g, i):
        at = strip(g)
        if i < 2:
            src, dst = ext.at[i, inner_high, at], ext.at[i, outer_low, at]
        else:
            src, dst = pick.at[1, :, at], far.at[0, tower, :, at]
        return remote(src, dst, high_send.at[g, i], high_recv.at[g, i], peers["high"])

    def down(g, i):
        at = strip(g)
        if i < 2:
            src, dst = ext.at[i, inner_low, at], ext.at[i, outer_high, at]
        else:
            src, dst = pick.at[0, :, at], far.at[1, tower, :, at]
        return remote(src, dst, low_send.at[g, i], low_recv.at[g, i], peers["low"])

    def mated(g):
        at = strip(g)
        other = pl.ds(pl.multiple_of((1 - seq) * half, half), half)
        return remote(
            cext.at[1 - tower, other, at], mate.at[other, at],
            mate_send.at[g], mate_recv.at[g], peers["tower"],
        )

    def shared(g, i):
        at = strip(g)
        return remote(
            far.at[i, tower, :, at], far.at[i, tower, :, at],
            far_send.at[g, i], far_recv.at[g, i], peers["tower"],
        )

    mask_y = remote(m_ref, mask_ext.at[1 + seq], mask_send.at[0], mask_recv.at[0], peers["y"])
    mask_up = remote(mask_ext.at[2], mask_ext.at[0], mask_send.at[1], mask_recv.at[1], peers["high"])
    mask_down = remote(mask_ext.at[1], mask_ext.at[3], mask_send.at[2], mask_recv.at[2], peers["low"])

    def pass_on(g, i, own):
        @pl.when(((seq == 1) if own else (seq == 0)) & has_high)
        def _():
            up(g, i).start()

        @pl.when(((seq == 0) if own else (seq == 1)) & has_low)
        def _():
            down(g, i).start()

    def choose(g, own):
        at = strip(g)
        tile = seq if own else 1 - seq
        where = here if own else pl.ds(pl.multiple_of((1 - seq) * half, half), half)
        high = tile == 1
        chain = jnp.where(high, jnp.where(off_above > 0, 1, 0), jnp.where(off_below < 0, 1, 0))
        pick[tile, :, at] = jnp.where(chain == 1, mate[where, at], cext[tower, where, at])
        pass_on(g, 2, own)

    locals_ = [
        pltpu.make_async_copy(k_ref.at[:, mine], ext.at[0, ext_here, :], local_sem.at[0]),
        pltpu.make_async_copy(v_ref.at[:, mine], ext.at[1, ext_here, :], local_sem.at[1]),
        pltpu.make_async_copy(m_ref, mask_ext.at[1 + seq], local_sem.at[2]),
        pltpu.make_async_copy(q_ref.at[:, mine], side.at[0, here, :], local_sem.at[3]),
        pltpu.make_async_copy(cq_ref.at[:, mine], side.at[1, here, :], local_sem.at[4]),
        pltpu.make_async_copy(g_ref.at[:, mine], side.at[2, here, :], local_sem.at[5]),
    ]
    for copy in locals_:
        copy.start()
    for chain, ref in enumerate((ck_ref, cv_ref)):
        @pl.when(tower == chain)
        def _():
            pltpu.make_async_copy(ref.at[:, mine], mate.at[here, :], local_sem.at[6]).start()

    @pl.when(blk == 0)
    def _():
        ext[:, :half, :] = jnp.zeros((2, half, cols), BF16)
        far[0] = jnp.zeros(far.shape[1:], BF16)
        mask_ext[0] = jnp.zeros(mask_ext.shape[1:], jnp.int32)
        recv[0] = jnp.zeros(recv.shape[1:], BF16)
        gfar[0] = jnp.zeros(gfar.shape[1:], BF16)

    @pl.when(blk == blks - 1)
    def _():
        ext[:, 3 * half :, :] = jnp.zeros((2, half, cols), BF16)
        far[1] = jnp.zeros(far.shape[1:], BF16)
        mask_ext[3] = jnp.zeros(mask_ext.shape[1:], jnp.int32)
        recv[1] = jnp.zeros(recv.shape[1:], BF16)
        gfar[1] = jnp.zeros(gfar.shape[1:], BF16)

    for copy in locals_:
        copy.wait()
    for chain, ref in enumerate((ck_ref, cv_ref)):
        @pl.when(tower == chain)
        def _():
            pltpu.make_async_copy(ref.at[:, mine], mate.at[here, :], local_sem.at[6]).wait()

    greet(blk, blks, peers)
    mask_y.start()
    for g in range(groups):
        for copy in incoming(g)[:6]:
            copy.start()
        for i in range(2):
            pass_on(g, i, True)
    for g in range(groups):
        for copy in incoming(g)[6:]:
            copy.start()
    mask_y.wait_recv()

    @pl.when(has_high)
    def _():
        mask_up.start()

    @pl.when(has_low)
    def _():
        mask_down.start()

    for g in range(groups):
        for copy in incoming(g)[4:6]:
            copy.wait_recv()
        choose(g, True)
    for g in range(groups):
        moved = incoming(g)
        for i in range(2):
            moved[i].wait_recv()
            pass_on(g, i, False)
        for i in range(2, 4):
            moved[i].wait_recv()
        mated(g).start()
        if g:
            mated(g - 1).wait_recv()
            choose(g - 1, False)
    mated(groups - 1).wait_recv()
    choose(groups - 1, False)

    @pl.when(has_high)
    def _():
        mask_down.wait_recv()

    @pl.when(has_low)
    def _():
        mask_up.wait_recv()

    cross_at = jnp.where(below, 0, half)
    band_low = off + half

    def column(part, chain):
        row = jnp.where(
            chain == 0, mask_ext[part, 0:1, :].astype(F32), mask_ext[part, 1:2, :].astype(F32)
        )
        return jnp.transpose(jnp.broadcast_to(row, (half, half)))

    own_valid = [column(part, tower) for part in range(4)]
    other_valid = [column(part, 1 - tower) for part in range(4)]
    row_at = lax.broadcasted_iota(jnp.int32, (half, half), 0)
    col_at = lax.broadcasted_iota(jnp.int32, (half, half), 1)
    for part_at in range(3):
        where = slice(part_at * half, (part_at + 1) * half)
        distance = col_at + half - (row_at + part_at * half)
        for tile in range(2):
            near = (jnp.abs(distance) <= half) & (own_valid[tile + part_at] > 0)
            add = jnp.where(near, 0.0, -1e30)
            bias[tile, where, :half] = add
            bias[tile, where, half:] = add
        at = row_at + part_at * half + cross_at
        valid = jnp.where(below, other_valid[part_at], other_valid[part_at + 1])
        inside = (at >= band_low) & (at < band_low + 2 * half) & (valid > 0)
        add = jnp.where(inside, 0.0, -1e30)
        bias[2, where, :half] = add
        bias[2, where, half:] = add

    lanes = lax.broadcasted_iota(jnp.int32, (half, wide), 1)
    zero = jnp.zeros((half, wide), BF16)

    def split(tile):
        return jnp.concatenate(
            (jnp.where(lanes < HEAD, tile, zero), jnp.where(lanes < HEAD, zero, tile)), 0
        )

    def dot_t(a, b):
        return lax.dot_general(a, b, (((1,), (1,)), ((), ())), preferred_element_type=F32)

    def dot(a, b):
        return jnp.dot(a, b, preferred_element_type=F32)

    def own_heads(both):
        return jnp.concatenate((both[:HEAD, :half], both[HEAD:, half:]), 0)

    def turned(x):
        return jnp.transpose(x.astype(F32)).astype(BF16)

    def one(query, cot, key, value, key_t, value_t, add):
        scores = dot_t(key, query) + bias[add]
        unnormed = jnp.exp(scores - jnp.max(scores, axis=0, keepdims=True))
        weights = unnormed * (1.0 / jnp.sum(unnormed, axis=0, keepdims=True))
        prob = weights.astype(BF16)
        grad_probs = dot_t(value, cot)
        row_dot = jnp.sum(weights * grad_probs, axis=0, keepdims=True)
        grad_scores = (weights * (grad_probs - row_dot)).astype(BF16)
        result = own_heads(dot(value_t, prob))
        grad_query = own_heads(dot(key_t, grad_scores)) * scale
        return result, grad_query, dot(grad_scores, query), dot(prob, cot)

    def cots(g):
        at = strip(g)
        return [split(side[2, tile * half : (tile + 1) * half, at]) for tile in range(2)]

    def cross_part(g, cot):
        at = strip(g)

        def band(i):
            first, second = cext[i, :half, at], cext[i, half:, at]
            return jnp.concatenate(
                (
                    jnp.where(below, far[0, i, :, at], first),
                    jnp.where(below, first, second),
                    jnp.where(below, second, far[1, i, :, at]),
                ),
                0,
            )

        ckey, cvalue = band(0), band(1)
        ckey_t, cvalue_t = turned(ckey), turned(cvalue)
        results = []
        for tile in range(2):
            cross = split(side[1, tile * half : (tile + 1) * half, at] * BF16(scale))
            results.append(one(cross, cot[tile], ckey, cvalue, ckey_t, cvalue_t, 2))
        for i in range(2):
            total = results[0][2 + i] + results[1][2 + i]
            a, b, c = total[:half], total[half : 2 * half], total[2 * half :]
            part[i, :, at] = jnp.where(below, a, c).astype(BF16)
            core[2 + i, 0, :, at] = jnp.where(below, b, a)
            core[2 + i, 1, :, at] = jnp.where(below, c, b)
        return [(result[0], result[1]) for result in results]

    def self_part(g, cot, crossed):
        at = strip(g)
        key, value = ext[0, :, at], ext[1, :, at]
        key_t, value_t = turned(key), turned(value)
        grad_parts, head_parts = [], []
        for tile in range(2):
            span = slice(tile * half, tile * half + keys)
            query = split(side[0, tile * half : (tile + 1) * half, at] * BF16(scale))
            so, sq, sk, sv = one(
                query, cot[tile], key[span], value[span], key_t[:, span], value_t[:, span], tile
            )
            head_parts.append((so + crossed[tile][0], sq, crossed[tile][1]))
            grad_parts.append((sk, sv))
        for i in range(2):
            first, second = grad_parts[0][i], grad_parts[1][i]
            low_stage[i, :, at] = first[:half].astype(BF16)
            core[i, 0, :, at] = first[half : 2 * half] + second[:half]
            core[i, 1, :, at] = first[2 * half :] + second[half : 2 * half]
            high_stage[i, :, at] = second[2 * half :].astype(BF16)
        for i in range(3):
            lower = turned(head_parts[0][i])
            upper = turned(head_parts[1][i])
            direct[i][:, strip(g, seq * cols)] = jnp.where(seq == 0, lower, upper)
            y_stage[i, :, at] = jnp.where(seq == 0, upper, lower)

    def grad_down(g, i):
        at = strip(g)
        if i < 2:
            src, dst = low_stage.at[i, :, at], recv.at[1, i, :, at]
        else:
            src, dst = gpick.at[0, :, at], gfar.at[1, tower, :, at]
        return remote(src, dst, glow_send.at[g, i], glow_recv.at[g, i], peers["low"])

    def grad_up(g, i):
        at = strip(g)
        if i < 2:
            src, dst = high_stage.at[i, :, at], recv.at[0, i, :, at]
        else:
            src, dst = gpick.at[1, :, at], gfar.at[0, tower, :, at]
        return remote(src, dst, ghigh_send.at[g, i], ghigh_recv.at[g, i], peers["high"])

    def swap(g):
        at = strip(g)
        return remote(
            part.at[1 - tower, :, at], mate_part.at[:, at],
            part_send.at[g], part_recv.at[g], peers["tower"],
        )

    def gshared(g, i):
        at = strip(g)
        return remote(
            gfar.at[i, tower, :, at], gfar.at[i, tower, :, at],
            gfar_send.at[g, i], gfar_recv.at[g, i], peers["tower"],
        )

    def outgoing(g):
        at, to_at = strip(g), strip(g, seq * cols)
        moves = [(y_stage.at[i, :, at], direct[i].at[:, to_at], "y") for i in range(3)]
        moves += [
            (y_stage.at[3 + i, :, at], grads[i].at[:, to_at], "y" if i < 2 else "diag")
            for i in range(4)
        ]
        moves += [(t_stage.at[i, :, at], grads[2 + i].at[:, to_at], "tower") for i in range(2)]
        return [
            remote(src, dst, out_send.at[g, i], out_recv.at[g, i], peers[to])
            for i, (src, dst, to) in enumerate(moves)
        ]

    def start_down(g):
        @pl.when(has_low)
        def _():
            for i in (2, 0, 1):
                grad_down(g, i).start()

    def start_up(g):
        @pl.when(has_high)
        def _():
            for i in (2, 0, 1):
                grad_up(g, i).start()

    def give(g):
        at = strip(g)
        swap(g).wait_recv()
        own, others = part[tower, :, at], mate_part[:, at]
        gpick[0, :, at] = jnp.where(below, own, others)
        gpick[1, :, at] = jnp.where(below, others, own)

        @pl.when(seq == 0)
        def _():
            start_down(g)
            start_up(g)

        @pl.when(seq == 1)
        def _():
            start_up(g)
            start_down(g)

        for copy in outgoing(g)[:3]:
            copy.start()

    def share(g):
        @pl.when(has_low)
        def _():
            up(g, 2).wait_recv()
            shared(g, 0).start()

        @pl.when(has_high)
        def _():
            down(g, 2).wait_recv()
            shared(g, 1).start()

    take_low, take_high = off_below > 0, off_above < 0

    def finish(g):
        at = strip(g)
        moves = outgoing(g)

        def on_side(low_side, high_side, low, high):
            @pl.when(low_side & has_low)
            def _():
                low()

            @pl.when(high_side & has_high)
            def _():
                high()

        def tile_of(tile, low_side, high_side, place):
            def relay_low():
                grad_up(g, 2).wait_recv()
                gshared(g, 0).start()

            def relay_high():
                grad_down(g, 2).wait_recv()
                gshared(g, 1).start()

            on_side(low_side, high_side, relay_low, relay_high)
            for i in range(2):
                on_side(
                    low_side, high_side, grad_up(g, i).wait_recv, grad_down(g, i).wait_recv
                )
                place(
                    i, (core[i, tile, :, at] + recv[tile, i, :, at].astype(F32)).astype(BF16)
                )
            on_side(low_side, high_side, gshared(g, 0).wait_recv, gshared(g, 1).wait_recv)
            wanted = jnp.where(low_side, jnp.where(take_low, 1, 0), jnp.where(take_high, 1, 0))
            for i in range(2):
                more = jnp.where(wanted == 1, gfar[tile, i, :, at].astype(F32), 0.0)
                place(2 + i, (core[2 + i, tile, :, at] + more).astype(BF16))

        def give_away(i, total):
            y_stage[3 + i, :, at] = total
            moves[3 + i].start()

        def keep_here(i, total):
            if i < 2:
                grads[i][:, strip(g, seq * cols)] = total
            else:
                t_stage[i - 2, :, at] = total
                moves[5 + i].start()

        tile_of(1 - seq, seq == 1, seq == 0, give_away)
        tile_of(seq, seq == 0, seq == 1, keep_here)

    def step(g, carry):
        for copy in incoming(g)[6:]:
            copy.wait_recv()

        @pl.when(has_low)
        def _():
            shared(g, 0).wait_recv()

        @pl.when(has_high)
        def _():
            shared(g, 1).wait_recv()

        cot = cots(g)
        crossed = cross_part(g, cot)
        swap(g).start()

        @pl.when(g + 1 < groups)
        def _():
            share(g + 1)

        @pl.when(has_high)
        def _():
            for i in range(2):
                down(g, i).wait_recv()

        @pl.when(has_low)
        def _():
            for i in range(2):
                up(g, i).wait_recv()

        self_part(g, cot, crossed)
        give(g)

        @pl.when(g >= LAG)
        def _():
            finish(g - LAG)

        return carry

    share(0)
    lax.fori_loop(0, groups, step, 0)
    for g in range(max(groups - LAG, 0), groups):
        finish(g)

    def close(g, carry):
        for copy in incoming(g):
            copy.wait_send()
        for copy in outgoing(g):
            copy.wait()
        mated(g).wait_send()
        swap(g).wait_send()

        @pl.when(has_high)
        def _():
            for i in range(3):
                up(g, i).wait_send()
                grad_up(g, i).wait_send()
            shared(g, 1).wait_send()
            gshared(g, 1).wait_send()

        @pl.when(has_low)
        def _():
            for i in range(3):
                down(g, i).wait_send()
                grad_down(g, i).wait_send()
            shared(g, 0).wait_send()
            gshared(g, 0).wait_send()

        return carry

    lax.fori_loop(0, groups, close, 0)
    mask_y.wait_send()

    @pl.when(has_high)
    def _():
        mask_up.wait_send()

    @pl.when(has_low)
    def _():
        mask_down.wait_send()


def copy_kernel(*refs):
    count = len(refs) // 2
    for src, dst in zip(refs[:count], refs[count:]):
        dst[...] = src[...]


def paired(
    queries, key_rows, value_rows, cross_queries, cross_keys, cross_values, grad_out,
    offsets, key_valid,
):
    blks = lax.axis_size("blk")
    cols = HEADS // lax.axis_size("seq") * HEAD
    values = [
        value[0] for value in (
            queries, key_rows, value_rows, cross_queries, cross_keys, cross_values, grad_out
        )
    ]
    rows = queries.shape[1]
    block, groups = 2 * rows, cols // (2 * HEAD)
    vmem = pl.BlockSpec(memory_space=pltpu.VMEM)
    dma = pltpu.SemaphoreType.DMA
    full = jax.ShapeDtypeStruct((rows, 2 * cols), BF16)
    outs = pl.pallas_call(
        functools.partial(fused_kernel, blks, rows, cols),
        out_shape=(full,) * 7,
        in_specs=[pl.BlockSpec(memory_space=pltpu.SMEM)] + [pl.BlockSpec(memory_space=pl.ANY)] * 8,
        out_specs=(vmem,) * 7,
        scratch_shapes=[
            pltpu.VMEM((3, block, cols), BF16),
            pltpu.VMEM((2, 2 * block, cols), BF16),
            pltpu.VMEM((2, block, cols), BF16),
            pltpu.VMEM((block, cols), BF16),
            pltpu.VMEM((2, rows, cols), BF16),
            pltpu.VMEM((2, 2, rows, cols), BF16),
            pltpu.VMEM((4,) + key_valid.shape, jnp.int32),
            pltpu.VMEM((3, 3 * rows, block), F32),
            pltpu.VMEM((7, rows, cols), BF16),
            pltpu.VMEM((2, rows, cols), BF16),
            pltpu.VMEM((2, rows, cols), BF16),
            pltpu.VMEM((2, rows, cols), BF16),
            pltpu.VMEM((4, 2, rows, cols), F32),
            pltpu.VMEM((2, 2, rows, cols), BF16),
            pltpu.VMEM((2, rows, cols), BF16),
            pltpu.VMEM((rows, cols), BF16),
            pltpu.VMEM((2, rows, cols), BF16),
            pltpu.VMEM((2, 2, rows, cols), BF16),
            dma((7,)), dma((3,)), dma((3,)),
            dma((groups, 9)), dma((groups, 9)),
            dma((groups, 3)), dma((groups, 3)), dma((groups, 3)), dma((groups, 3)),
            dma((groups,)), dma((groups,)), dma((groups, 2)), dma((groups, 2)),
            dma((groups, 9)), dma((groups, 9)),
            dma((groups, 3)), dma((groups, 3)), dma((groups, 3)), dma((groups, 3)),
            dma((groups,)), dma((groups,)), dma((groups, 2)), dma((groups, 2)),
        ],
        compiler_params=pltpu.CompilerParams(collective_id=0, has_side_effects=True),
        name="attend_pairs",
    )(offsets, *values, key_valid)
    outs = pl.pallas_call(
        copy_kernel,
        out_shape=(full,) * 7,
        in_specs=[vmem] * 7,
        out_specs=(vmem,) * 7,
        name="hand_over",
    )(*outs)
    return tuple(piece[None] for piece in outs)


def extended(block, sides, width):
    for axis, dim in sides:
        count = lax.axis_size(axis)
        forward = [(i, i + 1) for i in range(count - 1)]
        backward = [(target, source) for source, target in forward]
        low = lax.ppermute(
            lax.slice_in_dim(block, block.shape[dim] - width, None, axis=dim), axis, forward
        )
        high = lax.ppermute(lax.slice_in_dim(block, 0, width, axis=dim), axis, backward)
        block = jnp.concatenate([low, block, high], axis=dim)
    return block


def swapped(value, axis, bit):
    mask = 2**bit
    pairs = [(source, source ^ mask) for source in range(lax.axis_size(axis))]
    return lax.ppermute(value, axis, pairs)


def passed_along(block, axis, distance):
    devices = range(lax.axis_size(axis))
    route = [(i - distance, i) for i in devices if i - distance in devices]
    return lax.ppermute(block, axis, route)


def attend(query_tile, grad_tile, key_block, value_block, allowed, heads_here):
    score_scale = HEAD ** (-0.5)
    rows_count = query_tile.shape[0]
    keys_count = key_block.shape[0]
    q_heads = query_tile.reshape(rows_count, heads_here, HEAD)
    g_heads = grad_tile.reshape(rows_count, heads_here, HEAD)
    k_heads = key_block.reshape(keys_count, heads_here, HEAD)
    v_heads = value_block.reshape(keys_count, heads_here, HEAD)
    scores = (
        jnp.einsum("qhe,khe->hqk", q_heads, k_heads, preferred_element_type=jnp.float32)
        * score_scale
    )
    scores = jnp.where(allowed[None], scores, -1e30)
    row_max = jnp.max(scores, axis=2)
    unnormed = jnp.exp(scores - row_max[:, :, None])
    row_sum = jnp.sum(unnormed, axis=2)
    weights = unnormed / row_sum[:, :, None]
    prob_bf = weights.astype(jnp.bfloat16)
    result = jnp.einsum(
        "hqk,khe->qhe", prob_bf, v_heads, preferred_element_type=jnp.float32
    ).reshape(rows_count, -1)
    grad_probs = jnp.einsum("qhe,khe->hqk", g_heads, v_heads, preferred_element_type=jnp.float32)
    row_dot = jnp.sum(weights * grad_probs, axis=2)
    grad_scores = (weights * (grad_probs - row_dot[:, :, None]) * score_scale).astype(jnp.bfloat16)
    grad_query = jnp.einsum(
        "hqk,khe->qhe", grad_scores, k_heads, preferred_element_type=jnp.float32
    ).reshape(rows_count, -1)
    grad_key = jnp.einsum(
        "hqk,qhe->khe", grad_scores, q_heads, preferred_element_type=jnp.float32
    ).reshape(keys_count, -1)
    grad_value = jnp.einsum(
        "hqk,qhe->khe", prob_bf, g_heads, preferred_element_type=jnp.float32
    ).reshape(keys_count, -1)
    return (result, grad_query, grad_key, grad_value, jnp.stack((row_max, row_sum, row_dot)))


def shards(
    queries,
    key_rows,
    value_rows,
    cross_queries,
    cross_keys,
    cross_values,
    grad_out,
    offsets,
    key_valid,
):
    seq_count = lax.axis_size("seq")
    heads_here = HEADS // seq_count
    local_rows = (
        queries[0],
        key_rows[0],
        value_rows[0],
        cross_queries[0],
        cross_keys[0],
        cross_values[0],
        grad_out[0],
    )
    query_here, key_here, value_here, cross_query, cross_key, cross_value, cotangent = (
        lax.all_to_all(local_rows[0], "seq", split_axis=1, concat_axis=0, tiled=True),
        lax.all_to_all(local_rows[1], "seq", split_axis=1, concat_axis=0, tiled=True),
        lax.all_to_all(local_rows[2], "seq", split_axis=1, concat_axis=0, tiled=True),
        lax.all_to_all(local_rows[3], "seq", split_axis=1, concat_axis=0, tiled=True),
        lax.all_to_all(local_rows[4], "seq", split_axis=1, concat_axis=0, tiled=True),
        lax.all_to_all(local_rows[5], "seq", split_axis=1, concat_axis=0, tiled=True),
        lax.all_to_all(local_rows[6], "seq", split_axis=1, concat_axis=0, tiled=True),
    )
    block_len = query_here.shape[0]
    columns = query_here.shape[1]
    half_width = min(WINDOW // 2, block_len // 2)
    tile_rows = min(TILE, block_len)
    tile_count = block_len // tile_rows
    window_span = tile_rows + 2 * half_width
    tower_id = lax.axis_index("tower")
    block_id = lax.axis_index("blk")
    block_mask = lax.all_gather(key_valid, "seq", axis=1, tiled=True)
    mask_ext = extended(block_mask, (("blk", 1),), half_width)
    self_valid = lax.dynamic_index_in_dim(mask_ext, tower_id, 0, keepdims=False)
    other_valid = lax.dynamic_index_in_dim(mask_ext, 1 - tower_id, 0, keepdims=False)
    pair_ext = extended(jnp.stack((key_here, value_here)), (("blk", 1),), half_width)
    partner = swapped(jnp.stack((cross_key, cross_value)), "tower", 0)
    partner_ext = extended(partner, (("blk", 1),), half_width)
    align_shift = offsets[tower_id, block_id]
    band_start = half_width + align_shift
    band = lax.dynamic_slice_in_dim(partner_ext, band_start, block_len, 1)
    band_valid = lax.dynamic_slice_in_dim(other_valid, band_start, block_len) > 0
    rows_local = jnp.arange(tile_rows)
    keys_local = jnp.arange(window_span)
    near = jnp.abs(rows_local[:, None] + half_width - keys_local[None, :]) <= half_width

    def self_step(carry, tile_index):
        grad_key_acc, grad_value_acc = carry
        tile_start = tile_index * tile_rows
        query_tile = lax.dynamic_slice_in_dim(query_here, tile_start, tile_rows, 0)
        grad_tile = lax.dynamic_slice_in_dim(cotangent, tile_start, tile_rows, 0)
        key_window = lax.dynamic_slice_in_dim(pair_ext[0], tile_start, window_span, 0)
        value_window = lax.dynamic_slice_in_dim(pair_ext[1], tile_start, window_span, 0)
        allowed = (
            near & (lax.dynamic_slice_in_dim(self_valid, tile_start, window_span) > 0)[None, :]
        )
        result, grad_query, grad_key, grad_value, stats = attend(
            query_tile, grad_tile, key_window, value_window, allowed, heads_here
        )
        grad_key_acc = lax.dynamic_update_slice_in_dim(
            grad_key_acc,
            lax.dynamic_slice_in_dim(grad_key_acc, tile_start, window_span, 0) + grad_key,
            tile_start,
            0,
        )
        grad_value_acc = lax.dynamic_update_slice_in_dim(
            grad_value_acc,
            lax.dynamic_slice_in_dim(grad_value_acc, tile_start, window_span, 0) + grad_value,
            tile_start,
            0,
        )
        return ((grad_key_acc, grad_value_acc), (result, grad_query, stats))

    def cross_step(carry, tile_index):
        grad_key_acc, grad_value_acc = carry
        tile_start = tile_index * tile_rows
        query_tile = lax.dynamic_slice_in_dim(cross_query, tile_start, tile_rows, 0)
        grad_tile = lax.dynamic_slice_in_dim(cotangent, tile_start, tile_rows, 0)
        result, grad_query, grad_key, grad_value, stats = attend(
            query_tile, grad_tile, band[0], band[1], band_valid[None, :], heads_here
        )
        return ((grad_key_acc + grad_key, grad_value_acc + grad_value), (result, grad_query))

    zeros_ext = jnp.zeros((block_len + 2 * half_width, columns), jnp.float32)
    zeros_band = jnp.zeros((block_len, columns), jnp.float32)
    tile_ids = jnp.arange(tile_count)
    (self_gk, self_gv), (self_out, self_gq, self_stats) = lax.scan(
        self_step, (zeros_ext, zeros_ext), tile_ids
    )
    (cross_gk, cross_gv), (cross_out, cross_gq) = lax.scan(
        cross_step, (zeros_band, zeros_band), tile_ids
    )
    self_out = self_out.reshape(block_len, columns)
    cross_out = cross_out.reshape(block_len, columns)
    self_stats = jnp.transpose(self_stats, (1, 2, 0, 3)).reshape(3, heads_here, block_len)
    attended = (self_out + cross_out).astype(jnp.bfloat16)
    cross_ext = jnp.zeros((2, block_len + 2 * half_width, columns), jnp.float32)
    cross_ext = lax.dynamic_update_slice_in_dim(
        cross_ext, jnp.stack((cross_gk, cross_gv)), band_start, 1
    )
    self_ext = jnp.stack((self_gk, self_gv))
    self_core = self_ext[:, half_width : half_width + block_len]
    cross_core = cross_ext[:, half_width : half_width + block_len]
    upper_cut = block_len - half_width
    lower_send = jnp.concatenate((self_ext[:, :half_width], cross_ext[:, :half_width]), 0)
    upper_send = jnp.concatenate(
        (self_ext[:, block_len + half_width :], cross_ext[:, block_len + half_width :]), 0
    )
    from_above = passed_along(lower_send.astype(jnp.bfloat16), "blk", -1).astype(lower_send.dtype)
    from_below = passed_along(upper_send.astype(jnp.bfloat16), "blk", 1).astype(upper_send.dtype)
    self_core = (
        self_core.at[:, upper_cut:].add(from_above[:2]).at[:, :half_width].add(from_below[:2])
    )
    cross_core = (
        cross_core.at[:, upper_cut:].add(from_above[2:]).at[:, :half_width].add(from_below[2:])
    )
    returned = swapped(cross_core.astype(jnp.bfloat16), "tower", 0)
    head_outs = (
        attended,
        self_gq.reshape(block_len, columns).astype(jnp.bfloat16),
        self_core[0].astype(jnp.bfloat16),
        self_core[1].astype(jnp.bfloat16),
        cross_gq.reshape(block_len, columns).astype(jnp.bfloat16),
        returned[0],
        returned[1],
    )
    token_outs = (
        lax.all_to_all(head_outs[0], "seq", split_axis=0, concat_axis=1, tiled=True),
        lax.all_to_all(head_outs[1], "seq", split_axis=0, concat_axis=1, tiled=True),
        lax.all_to_all(head_outs[2], "seq", split_axis=0, concat_axis=1, tiled=True),
        lax.all_to_all(head_outs[3], "seq", split_axis=0, concat_axis=1, tiled=True),
        lax.all_to_all(head_outs[4], "seq", split_axis=0, concat_axis=1, tiled=True),
        lax.all_to_all(head_outs[5], "seq", split_axis=0, concat_axis=1, tiled=True),
        lax.all_to_all(head_outs[6], "seq", split_axis=0, concat_axis=1, tiled=True),
    )
    return tuple((piece[None] for piece in token_outs))


def solution(mesh):
    in_specs = (
        P("tower", ("blk", "seq"), None),
        P("tower", ("blk", "seq"), None),
        P("tower", ("blk", "seq"), None),
        P("tower", ("blk", "seq"), None),
        P("tower", ("blk", "seq"), None),
        P("tower", ("blk", "seq"), None),
        P("tower", ("blk", "seq"), None),
        P(),
        P(None, ("blk", "seq")),
    )
    out_specs = (
        P("tower", ("blk", "seq"), None),
        P("tower", ("blk", "seq"), None),
        P("tower", ("blk", "seq"), None),
        P("tower", ("blk", "seq"), None),
        P("tower", ("blk", "seq"), None),
        P("tower", ("blk", "seq"), None),
        P("tower", ("blk", "seq"), None),
    )
    body = paired if mesh.shape["seq"] == 2 else shards
    return jax.shard_map(body, mesh=mesh, in_specs=in_specs, out_specs=out_specs, check_vma=False)
```

```python
import functools

import jax
import jax.numpy as jnp
from jax import lax
from jax.experimental import pallas as pl
from jax.experimental.pallas import tpu as pltpu
from jax.sharding import PartitionSpec as P

HEADS = 16
HEAD = 64
WINDOW = 2048
TILE = 512
LAG = 4
MESH = pl.DeviceIdType.MESH
F32, BF16 = jnp.float32, jnp.bfloat16


def places():
    tower, blk, seq = lax.axis_index("tower"), lax.axis_index("blk"), lax.axis_index("seq")
    peers = dict(
        y=(tower, blk, 1 - seq),
        tower=(1 - tower, blk, seq),
        diag=(1 - tower, blk, 1 - seq),
        low=(tower, blk - 1, seq),
        high=(tower, blk + 1, seq),
    )
    return tower, blk, seq, peers


def greet(blk, blks, peers):
    barrier = pltpu.get_barrier_semaphore()
    for name in ("y", "tower", "diag"):
        pl.semaphore_signal(barrier, inc=1, device_id=peers[name], device_id_type=MESH)

    @pl.when(blk > 0)
    def _():
        pl.semaphore_signal(barrier, inc=1, device_id=peers["low"], device_id_type=MESH)

    @pl.when(blk < blks - 1)
    def _():
        pl.semaphore_signal(barrier, inc=1, device_id=peers["high"], device_id_type=MESH)

    count = 3 + jnp.where(blk > 0, 1, 0) + jnp.where(blk < blks - 1, 1, 0)
    pl.semaphore_wait(barrier, count)


def remote(src, dst, send, recv, device):
    return pltpu.make_async_remote_copy(
        src_ref=src, dst_ref=dst, send_sem=send, recv_sem=recv,
        device_id=device, device_id_type=MESH,
    )


def fused_kernel(
    blks, rows, cols,
    off_ref, q_ref, k_ref, v_ref, cq_ref, ck_ref, cv_ref, g_ref, m_ref,
    o_out, gq_out, gk_out, gv_out, gcq_out, gck_out, gcv_out,
    side, ext, cext, mate, pick, far, mask_ext, bias,
    y_stage, t_stage, low_stage, high_stage, core, recv, part, mate_part, gpick, gfar,
    local_sem, mask_send, mask_recv, in_send, in_recv,
    low_send, low_recv, high_send, high_recv, mate_send, mate_recv, far_send, far_recv,
    out_send, out_recv, glow_send, glow_recv, ghigh_send, ghigh_recv,
    part_send, part_recv, gfar_send, gfar_recv,
):
    tower, blk, seq, peers = places()
    half, wide = rows, 2 * HEAD
    keys, groups = 3 * rows, cols // (2 * HEAD)
    scale = HEAD ** (-0.5)
    has_low, has_high = blk > 0, blk < blks - 1
    here = pl.ds(pl.multiple_of(seq * half, half), half)
    ext_here = pl.ds(pl.multiple_of((1 + seq) * half, half), half)
    mine = pl.ds(pl.multiple_of(seq * cols, cols), cols)
    inner_low, inner_high = pl.ds(half, half), pl.ds(2 * half, half)
    outer_low, outer_high = pl.ds(0, half), pl.ds(3 * half, half)
    direct = [o_out, gq_out, gcq_out]
    grads = [gk_out, gv_out, gck_out, gcv_out]

    off = off_ref[tower, blk]
    off_below = off_ref[tower, jnp.maximum(blk - 1, 0)]
    off_above = off_ref[tower, jnp.minimum(blk + 1, blks - 1)]
    below = off < 0

    def strip(g, base=0):
        return pl.ds(pl.multiple_of(base + g * wide, wide), wide)

    def incoming(g):
        at = strip(g)
        keep, give = strip(g, seq * cols), strip(g, (1 - seq) * cols)
        moves = [
            (k_ref.at[:, give], ext.at[0, ext_here, at], "y"),
            (v_ref.at[:, give], ext.at[1, ext_here, at], "y"),
            (ck_ref.at[:, give], cext.at[0, here, at], "diag"),
            (cv_ref.at[:, give], cext.at[1, here, at], "diag"),
            (ck_ref.at[:, keep], cext.at[0, here, at], "tower"),
            (cv_ref.at[:, keep], cext.at[1, here, at], "tower"),
            (q_ref.at[:, give], side.at[0, here, at], "y"),
            (g_ref.at[:, give], side.at[2, here, at], "y"),
            (cq_ref.at[:, give], side.at[1, here, at], "y"),
        ]
        return [
            remote(src, dst, in_send.at[g, i], in_recv.at[g, i], peers[to])
            for i, (src, dst, to) in enumerate(moves)
        ]

    def up(g, i):
        at = strip(g)
        if i < 2:
            src, dst = ext.at[i, inner_high, at], ext.at[i, outer_low, at]
        else:
            src, dst = pick.at[1, :, at], far.at[0, tower, :, at]
        return remote(src, dst, high_send.at[g, i], high_recv.at[g, i], peers["high"])

    def down(g, i):
        at = strip(g)
        if i < 2:
            src, dst = ext.at[i, inner_low, at], ext.at[i, outer_high, at]
        else:
            src, dst = pick.at[0, :, at], far.at[1, tower, :, at]
        return remote(src, dst, low_send.at[g, i], low_recv.at[g, i], peers["low"])

    def mated(g):
        at = strip(g)
        other = pl.ds(pl.multiple_of((1 - seq) * half, half), half)
        return remote(
            cext.at[1 - tower, other, at], mate.at[other, at],
            mate_send.at[g], mate_recv.at[g], peers["tower"],
        )

    def shared(g, i):
        at = strip(g)
        return remote(
            far.at[i, tower, :, at], far.at[i, tower, :, at],
            far_send.at[g, i], far_recv.at[g, i], peers["tower"],
        )

    mask_y = remote(m_ref, mask_ext.at[1 + seq], mask_send.at[0], mask_recv.at[0], peers["y"])
    mask_up = remote(mask_ext.at[2], mask_ext.at[0], mask_send.at[1], mask_recv.at[1], peers["high"])
    mask_down = remote(mask_ext.at[1], mask_ext.at[3], mask_send.at[2], mask_recv.at[2], peers["low"])

    def pass_on(g, i, own):
        @pl.when(((seq == 1) if own else (seq == 0)) & has_high)
        def _():
            up(g, i).start()

        @pl.when(((seq == 0) if own else (seq == 1)) & has_low)
        def _():
            down(g, i).start()

    def choose(g, own):
        at = strip(g)
        tile = seq if own else 1 - seq
        where = here if own else pl.ds(pl.multiple_of((1 - seq) * half, half), half)
        high = tile == 1
        chain = jnp.where(high, jnp.where(off_above > 0, 1, 0), jnp.where(off_below < 0, 1, 0))
        pick[tile, :, at] = jnp.where(chain == 1, mate[where, at], cext[tower, where, at])
        pass_on(g, 2, own)

    locals_ = [
        pltpu.make_async_copy(k_ref.at[:, mine], ext.at[0, ext_here, :], local_sem.at[0]),
        pltpu.make_async_copy(v_ref.at[:, mine], ext.at[1, ext_here, :], local_sem.at[1]),
        pltpu.make_async_copy(m_ref, mask_ext.at[1 + seq], local_sem.at[2]),
        pltpu.make_async_copy(q_ref.at[:, mine], side.at[0, here, :], local_sem.at[3]),
        pltpu.make_async_copy(cq_ref.at[:, mine], side.at[1, here, :], local_sem.at[4]),
        pltpu.make_async_copy(g_ref.at[:, mine], side.at[2, here, :], local_sem.at[5]),
    ]
    for copy in locals_:
        copy.start()
    for chain, ref in enumerate((ck_ref, cv_ref)):
        @pl.when(tower == chain)
        def _():
            pltpu.make_async_copy(ref.at[:, mine], mate.at[here, :], local_sem.at[6]).start()

    @pl.when(blk == 0)
    def _():
        ext[:, :half, :] = jnp.zeros((2, half, cols), BF16)
        far[0] = jnp.zeros(far.shape[1:], BF16)
        mask_ext[0] = jnp.zeros(mask_ext.shape[1:], jnp.int32)
        recv[0] = jnp.zeros(recv.shape[1:], BF16)
        gfar[0] = jnp.zeros(gfar.shape[1:], BF16)

    @pl.when(blk == blks - 1)
    def _():
        ext[:, 3 * half :, :] = jnp.zeros((2, half, cols), BF16)
        far[1] = jnp.zeros(far.shape[1:], BF16)
        mask_ext[3] = jnp.zeros(mask_ext.shape[1:], jnp.int32)
        recv[1] = jnp.zeros(recv.shape[1:], BF16)
        gfar[1] = jnp.zeros(gfar.shape[1:], BF16)

    for copy in locals_:
        copy.wait()
    for chain, ref in enumerate((ck_ref, cv_ref)):
        @pl.when(tower == chain)
        def _():
            pltpu.make_async_copy(ref.at[:, mine], mate.at[here, :], local_sem.at[6]).wait()

    greet(blk, blks, peers)
    mask_y.start()
    for g in range(groups):
        for copy in incoming(g)[:6]:
            copy.start()
        for i in range(2):
            pass_on(g, i, True)
    for g in range(groups):
        for copy in incoming(g)[6:]:
            copy.start()
    mask_y.wait_recv()

    @pl.when(has_high)
    def _():
        mask_up.start()

    @pl.when(has_low)
    def _():
        mask_down.start()

    for g in range(groups):
        for copy in incoming(g)[4:6]:
            copy.wait_recv()
        choose(g, True)
    for g in range(groups):
        moved = incoming(g)
        for i in range(2):
            moved[i].wait_recv()
            pass_on(g, i, False)
        for i in range(2, 4):
            moved[i].wait_recv()
        mated(g).start()
        if g:
            mated(g - 1).wait_recv()
            choose(g - 1, False)
    mated(groups - 1).wait_recv()
    choose(groups - 1, False)

    @pl.when(has_high)
    def _():
        mask_down.wait_recv()

    @pl.when(has_low)
    def _():
        mask_up.wait_recv()

    cross_at = jnp.where(below, 0, half)
    band_low = off + half

    def column(part, chain):
        row = jnp.where(
            chain == 0, mask_ext[part, 0:1, :].astype(F32), mask_ext[part, 1:2, :].astype(F32)
        )
        return jnp.transpose(jnp.broadcast_to(row, (half, half)))

    own_valid = [column(part, tower) for part in range(4)]
    other_valid = [column(part, 1 - tower) for part in range(4)]
    row_at = lax.broadcasted_iota(jnp.int32, (half, half), 0)
    col_at = lax.broadcasted_iota(jnp.int32, (half, half), 1)
    for part_at in range(3):
        where = slice(part_at * half, (part_at + 1) * half)
        distance = col_at + half - (row_at + part_at * half)
        for tile in range(2):
            near = (jnp.abs(distance) <= half) & (own_valid[tile + part_at] > 0)
            add = jnp.where(near, 0.0, -1e30)
            bias[tile, where, :half] = add
            bias[tile, where, half:] = add
        at = row_at + part_at * half + cross_at
        valid = jnp.where(below, other_valid[part_at], other_valid[part_at + 1])
        inside = (at >= band_low) & (at < band_low + 2 * half) & (valid > 0)
        add = jnp.where(inside, 0.0, -1e30)
        bias[2, where, :half] = add
        bias[2, where, half:] = add

    lanes = lax.broadcasted_iota(jnp.int32, (half, wide), 1)
    zero = jnp.zeros((half, wide), BF16)

    def split(tile):
        return jnp.concatenate(
            (jnp.where(lanes < HEAD, tile, zero), jnp.where(lanes < HEAD, zero, tile)), 0
        )

    def dot_t(a, b):
        return lax.dot_general(a, b, (((1,), (1,)), ((), ())), preferred_element_type=F32)

    def dot(a, b):
        return jnp.dot(a, b, preferred_element_type=F32)

    def own_heads(both):
        return jnp.concatenate((both[:HEAD, :half], both[HEAD:, half:]), 0)

    def turned(x):
        return jnp.transpose(x.astype(F32)).astype(BF16)

    def one(query, cot, key, value, key_t, value_t, add):
        scores = dot_t(key, query) + bias[add]
        unnormed = jnp.exp(scores - jnp.max(scores, axis=0, keepdims=True))
        weights = unnormed * (1.0 / jnp.sum(unnormed, axis=0, keepdims=True))
        prob = weights.astype(BF16)
        grad_probs = dot_t(value, cot)
        row_dot = jnp.sum(weights * grad_probs, axis=0, keepdims=True)
        grad_scores = (weights * (grad_probs - row_dot)).astype(BF16)
        result = own_heads(dot(value_t, prob))
        grad_query = own_heads(dot(key_t, grad_scores)) * scale
        return result, grad_query, dot(grad_scores, query), dot(prob, cot)

    def cots(g):
        at = strip(g)
        return [split(side[2, tile * half : (tile + 1) * half, at]) for tile in range(2)]

    def cross_part(g, cot):
        at = strip(g)

        def band(i):
            first, second = cext[i, :half, at], cext[i, half:, at]
            return jnp.concatenate(
                (
                    jnp.where(below, far[0, i, :, at], first),
                    jnp.where(below, first, second),
                    jnp.where(below, second, far[1, i, :, at]),
                ),
                0,
            )

        ckey, cvalue = band(0), band(1)
        ckey_t, cvalue_t = turned(ckey), turned(cvalue)
        results = []
        for tile in range(2):
            cross = split(side[1, tile * half : (tile + 1) * half, at] * BF16(scale))
            results.append(one(cross, cot[tile], ckey, cvalue, ckey_t, cvalue_t, 2))
        for i in range(2):
            total = results[0][2 + i] + results[1][2 + i]
            a, b, c = total[:half], total[half : 2 * half], total[2 * half :]
            part[i, :, at] = jnp.where(below, a, c).astype(BF16)
            core[2 + i, 0, :, at] = jnp.where(below, b, a)
            core[2 + i, 1, :, at] = jnp.where(below, c, b)
        return [(result[0], result[1]) for result in results]

    def self_part(g, cot, crossed):
        at = strip(g)
        key, value = ext[0, :, at], ext[1, :, at]
        key_t, value_t = turned(key), turned(value)
        grad_parts, head_parts = [], []
        for tile in range(2):
            span = slice(tile * half, tile * half + keys)
            query = split(side[0, tile * half : (tile + 1) * half, at] * BF16(scale))
            so, sq, sk, sv = one(
                query, cot[tile], key[span], value[span], key_t[:, span], value_t[:, span], tile
            )
            head_parts.append((so + crossed[tile][0], sq, crossed[tile][1]))
            grad_parts.append((sk, sv))
        for i in range(2):
            first, second = grad_parts[0][i], grad_parts[1][i]
            low_stage[i, :, at] = first[:half].astype(BF16)
            core[i, 0, :, at] = first[half : 2 * half] + second[:half]
            core[i, 1, :, at] = first[2 * half :] + second[half : 2 * half]
            high_stage[i, :, at] = second[2 * half :].astype(BF16)
        for i in range(3):
            lower = turned(head_parts[0][i])
            upper = turned(head_parts[1][i])
            direct[i][:, strip(g, seq * cols)] = jnp.where(seq == 0, lower, upper)
            y_stage[i, :, at] = jnp.where(seq == 0, upper, lower)

    def grad_down(g, i):
        at = strip(g)
        if i < 2:
            src, dst = low_stage.at[i, :, at], recv.at[1, i, :, at]
        else:
            src, dst = gpick.at[0, :, at], gfar.at[1, tower, :, at]
        return remote(src, dst, glow_send.at[g, i], glow_recv.at[g, i], peers["low"])

    def grad_up(g, i):
        at = strip(g)
        if i < 2:
            src, dst = high_stage.at[i, :, at], recv.at[0, i, :, at]
        else:
            src, dst = gpick.at[1, :, at], gfar.at[0, tower, :, at]
        return remote(src, dst, ghigh_send.at[g, i], ghigh_recv.at[g, i], peers["high"])

    def swap(g):
        at = strip(g)
        return remote(
            part.at[1 - tower, :, at], mate_part.at[:, at],
            part_send.at[g], part_recv.at[g], peers["tower"],
        )

    def gshared(g, i):
        at = strip(g)
        return remote(
            gfar.at[i, tower, :, at], gfar.at[i, tower, :, at],
            gfar_send.at[g, i], gfar_recv.at[g, i], peers["tower"],
        )

    def outgoing(g):
        at, to_at = strip(g), strip(g, seq * cols)
        moves = [(y_stage.at[i, :, at], direct[i].at[:, to_at], "y") for i in range(3)]
        moves += [
            (y_stage.at[3 + i, :, at], grads[i].at[:, to_at], "y" if i < 2 else "diag")
            for i in range(4)
        ]
        moves += [(t_stage.at[i, :, at], grads[2 + i].at[:, to_at], "tower") for i in range(2)]
        return [
            remote(src, dst, out_send.at[g, i], out_recv.at[g, i], peers[to])
            for i, (src, dst, to) in enumerate(moves)
        ]

    def start_down(g):
        @pl.when(has_low)
        def _():
            for i in (2, 0, 1):
                grad_down(g, i).start()

    def start_up(g):
        @pl.when(has_high)
        def _():
            for i in (2, 0, 1):
                grad_up(g, i).start()

    def give(g):
        at = strip(g)
        swap(g).wait_recv()
        own, others = part[tower, :, at], mate_part[:, at]
        gpick[0, :, at] = jnp.where(below, own, others)
        gpick[1, :, at] = jnp.where(below, others, own)

        @pl.when(seq == 0)
        def _():
            start_down(g)
            start_up(g)

        @pl.when(seq == 1)
        def _():
            start_up(g)
            start_down(g)

        for copy in outgoing(g)[:3]:
            copy.start()

    def share(g):
        @pl.when(has_low)
        def _():
            up(g, 2).wait_recv()
            shared(g, 0).start()

        @pl.when(has_high)
        def _():
            down(g, 2).wait_recv()
            shared(g, 1).start()

    take_low, take_high = off_below > 0, off_above < 0

    def finish(g):
        at = strip(g)
        moves = outgoing(g)

        def on_side(low_side, high_side, low, high):
            @pl.when(low_side & has_low)
            def _():
                low()

            @pl.when(high_side & has_high)
            def _():
                high()

        def tile_of(tile, low_side, high_side, place):
            def relay_low():
                grad_up(g, 2).wait_recv()
                gshared(g, 0).start()

            def relay_high():
                grad_down(g, 2).wait_recv()
                gshared(g, 1).start()

            on_side(low_side, high_side, relay_low, relay_high)
            for i in range(2):
                on_side(
                    low_side, high_side, grad_up(g, i).wait_recv, grad_down(g, i).wait_recv
                )
                place(
                    i, (core[i, tile, :, at] + recv[tile, i, :, at].astype(F32)).astype(BF16)
                )
            on_side(low_side, high_side, gshared(g, 0).wait_recv, gshared(g, 1).wait_recv)
            wanted = jnp.where(low_side, jnp.where(take_low, 1, 0), jnp.where(take_high, 1, 0))
            for i in range(2):
                more = jnp.where(wanted == 1, gfar[tile, i, :, at].astype(F32), 0.0)
                place(2 + i, (core[2 + i, tile, :, at] + more).astype(BF16))

        def give_away(i, total):
            y_stage[3 + i, :, at] = total
            moves[3 + i].start()

        def keep_here(i, total):
            if i < 2:
                grads[i][:, strip(g, seq * cols)] = total
            else:
                t_stage[i - 2, :, at] = total
                moves[5 + i].start()

        tile_of(1 - seq, seq == 1, seq == 0, give_away)
        tile_of(seq, seq == 0, seq == 1, keep_here)

    def step(g, carry):
        for copy in incoming(g)[6:]:
            copy.wait_recv()

        @pl.when(has_low)
        def _():
            shared(g, 0).wait_recv()

        @pl.when(has_high)
        def _():
            shared(g, 1).wait_recv()

        cot = cots(g)
        crossed = cross_part(g, cot)
        swap(g).start()

        @pl.when(g + 1 < groups)
        def _():
            share(g + 1)

        @pl.when(has_high)
        def _():
            for i in range(2):
                down(g, i).wait_recv()

        @pl.when(has_low)
        def _():
            for i in range(2):
                up(g, i).wait_recv()

        self_part(g, cot, crossed)
        give(g)

        @pl.when(g >= LAG)
        def _():
            finish(g - LAG)

        return carry

    share(0)
    lax.fori_loop(0, groups, step, 0)
    for g in range(max(groups - LAG, 0), groups):
        finish(g)

    def close(g, carry):
        for copy in incoming(g):
            copy.wait_send()
        for copy in outgoing(g):
            copy.wait()
        mated(g).wait_send()
        swap(g).wait_send()

        @pl.when(has_high)
        def _():
            for i in range(3):
                up(g, i).wait_send()
                grad_up(g, i).wait_send()
            shared(g, 1).wait_send()
            gshared(g, 1).wait_send()

        @pl.when(has_low)
        def _():
            for i in range(3):
                down(g, i).wait_send()
                grad_down(g, i).wait_send()
            shared(g, 0).wait_send()
            gshared(g, 0).wait_send()

        return carry

    lax.fori_loop(0, groups, close, 0)
    mask_y.wait_send()

    @pl.when(has_high)
    def _():
        mask_up.wait_send()

    @pl.when(has_low)
    def _():
        mask_down.wait_send()


def copy_kernel(*refs):
    count = len(refs) // 2
    sem = refs[-1]
    copies = [
        pltpu.make_async_copy(src, dst, sem.at[i])
        for i, (src, dst) in enumerate(zip(refs[:count], refs[count:-1]))
    ]
    for copy in copies:
        copy.start()
    for copy in copies:
        copy.wait()


def paired(
    queries, key_rows, value_rows, cross_queries, cross_keys, cross_values, grad_out,
    offsets, key_valid,
):
    blks = lax.axis_size("blk")
    cols = HEADS // lax.axis_size("seq") * HEAD
    values = [
        value[0] for value in (
            queries, key_rows, value_rows, cross_queries, cross_keys, cross_values, grad_out
        )
    ]
    rows = queries.shape[1]
    block, groups = 2 * rows, cols // (2 * HEAD)
    vmem = pl.BlockSpec(memory_space=pltpu.VMEM)
    dma = pltpu.SemaphoreType.DMA
    full = jax.ShapeDtypeStruct((rows, 2 * cols), BF16)
    outs = pl.pallas_call(
        functools.partial(fused_kernel, blks, rows, cols),
        out_shape=(pltpu.VMEM((rows, 2 * cols), BF16),) * 7,
        in_specs=[pl.BlockSpec(memory_space=pltpu.SMEM)] + [pl.BlockSpec(memory_space=pl.ANY)] * 8,
        out_specs=(vmem,) * 7,
        scratch_shapes=[
            pltpu.VMEM((3, block, cols), BF16),
            pltpu.VMEM((2, 2 * block, cols), BF16),
            pltpu.VMEM((2, block, cols), BF16),
            pltpu.VMEM((block, cols), BF16),
            pltpu.VMEM((2, rows, cols), BF16),
            pltpu.VMEM((2, 2, rows, cols), BF16),
            pltpu.VMEM((4,) + key_valid.shape, jnp.int32),
            pltpu.VMEM((3, 3 * rows, block), F32),
            pltpu.VMEM((7, rows, cols), BF16),
            pltpu.VMEM((2, rows, cols), BF16),
            pltpu.VMEM((2, rows, cols), BF16),
            pltpu.VMEM((2, rows, cols), BF16),
            pltpu.VMEM((4, 2, rows, cols), F32),
            pltpu.VMEM((2, 2, rows, cols), BF16),
            pltpu.VMEM((2, rows, cols), BF16),
            pltpu.VMEM((rows, cols), BF16),
            pltpu.VMEM((2, rows, cols), BF16),
            pltpu.VMEM((2, 2, rows, cols), BF16),
            dma((7,)), dma((3,)), dma((3,)),
            dma((groups, 9)), dma((groups, 9)),
            dma((groups, 3)), dma((groups, 3)), dma((groups, 3)), dma((groups, 3)),
            dma((groups,)), dma((groups,)), dma((groups, 2)), dma((groups, 2)),
            dma((groups, 9)), dma((groups, 9)),
            dma((groups, 3)), dma((groups, 3)), dma((groups, 3)), dma((groups, 3)),
            dma((groups,)), dma((groups,)), dma((groups, 2)), dma((groups, 2)),
        ],
        compiler_params=pltpu.CompilerParams(collective_id=0, has_side_effects=True),
        name="attend_pairs",
    )(offsets, *values, key_valid)
    outs = pl.pallas_call(
        copy_kernel,
        out_shape=(full,) * 7,
        in_specs=[pl.BlockSpec(memory_space=pl.ANY)] * 7,
        out_specs=(pl.BlockSpec(memory_space=pl.ANY),) * 7,
        scratch_shapes=[dma((7,))],
        compiler_params=pltpu.CompilerParams(vmem_limit_bytes=1 << 20),
        name="hand_over",
    )(*outs)
    return tuple(piece[None] for piece in outs)


def extended(block, sides, width):
    for axis, dim in sides:
        count = lax.axis_size(axis)
        forward = [(i, i + 1) for i in range(count - 1)]
        backward = [(target, source) for source, target in forward]
        low = lax.ppermute(
            lax.slice_in_dim(block, block.shape[dim] - width, None, axis=dim), axis, forward
        )
        high = lax.ppermute(lax.slice_in_dim(block, 0, width, axis=dim), axis, backward)
        block = jnp.concatenate([low, block, high], axis=dim)
    return block


def swapped(value, axis, bit):
    mask = 2**bit
    pairs = [(source, source ^ mask) for source in range(lax.axis_size(axis))]
    return lax.ppermute(value, axis, pairs)


def passed_along(block, axis, distance):
    devices = range(lax.axis_size(axis))
    route = [(i - distance, i) for i in devices if i - distance in devices]
    return lax.ppermute(block, axis, route)


def attend(query_tile, grad_tile, key_block, value_block, allowed, heads_here):
    score_scale = HEAD ** (-0.5)
    rows_count = query_tile.shape[0]
    keys_count = key_block.shape[0]
    q_heads = query_tile.reshape(rows_count, heads_here, HEAD)
    g_heads = grad_tile.reshape(rows_count, heads_here, HEAD)
    k_heads = key_block.reshape(keys_count, heads_here, HEAD)
    v_heads = value_block.reshape(keys_count, heads_here, HEAD)
    scores = (
        jnp.einsum("qhe,khe->hqk", q_heads, k_heads, preferred_element_type=jnp.float32)
        * score_scale
    )
    scores = jnp.where(allowed[None], scores, -1e30)
    row_max = jnp.max(scores, axis=2)
    unnormed = jnp.exp(scores - row_max[:, :, None])
    row_sum = jnp.sum(unnormed, axis=2)
    weights = unnormed / row_sum[:, :, None]
    prob_bf = weights.astype(jnp.bfloat16)
    result = jnp.einsum(
        "hqk,khe->qhe", prob_bf, v_heads, preferred_element_type=jnp.float32
    ).reshape(rows_count, -1)
    grad_probs = jnp.einsum("qhe,khe->hqk", g_heads, v_heads, preferred_element_type=jnp.float32)
    row_dot = jnp.sum(weights * grad_probs, axis=2)
    grad_scores = (weights * (grad_probs - row_dot[:, :, None]) * score_scale).astype(jnp.bfloat16)
    grad_query = jnp.einsum(
        "hqk,khe->qhe", grad_scores, k_heads, preferred_element_type=jnp.float32
    ).reshape(rows_count, -1)
    grad_key = jnp.einsum(
        "hqk,qhe->khe", grad_scores, q_heads, preferred_element_type=jnp.float32
    ).reshape(keys_count, -1)
    grad_value = jnp.einsum(
        "hqk,qhe->khe", prob_bf, g_heads, preferred_element_type=jnp.float32
    ).reshape(keys_count, -1)
    return (result, grad_query, grad_key, grad_value, jnp.stack((row_max, row_sum, row_dot)))


def shards(
    queries,
    key_rows,
    value_rows,
    cross_queries,
    cross_keys,
    cross_values,
    grad_out,
    offsets,
    key_valid,
):
    seq_count = lax.axis_size("seq")
    heads_here = HEADS // seq_count
    local_rows = (
        queries[0],
        key_rows[0],
        value_rows[0],
        cross_queries[0],
        cross_keys[0],
        cross_values[0],
        grad_out[0],
    )
    query_here, key_here, value_here, cross_query, cross_key, cross_value, cotangent = (
        lax.all_to_all(local_rows[0], "seq", split_axis=1, concat_axis=0, tiled=True),
        lax.all_to_all(local_rows[1], "seq", split_axis=1, concat_axis=0, tiled=True),
        lax.all_to_all(local_rows[2], "seq", split_axis=1, concat_axis=0, tiled=True),
        lax.all_to_all(local_rows[3], "seq", split_axis=1, concat_axis=0, tiled=True),
        lax.all_to_all(local_rows[4], "seq", split_axis=1, concat_axis=0, tiled=True),
        lax.all_to_all(local_rows[5], "seq", split_axis=1, concat_axis=0, tiled=True),
        lax.all_to_all(local_rows[6], "seq", split_axis=1, concat_axis=0, tiled=True),
    )
    block_len = query_here.shape[0]
    columns = query_here.shape[1]
    half_width = min(WINDOW // 2, block_len // 2)
    tile_rows = min(TILE, block_len)
    tile_count = block_len // tile_rows
    window_span = tile_rows + 2 * half_width
    tower_id = lax.axis_index("tower")
    block_id = lax.axis_index("blk")
    block_mask = lax.all_gather(key_valid, "seq", axis=1, tiled=True)
    mask_ext = extended(block_mask, (("blk", 1),), half_width)
    self_valid = lax.dynamic_index_in_dim(mask_ext, tower_id, 0, keepdims=False)
    other_valid = lax.dynamic_index_in_dim(mask_ext, 1 - tower_id, 0, keepdims=False)
    pair_ext = extended(jnp.stack((key_here, value_here)), (("blk", 1),), half_width)
    partner = swapped(jnp.stack((cross_key, cross_value)), "tower", 0)
    partner_ext = extended(partner, (("blk", 1),), half_width)
    align_shift = offsets[tower_id, block_id]
    band_start = half_width + align_shift
    band = lax.dynamic_slice_in_dim(partner_ext, band_start, block_len, 1)
    band_valid = lax.dynamic_slice_in_dim(other_valid, band_start, block_len) > 0
    rows_local = jnp.arange(tile_rows)
    keys_local = jnp.arange(window_span)
    near = jnp.abs(rows_local[:, None] + half_width - keys_local[None, :]) <= half_width

    def self_step(carry, tile_index):
        grad_key_acc, grad_value_acc = carry
        tile_start = tile_index * tile_rows
        query_tile = lax.dynamic_slice_in_dim(query_here, tile_start, tile_rows, 0)
        grad_tile = lax.dynamic_slice_in_dim(cotangent, tile_start, tile_rows, 0)
        key_window = lax.dynamic_slice_in_dim(pair_ext[0], tile_start, window_span, 0)
        value_window = lax.dynamic_slice_in_dim(pair_ext[1], tile_start, window_span, 0)
        allowed = (
            near & (lax.dynamic_slice_in_dim(self_valid, tile_start, window_span) > 0)[None, :]
        )
        result, grad_query, grad_key, grad_value, stats = attend(
            query_tile, grad_tile, key_window, value_window, allowed, heads_here
        )
        grad_key_acc = lax.dynamic_update_slice_in_dim(
            grad_key_acc,
            lax.dynamic_slice_in_dim(grad_key_acc, tile_start, window_span, 0) + grad_key,
            tile_start,
            0,
        )
        grad_value_acc = lax.dynamic_update_slice_in_dim(
            grad_value_acc,
            lax.dynamic_slice_in_dim(grad_value_acc, tile_start, window_span, 0) + grad_value,
            tile_start,
            0,
        )
        return ((grad_key_acc, grad_value_acc), (result, grad_query, stats))

    def cross_step(carry, tile_index):
        grad_key_acc, grad_value_acc = carry
        tile_start = tile_index * tile_rows
        query_tile = lax.dynamic_slice_in_dim(cross_query, tile_start, tile_rows, 0)
        grad_tile = lax.dynamic_slice_in_dim(cotangent, tile_start, tile_rows, 0)
        result, grad_query, grad_key, grad_value, stats = attend(
            query_tile, grad_tile, band[0], band[1], band_valid[None, :], heads_here
        )
        return ((grad_key_acc + grad_key, grad_value_acc + grad_value), (result, grad_query))

    zeros_ext = jnp.zeros((block_len + 2 * half_width, columns), jnp.float32)
    zeros_band = jnp.zeros((block_len, columns), jnp.float32)
    tile_ids = jnp.arange(tile_count)
    (self_gk, self_gv), (self_out, self_gq, self_stats) = lax.scan(
        self_step, (zeros_ext, zeros_ext), tile_ids
    )
    (cross_gk, cross_gv), (cross_out, cross_gq) = lax.scan(
        cross_step, (zeros_band, zeros_band), tile_ids
    )
    self_out = self_out.reshape(block_len, columns)
    cross_out = cross_out.reshape(block_len, columns)
    self_stats = jnp.transpose(self_stats, (1, 2, 0, 3)).reshape(3, heads_here, block_len)
    attended = (self_out + cross_out).astype(jnp.bfloat16)
    cross_ext = jnp.zeros((2, block_len + 2 * half_width, columns), jnp.float32)
    cross_ext = lax.dynamic_update_slice_in_dim(
        cross_ext, jnp.stack((cross_gk, cross_gv)), band_start, 1
    )
    self_ext = jnp.stack((self_gk, self_gv))
    self_core = self_ext[:, half_width : half_width + block_len]
    cross_core = cross_ext[:, half_width : half_width + block_len]
    upper_cut = block_len - half_width
    lower_send = jnp.concatenate((self_ext[:, :half_width], cross_ext[:, :half_width]), 0)
    upper_send = jnp.concatenate(
        (self_ext[:, block_len + half_width :], cross_ext[:, block_len + half_width :]), 0
    )
    from_above = passed_along(lower_send.astype(jnp.bfloat16), "blk", -1).astype(lower_send.dtype)
    from_below = passed_along(upper_send.astype(jnp.bfloat16), "blk", 1).astype(upper_send.dtype)
    self_core = (
        self_core.at[:, upper_cut:].add(from_above[:2]).at[:, :half_width].add(from_below[:2])
    )
    cross_core = (
        cross_core.at[:, upper_cut:].add(from_above[2:]).at[:, :half_width].add(from_below[2:])
    )
    returned = swapped(cross_core.astype(jnp.bfloat16), "tower", 0)
    head_outs = (
        attended,
        self_gq.reshape(block_len, columns).astype(jnp.bfloat16),
        self_core[0].astype(jnp.bfloat16),
        self_core[1].astype(jnp.bfloat16),
        cross_gq.reshape(block_len, columns).astype(jnp.bfloat16),
        returned[0],
        returned[1],
    )
    token_outs = (
        lax.all_to_all(head_outs[0], "seq", split_axis=0, concat_axis=1, tiled=True),
        lax.all_to_all(head_outs[1], "seq", split_axis=0, concat_axis=1, tiled=True),
        lax.all_to_all(head_outs[2], "seq", split_axis=0, concat_axis=1, tiled=True),
        lax.all_to_all(head_outs[3], "seq", split_axis=0, concat_axis=1, tiled=True),
        lax.all_to_all(head_outs[4], "seq", split_axis=0, concat_axis=1, tiled=True),
        lax.all_to_all(head_outs[5], "seq", split_axis=0, concat_axis=1, tiled=True),
        lax.all_to_all(head_outs[6], "seq", split_axis=0, concat_axis=1, tiled=True),
    )
    return tuple((piece[None] for piece in token_outs))


def solution(mesh):
    in_specs = (
        P("tower", ("blk", "seq"), None),
        P("tower", ("blk", "seq"), None),
        P("tower", ("blk", "seq"), None),
        P("tower", ("blk", "seq"), None),
        P("tower", ("blk", "seq"), None),
        P("tower", ("blk", "seq"), None),
        P("tower", ("blk", "seq"), None),
        P(),
        P(None, ("blk", "seq")),
    )
    out_specs = (
        P("tower", ("blk", "seq"), None),
        P("tower", ("blk", "seq"), None),
        P("tower", ("blk", "seq"), None),
        P("tower", ("blk", "seq"), None),
        P("tower", ("blk", "seq"), None),
        P("tower", ("blk", "seq"), None),
        P("tower", ("blk", "seq"), None),
    )
    body = paired if mesh.shape["seq"] == 2 else shards
    return jax.shard_map(body, mesh=mesh, in_specs=in_specs, out_specs=out_specs, check_vma=False)
```

```python
import functools

import jax
import jax.numpy as jnp
from jax import lax
from jax.experimental import pallas as pl
from jax.experimental.pallas import tpu as pltpu
from jax.sharding import PartitionSpec as P

HEADS = 16
HEAD = 64
WINDOW = 2048
TILE = 512
LAG = 4
AHEAD = 5
MESH = pl.DeviceIdType.MESH
F32, BF16 = jnp.float32, jnp.bfloat16


def places():
    tower, blk, seq = lax.axis_index("tower"), lax.axis_index("blk"), lax.axis_index("seq")
    toward = 2 * seq - 1
    peers = dict(
        y=(tower, blk, 1 - seq),
        tower=(1 - tower, blk, seq),
        ahead=(tower, blk + toward, seq),
        behind=(tower, blk - toward, seq),
    )
    return tower, blk, seq, peers


def greet(has_ahead, has_behind, peers):
    barrier = pltpu.get_barrier_semaphore()
    for name in ("y", "tower"):
        pl.semaphore_signal(barrier, inc=1, device_id=peers[name], device_id_type=MESH)
    for name, present in (("ahead", has_ahead), ("behind", has_behind)):
        @pl.when(present)
        def _():
            pl.semaphore_signal(barrier, inc=1, device_id=peers[name], device_id_type=MESH)

    count = 2 + jnp.where(has_ahead, 1, 0) + jnp.where(has_behind, 1, 0)
    pl.semaphore_wait(barrier, count)


def remote(src, dst, send, recv, device):
    return pltpu.make_async_remote_copy(
        src_ref=src, dst_ref=dst, send_sem=send, recv_sem=recv,
        device_id=device, device_id_type=MESH,
    )


def fused_kernel(
    blks, rows, cols,
    off_ref, q_ref, k_ref, v_ref, cq_ref, ck_ref, cv_ref, g_ref, m_ref,
    o_out, gq_out, gk_out, gv_out, gcq_out, gck_out, gcv_out,
    side, pair, halo, partner, far, mate, pick, mask_ext, bias,
    exps, dots, sums, stat, peer_stat,
    mine, y_stage, y_recv, core, x_stage, x_recv, own_stage, own_recv,
    part, mate_part, gpick, gfar,
    local_sem, mask_send, mask_recv, in_send, in_recv, halo_send, halo_recv,
    partner_send, partner_recv, far_send, far_recv, share_send, share_recv,
    stat_send, stat_recv, y_send, y_recv_sem, x_send, x_recv_sem, own_send, own_recv_sem,
    swap_send, swap_recv, gfar_send, gfar_recv, gshare_send, gshare_recv,
):
    tower, blk, seq, peers = places()
    half, wide = rows, 2 * HEAD
    groups = cols // wide
    scale = HEAD ** (-0.5)
    has_low, has_high = blk > 0, blk < blks - 1
    has_ahead = ((seq == 1) & has_high) | ((seq == 0) & has_low)
    has_behind = ((seq == 1) & has_low) | ((seq == 0) & has_high)
    outs = [o_out, gq_out, gcq_out]
    grads = [gk_out, gv_out, gck_out, gcv_out]

    off = off_ref[tower, blk]
    off_ahead = off_ref[tower, jnp.clip(blk + 2 * seq - 1, 0, blks - 1)]
    chosen = jnp.where(seq == 1, jnp.where(off_ahead > 0, 1, 0), jnp.where(off_ahead < 0, 1, 0))
    uses_far = jnp.where(seq == 0, jnp.where(off > 0, 1, 0), jnp.where(off < 0, 1, 0))
    far_from = jnp.where(seq == 0, 0, jnp.where(off < 0, half + off, half))
    far_to = jnp.where(seq == 0, jnp.maximum(off, 0), half)

    def strip(g):
        return pl.ds(pl.multiple_of(g * wide, wide), wide)

    def incoming(g):
        at = strip(g)
        return [
            remote(ref.at[:, at], side.at[i, 1, :, at], in_send.at[g, i], in_recv.at[g, i], peers["y"])
            for i, ref in enumerate((q_ref, cq_ref, g_ref))
        ]

    def haloed(g):
        at = strip(g)
        return [
            remote(
                ref.at[:, at], halo.at[i, :, at], halo_send.at[g, i], halo_recv.at[g, i],
                peers["ahead"],
            )
            for i, ref in enumerate((k_ref, v_ref))
        ]

    def afar(g):
        at = strip(g)
        return remote(
            pick.at[:, at], far.at[tower, :, at], far_send.at[g], far_recv.at[g], peers["ahead"]
        )

    def shared(g):
        at = strip(g)
        return remote(
            far.at[tower, :, at], far.at[tower, :, at], share_send.at[g], share_recv.at[g],
            peers["tower"],
        )

    partners = [
        remote(ref, partner.at[i], partner_send.at[i], partner_recv.at[i], peers["tower"])
        for i, ref in enumerate((ck_ref, cv_ref))
    ]
    mask_ahead = remote(m_ref, mask_ext.at[1], mask_send.at[0], mask_recv.at[0], peers["ahead"])

    def issue(g):
        for copy in incoming(g):
            copy.start()

    def issue_halo(g):
        @pl.when(has_ahead)
        def _():
            for copy in haloed(g):
                copy.start()

    def issue_far(g):
        @pl.when(has_ahead)
        def _():
            afar(g).start()

    locals_ = [
        pltpu.make_async_copy(k_ref, pair.at[0], local_sem.at[0]),
        pltpu.make_async_copy(v_ref, pair.at[1], local_sem.at[1]),
        pltpu.make_async_copy(m_ref, mask_ext.at[0], local_sem.at[2]),
        pltpu.make_async_copy(q_ref, side.at[0, 0], local_sem.at[3]),
        pltpu.make_async_copy(cq_ref, side.at[1, 0], local_sem.at[4]),
        pltpu.make_async_copy(g_ref, side.at[2, 0], local_sem.at[5]),
    ]
    for copy in locals_:
        copy.start()
    for chain, ref in enumerate((ck_ref, cv_ref)):
        @pl.when(tower == chain)
        def _():
            pltpu.make_async_copy(ref, mate, local_sem.at[6]).start()

    @pl.when(jnp.logical_not(has_behind))
    def _():
        halo[...] = jnp.zeros(halo.shape, BF16)
        far[...] = jnp.zeros(far.shape, BF16)
        mask_ext[1] = jnp.zeros(mask_ext.shape[1:], jnp.int32)

    @pl.when(jnp.logical_not(has_ahead))
    def _():
        x_recv[...] = jnp.zeros(x_recv.shape, BF16)
        gfar[...] = jnp.zeros(gfar.shape, BF16)

    for copy in locals_:
        copy.wait()
    for chain, ref in enumerate((ck_ref, cv_ref)):
        @pl.when(tower == chain)
        def _():
            pltpu.make_async_copy(ref, mate, local_sem.at[6]).wait()

    greet(has_ahead, has_behind, peers)

    @pl.when(has_ahead)
    def _():
        mask_ahead.start()

    for copy in partners:
        copy.start()
    first = min(AHEAD, groups)
    for g in range(first):
        issue(g)
    for g in range(min(2, groups)):
        issue_halo(g)
    for copy in partners:
        copy.wait_recv()
    pick[...] = jnp.where(chosen == 1, mate[...], partner[tower])
    for g in range(groups):
        if g >= 2:
            issue_halo(g)
        issue_far(g)

    @pl.when(has_behind)
    def _():
        mask_ahead.wait_recv()

    def column(part_at, chain):
        row = jnp.where(
            chain == 0, mask_ext[part_at, 0:1, :].astype(F32), mask_ext[part_at, 1:2, :].astype(F32)
        )
        return jnp.transpose(jnp.broadcast_to(row, (half, half)))

    row_at = lax.broadcasted_iota(jnp.int32, (half, half), 0)
    col_at = lax.broadcasted_iota(jnp.int32, (half, half), 1)
    apart = (row_at - col_at) * jnp.where(seq == 0, 1, -1)
    from_far = (row_at >= far_from) & (row_at < far_to)
    own_valid, halo_valid = column(0, tower), column(1, tower)
    cross_valid = jnp.where(from_far, column(1, 1 - tower), column(0, 1 - tower))
    allowed = (
        own_valid > 0,
        (own_valid > 0) & (apart >= 0),
        (halo_valid > 0) & (apart <= 0),
        cross_valid > 0,
    )
    for i, near in enumerate(allowed):
        add = jnp.where(near, 0.0, -1e30)
        bias[i, :, :half] = add
        bias[i, :, half:] = add

    lanes = lax.broadcasted_iota(jnp.int32, (half, wide), 1)
    zero = jnp.zeros((half, wide), BF16)

    def split(tile):
        return jnp.concatenate(
            (jnp.where(lanes < HEAD, tile, zero), jnp.where(lanes < HEAD, zero, tile)), 0
        )

    def dot_t(a, b):
        return lax.dot_general(a, b, (((1,), (1,)), ((), ())), preferred_element_type=F32)

    def dot(a, b):
        return jnp.dot(a, b, preferred_element_type=F32)

    def own_heads(both):
        return jnp.concatenate((both[:HEAD, :half], both[HEAD:, half:]), 0)

    def turned(x):
        return jnp.transpose(x.astype(F32)).astype(BF16)

    def operands(g):
        at = strip(g)
        query = [split(side[0, i, :, at] * BF16(scale)) for i in range(2)]
        cross = [split(side[1, i, :, at] * BF16(scale)) for i in range(2)]
        cot = [split(side[2, i, :, at]) for i in range(2)]
        near = [pair[i, :, at] for i in range(2)]
        edge = [halo[i, :, at] for i in range(2)]
        band = [jnp.where(from_far, far[i, :, at], partner[i, :, at]) for i in range(2)]
        return query, cross, cot, near, edge, band

    spans = (slice(0, half), slice(half, 3 * half), slice(3 * half, 4 * half), slice(4 * half, 5 * half))

    def score(g):
        query, cross, cot, near, edge, band = operands(g)
        keys = (near, [jnp.concatenate((n, e), 0) for n, e in zip(near, edge)], band, band)
        asks = (query[0], query[1], cross[0], cross[1])
        adds = (bias[0], jnp.concatenate((bias[1], bias[2]), 0), bias[3], bias[3])
        for kind in range(4):
            key, value = keys[kind]
            scores = dot_t(key, asks[kind]) + adds[kind]
            products = dot_t(value, cot[kind % 2])
            top = jnp.max(scores, axis=0, keepdims=True)
            unnormed = jnp.exp(scores - top)
            total = jnp.sum(unnormed, axis=0, keepdims=True)
            exps[g, spans[kind], :] = unnormed
            dots[g, spans[kind], :] = products
            sums[g, kind : kind + 1, :] = total
            stat[g, 2 * kind : 2 * kind + 1, :] = top + jnp.log(total)
            stat[g, 2 * kind + 1 : 2 * kind + 2, :] = (
                jnp.sum(unnormed * products, axis=0, keepdims=True) / total
            )

    def exchange(g):
        return remote(
            stat.at[g], peer_stat.at[g], stat_send.at[g], stat_recv.at[g], peers["y"]
        )

    def weigh(g, kind):
        other = kind ^ 1
        here, there = stat[g, 2 * kind : 2 * kind + 1, :], peer_stat[g, 2 * other : 2 * other + 1, :]
        top = jnp.maximum(here, there)
        whole = top + jnp.log(jnp.exp(here - top) + jnp.exp(there - top))
        share_here, share_there = jnp.exp(here - whole), jnp.exp(there - whole)
        row_dot = (
            share_here * stat[g, 2 * kind + 1 : 2 * kind + 2, :]
            + share_there * peer_stat[g, 2 * other + 1 : 2 * other + 2, :]
        )
        weights = exps[g, spans[kind], :] * (share_here / sums[g, kind : kind + 1, :])
        grad_scores = weights * (dots[g, spans[kind], :] - row_dot)
        return weights.astype(BF16), grad_scores.astype(BF16)

    def settle(g, swap, relay):
        at = strip(g)
        query, cross, cot, near, edge, band = operands(g)
        band_t = [turned(x) for x in band]
        prob, slope = zip(*[weigh(g, kind) for kind in (2, 3)])
        cross_out = [own_heads(dot(band_t[1], prob[i])) for i in range(2)]
        cross_grad = [own_heads(dot(band_t[0], slope[i])) * scale for i in range(2)]
        band_grad = (
            dot(slope[0], cross[0]) + dot(slope[1], cross[1]),
            dot(prob[0], cot[0]) + dot(prob[1], cot[1]),
        )
        for i in range(2):
            part[i, :, at] = jnp.where(from_far, band_grad[i], 0.0).astype(BF16)
            own_stage[i, :, at] = jnp.where(from_far, 0.0, band_grad[i]).astype(BF16)
        swap()
        near_t = [turned(x) for x in near]
        both_t = [jnp.concatenate((n, turned(e)), 1) for n, e in zip(near_t, edge)]
        prob, slope = zip(*[weigh(g, kind) for kind in (0, 1)])
        self_out = [own_heads(dot(near_t[1], prob[0])), own_heads(dot(both_t[1], prob[1]))]
        self_grad = [own_heads(dot(near_t[0], slope[0])), own_heads(dot(both_t[0], slope[1]))]
        ours = (self_out[0] + cross_out[0], self_grad[0] * scale, cross_grad[0])
        theirs = (self_out[1] + cross_out[1], self_grad[1] * scale, cross_grad[1])
        for i in range(3):
            y_stage[i, :, at] = turned(theirs[i])
            mine[i, :, at] = jnp.transpose(ours[i])
        for i, (left, right, ask) in enumerate(
            ((slope[0], slope[1], query), (prob[0], prob[1], cot))
        ):
            core[i, :, at] = dot(left, ask[0]) + dot(right[:half], ask[1])
            x_stage[i, :, at] = dot(right[half:], ask[1]).astype(BF16)
        relay()

    def outgoing(g):
        at = strip(g)
        return [
            remote(
                y_stage.at[i, :, at], y_recv.at[i, :, at], y_send.at[g, i], y_recv_sem.at[g, i],
                peers["y"],
            )
            for i in range(3)
        ]

    def back(g):
        at = strip(g)
        return [
            remote(
                x_stage.at[i, :, at], x_recv.at[i, :, at], x_send.at[g, i], x_recv_sem.at[g, i],
                peers["behind"],
            )
            for i in range(2)
        ]

    def homeward(g):
        at = strip(g)
        return [
            remote(
                own_stage.at[i, :, at], own_recv.at[i, :, at],
                own_send.at[g, i], own_recv_sem.at[g, i], peers["tower"],
            )
            for i in range(2)
        ]

    def swapped_part(g):
        at = strip(g)
        return remote(
            part.at[1 - tower, :, at], mate_part.at[:, at], swap_send.at[g], swap_recv.at[g],
            peers["tower"],
        )

    def far_back(g):
        at = strip(g)
        return remote(
            gpick.at[:, at], gfar.at[tower, :, at], gfar_send.at[g], gfar_recv.at[g],
            peers["behind"],
        )

    def gshared(g):
        at = strip(g)
        return remote(
            gfar.at[tower, :, at], gfar.at[tower, :, at], gshare_send.at[g], gshare_recv.at[g],
            peers["tower"],
        )

    def share(g):
        @pl.when(has_behind)
        def _():
            afar(g).wait_recv()
            shared(g).start()

    def compute(g):
        def swap():
            swapped_part(g).start()
            for copy in homeward(g):
                copy.start()

        def relay():
            at = strip(g)
            for copy in outgoing(g):
                copy.start()
            swapped_part(g).wait_recv()
            gpick[:, at] = jnp.where(uses_far == 1, part[tower, :, at], mate_part[:, at])

            @pl.when(has_behind)
            def _():
                far_back(g).start()
                for copy in back(g):
                    copy.start()

        settle(g, swap, relay)

    def finish(g):
        at = strip(g)

        @pl.when(has_ahead)
        def _():
            far_back(g).wait_recv()
            gshared(g).start()
            for copy in back(g):
                copy.wait_recv()

        for i in range(2):
            grads[i][:, at] = (core[i, :, at] + x_recv[i, :, at].astype(F32)).astype(BF16)
        for i, copy in enumerate(outgoing(g)):
            copy.wait_recv()
            outs[i][:, at] = (mine[i, :, at] + y_recv[i, :, at].astype(F32)).astype(BF16)

        @pl.when(has_ahead)
        def _():
            gshared(g).wait_recv()

        for i, copy in enumerate(homeward(g)):
            copy.wait_recv()
            more = jnp.where(chosen == 1, gfar[i, :, at].astype(F32), 0.0)
            grads[2 + i][:, at] = (own_recv[i, :, at].astype(F32) + more).astype(BF16)

    def step(g, carry):
        @pl.when(g + AHEAD < groups)
        def _():
            issue(g + AHEAD)

        @pl.when(g < groups)
        def _():
            for copy in incoming(g):
                copy.wait_recv()

            @pl.when(has_behind)
            def _():
                for copy in haloed(g):
                    copy.wait_recv()
                shared(g).wait_recv()

            score(g)
            exchange(g).start()

        @pl.when(g + 1 < groups)
        def _():
            share(g + 1)

        @pl.when(g >= LAG)
        def _():
            exchange(g - LAG).wait_recv()
            compute(g - LAG)

        return carry

    share(0)
    lax.fori_loop(0, groups + LAG, step, 0)

    def end(g, carry):
        finish(g)
        return carry

    lax.fori_loop(0, groups, end, 0)

    def close(g, carry):
        for copy in incoming(g) + outgoing(g) + homeward(g):
            copy.wait_send()
        exchange(g).wait_send()
        swapped_part(g).wait_send()

        @pl.when(has_ahead)
        def _():
            for copy in haloed(g):
                copy.wait_send()
            afar(g).wait_send()
            gshared(g).wait_send()

        @pl.when(has_behind)
        def _():
            shared(g).wait_send()
            far_back(g).wait_send()
            for copy in back(g):
                copy.wait_send()

        return carry

    lax.fori_loop(0, groups, close, 0)
    for copy in partners:
        copy.wait_send()

    @pl.when(has_ahead)
    def _():
        mask_ahead.wait_send()


def copy_kernel(*refs):
    count = len(refs) // 2
    sem = refs[-1]
    copies = [
        pltpu.make_async_copy(src, dst, sem.at[i])
        for i, (src, dst) in enumerate(zip(refs[:count], refs[count:-1]))
    ]
    for copy in copies:
        copy.start()
    for copy in copies:
        copy.wait()


def paired(
    queries, key_rows, value_rows, cross_queries, cross_keys, cross_values, grad_out,
    offsets, key_valid,
):
    blks = lax.axis_size("blk")
    values = [
        value[0] for value in (
            queries, key_rows, value_rows, cross_queries, cross_keys, cross_values, grad_out
        )
    ]
    rows, cols = queries.shape[1:]
    groups, wide = cols // (2 * HEAD), 2 * rows
    dma = pltpu.SemaphoreType.DMA
    full = jax.ShapeDtypeStruct((rows, cols), BF16)
    narrow = pltpu.VMEM((2, rows, cols), BF16)
    single = pltpu.VMEM((rows, cols), BF16)
    scored = pltpu.VMEM((groups, 5 * rows, wide), F32)
    stats = pltpu.VMEM((groups, 8, wide), F32)
    pairs = (dma((groups, 2)),) * 2
    ones = (dma((groups,)),) * 2
    outs = pl.pallas_call(
        functools.partial(fused_kernel, blks, rows, cols),
        out_shape=(pltpu.VMEM((rows, cols), BF16),) * 7,
        in_specs=[pl.BlockSpec(memory_space=pltpu.SMEM)] + [pl.BlockSpec(memory_space=pl.ANY)] * 8,
        out_specs=(pl.BlockSpec(memory_space=pltpu.VMEM),) * 7,
        scratch_shapes=[
            pltpu.VMEM((3, 2, rows, cols), BF16),
            narrow, narrow, narrow, narrow, single, single,
            pltpu.VMEM((2,) + key_valid.shape, jnp.int32),
            pltpu.VMEM((4, rows, wide), F32),
            scored, scored, stats, stats, stats,
            pltpu.VMEM((3, rows, cols), F32),
            pltpu.VMEM((3, rows, cols), BF16), pltpu.VMEM((3, rows, cols), BF16),
            pltpu.VMEM((2, rows, cols), F32),
            narrow, narrow, narrow, narrow, narrow, single, single, narrow,
            dma((7,)), dma((1,)), dma((1,)),
            dma((groups, 3)), dma((groups, 3)), *pairs,
            dma((2,)), dma((2,)), *ones, *ones,
            *ones, dma((groups, 3)), dma((groups, 3)), *pairs, *pairs,
            *ones, *ones, *ones,
        ],
        compiler_params=pltpu.CompilerParams(collective_id=0, has_side_effects=True),
        name="attend_pairs",
    )(offsets, *values, key_valid)
    outs = pl.pallas_call(
        copy_kernel,
        out_shape=(full,) * 7,
        in_specs=[pl.BlockSpec(memory_space=pl.ANY)] * 7,
        out_specs=(pl.BlockSpec(memory_space=pl.ANY),) * 7,
        scratch_shapes=[dma((7,))],
        compiler_params=pltpu.CompilerParams(vmem_limit_bytes=1 << 20),
        name="hand_over",
    )(*outs)
    return tuple(piece[None] for piece in outs)


def extended(block, sides, width):
    for axis, dim in sides:
        count = lax.axis_size(axis)
        forward = [(i, i + 1) for i in range(count - 1)]
        backward = [(target, source) for source, target in forward]
        low = lax.ppermute(
            lax.slice_in_dim(block, block.shape[dim] - width, None, axis=dim), axis, forward
        )
        high = lax.ppermute(lax.slice_in_dim(block, 0, width, axis=dim), axis, backward)
        block = jnp.concatenate([low, block, high], axis=dim)
    return block


def swapped(value, axis, bit):
    mask = 2**bit
    pairs = [(source, source ^ mask) for source in range(lax.axis_size(axis))]
    return lax.ppermute(value, axis, pairs)


def passed_along(block, axis, distance):
    devices = range(lax.axis_size(axis))
    route = [(i - distance, i) for i in devices if i - distance in devices]
    return lax.ppermute(block, axis, route)


def attend(query_tile, grad_tile, key_block, value_block, allowed, heads_here):
    score_scale = HEAD ** (-0.5)
    rows_count = query_tile.shape[0]
    keys_count = key_block.shape[0]
    q_heads = query_tile.reshape(rows_count, heads_here, HEAD)
    g_heads = grad_tile.reshape(rows_count, heads_here, HEAD)
    k_heads = key_block.reshape(keys_count, heads_here, HEAD)
    v_heads = value_block.reshape(keys_count, heads_here, HEAD)
    scores = (
        jnp.einsum("qhe,khe->hqk", q_heads, k_heads, preferred_element_type=jnp.float32)
        * score_scale
    )
    scores = jnp.where(allowed[None], scores, -1e30)
    row_max = jnp.max(scores, axis=2)
    unnormed = jnp.exp(scores - row_max[:, :, None])
    row_sum = jnp.sum(unnormed, axis=2)
    weights = unnormed / row_sum[:, :, None]
    prob_bf = weights.astype(jnp.bfloat16)
    result = jnp.einsum(
        "hqk,khe->qhe", prob_bf, v_heads, preferred_element_type=jnp.float32
    ).reshape(rows_count, -1)
    grad_probs = jnp.einsum("qhe,khe->hqk", g_heads, v_heads, preferred_element_type=jnp.float32)
    row_dot = jnp.sum(weights * grad_probs, axis=2)
    grad_scores = (weights * (grad_probs - row_dot[:, :, None]) * score_scale).astype(jnp.bfloat16)
    grad_query = jnp.einsum(
        "hqk,khe->qhe", grad_scores, k_heads, preferred_element_type=jnp.float32
    ).reshape(rows_count, -1)
    grad_key = jnp.einsum(
        "hqk,qhe->khe", grad_scores, q_heads, preferred_element_type=jnp.float32
    ).reshape(keys_count, -1)
    grad_value = jnp.einsum(
        "hqk,qhe->khe", prob_bf, g_heads, preferred_element_type=jnp.float32
    ).reshape(keys_count, -1)
    return (result, grad_query, grad_key, grad_value, jnp.stack((row_max, row_sum, row_dot)))


def shards(
    queries,
    key_rows,
    value_rows,
    cross_queries,
    cross_keys,
    cross_values,
    grad_out,
    offsets,
    key_valid,
):
    seq_count = lax.axis_size("seq")
    heads_here = HEADS // seq_count
    local_rows = (
        queries[0],
        key_rows[0],
        value_rows[0],
        cross_queries[0],
        cross_keys[0],
        cross_values[0],
        grad_out[0],
    )
    query_here, key_here, value_here, cross_query, cross_key, cross_value, cotangent = (
        lax.all_to_all(local_rows[0], "seq", split_axis=1, concat_axis=0, tiled=True),
        lax.all_to_all(local_rows[1], "seq", split_axis=1, concat_axis=0, tiled=True),
        lax.all_to_all(local_rows[2], "seq", split_axis=1, concat_axis=0, tiled=True),
        lax.all_to_all(local_rows[3], "seq", split_axis=1, concat_axis=0, tiled=True),
        lax.all_to_all(local_rows[4], "seq", split_axis=1, concat_axis=0, tiled=True),
        lax.all_to_all(local_rows[5], "seq", split_axis=1, concat_axis=0, tiled=True),
        lax.all_to_all(local_rows[6], "seq", split_axis=1, concat_axis=0, tiled=True),
    )
    block_len = query_here.shape[0]
    columns = query_here.shape[1]
    half_width = min(WINDOW // 2, block_len // 2)
    tile_rows = min(TILE, block_len)
    tile_count = block_len // tile_rows
    window_span = tile_rows + 2 * half_width
    tower_id = lax.axis_index("tower")
    block_id = lax.axis_index("blk")
    block_mask = lax.all_gather(key_valid, "seq", axis=1, tiled=True)
    mask_ext = extended(block_mask, (("blk", 1),), half_width)
    self_valid = lax.dynamic_index_in_dim(mask_ext, tower_id, 0, keepdims=False)
    other_valid = lax.dynamic_index_in_dim(mask_ext, 1 - tower_id, 0, keepdims=False)
    pair_ext = extended(jnp.stack((key_here, value_here)), (("blk", 1),), half_width)
    partner = swapped(jnp.stack((cross_key, cross_value)), "tower", 0)
    partner_ext = extended(partner, (("blk", 1),), half_width)
    align_shift = offsets[tower_id, block_id]
    band_start = half_width + align_shift
    band = lax.dynamic_slice_in_dim(partner_ext, band_start, block_len, 1)
    band_valid = lax.dynamic_slice_in_dim(other_valid, band_start, block_len) > 0
    rows_local = jnp.arange(tile_rows)
    keys_local = jnp.arange(window_span)
    near = jnp.abs(rows_local[:, None] + half_width - keys_local[None, :]) <= half_width

    def self_step(carry, tile_index):
        grad_key_acc, grad_value_acc = carry
        tile_start = tile_index * tile_rows
        query_tile = lax.dynamic_slice_in_dim(query_here, tile_start, tile_rows, 0)
        grad_tile = lax.dynamic_slice_in_dim(cotangent, tile_start, tile_rows, 0)
        key_window = lax.dynamic_slice_in_dim(pair_ext[0], tile_start, window_span, 0)
        value_window = lax.dynamic_slice_in_dim(pair_ext[1], tile_start, window_span, 0)
        allowed = (
            near & (lax.dynamic_slice_in_dim(self_valid, tile_start, window_span) > 0)[None, :]
        )
        result, grad_query, grad_key, grad_value, stats = attend(
            query_tile, grad_tile, key_window, value_window, allowed, heads_here
        )
        grad_key_acc = lax.dynamic_update_slice_in_dim(
            grad_key_acc,
            lax.dynamic_slice_in_dim(grad_key_acc, tile_start, window_span, 0) + grad_key,
            tile_start,
            0,
        )
        grad_value_acc = lax.dynamic_update_slice_in_dim(
            grad_value_acc,
            lax.dynamic_slice_in_dim(grad_value_acc, tile_start, window_span, 0) + grad_value,
            tile_start,
            0,
        )
        return ((grad_key_acc, grad_value_acc), (result, grad_query, stats))

    def cross_step(carry, tile_index):
        grad_key_acc, grad_value_acc = carry
        tile_start = tile_index * tile_rows
        query_tile = lax.dynamic_slice_in_dim(cross_query, tile_start, tile_rows, 0)
        grad_tile = lax.dynamic_slice_in_dim(cotangent, tile_start, tile_rows, 0)
        result, grad_query, grad_key, grad_value, stats = attend(
            query_tile, grad_tile, band[0], band[1], band_valid[None, :], heads_here
        )
        return ((grad_key_acc + grad_key, grad_value_acc + grad_value), (result, grad_query))

    zeros_ext = jnp.zeros((block_len + 2 * half_width, columns), jnp.float32)
    zeros_band = jnp.zeros((block_len, columns), jnp.float32)
    tile_ids = jnp.arange(tile_count)
    (self_gk, self_gv), (self_out, self_gq, self_stats) = lax.scan(
        self_step, (zeros_ext, zeros_ext), tile_ids
    )
    (cross_gk, cross_gv), (cross_out, cross_gq) = lax.scan(
        cross_step, (zeros_band, zeros_band), tile_ids
    )
    self_out = self_out.reshape(block_len, columns)
    cross_out = cross_out.reshape(block_len, columns)
    self_stats = jnp.transpose(self_stats, (1, 2, 0, 3)).reshape(3, heads_here, block_len)
    attended = (self_out + cross_out).astype(jnp.bfloat16)
    cross_ext = jnp.zeros((2, block_len + 2 * half_width, columns), jnp.float32)
    cross_ext = lax.dynamic_update_slice_in_dim(
        cross_ext, jnp.stack((cross_gk, cross_gv)), band_start, 1
    )
    self_ext = jnp.stack((self_gk, self_gv))
    self_core = self_ext[:, half_width : half_width + block_len]
    cross_core = cross_ext[:, half_width : half_width + block_len]
    upper_cut = block_len - half_width
    lower_send = jnp.concatenate((self_ext[:, :half_width], cross_ext[:, :half_width]), 0)
    upper_send = jnp.concatenate(
        (self_ext[:, block_len + half_width :], cross_ext[:, block_len + half_width :]), 0
    )
    from_above = passed_along(lower_send.astype(jnp.bfloat16), "blk", -1).astype(lower_send.dtype)
    from_below = passed_along(upper_send.astype(jnp.bfloat16), "blk", 1).astype(upper_send.dtype)
    self_core = (
        self_core.at[:, upper_cut:].add(from_above[:2]).at[:, :half_width].add(from_below[:2])
    )
    cross_core = (
        cross_core.at[:, upper_cut:].add(from_above[2:]).at[:, :half_width].add(from_below[2:])
    )
    returned = swapped(cross_core.astype(jnp.bfloat16), "tower", 0)
    head_outs = (
        attended,
        self_gq.reshape(block_len, columns).astype(jnp.bfloat16),
        self_core[0].astype(jnp.bfloat16),
        self_core[1].astype(jnp.bfloat16),
        cross_gq.reshape(block_len, columns).astype(jnp.bfloat16),
        returned[0],
        returned[1],
    )
    token_outs = (
        lax.all_to_all(head_outs[0], "seq", split_axis=0, concat_axis=1, tiled=True),
        lax.all_to_all(head_outs[1], "seq", split_axis=0, concat_axis=1, tiled=True),
        lax.all_to_all(head_outs[2], "seq", split_axis=0, concat_axis=1, tiled=True),
        lax.all_to_all(head_outs[3], "seq", split_axis=0, concat_axis=1, tiled=True),
        lax.all_to_all(head_outs[4], "seq", split_axis=0, concat_axis=1, tiled=True),
        lax.all_to_all(head_outs[5], "seq", split_axis=0, concat_axis=1, tiled=True),
        lax.all_to_all(head_outs[6], "seq", split_axis=0, concat_axis=1, tiled=True),
    )
    return tuple((piece[None] for piece in token_outs))


def solution(mesh):
    in_specs = (
        P("tower", ("blk", "seq"), None),
        P("tower", ("blk", "seq"), None),
        P("tower", ("blk", "seq"), None),
        P("tower", ("blk", "seq"), None),
        P("tower", ("blk", "seq"), None),
        P("tower", ("blk", "seq"), None),
        P("tower", ("blk", "seq"), None),
        P(),
        P(None, ("blk", "seq")),
    )
    out_specs = (
        P("tower", ("blk", "seq"), None),
        P("tower", ("blk", "seq"), None),
        P("tower", ("blk", "seq"), None),
        P("tower", ("blk", "seq"), None),
        P("tower", ("blk", "seq"), None),
        P("tower", ("blk", "seq"), None),
        P("tower", ("blk", "seq"), None),
    )
    body = paired if mesh.shape["seq"] == 2 else shards
    return jax.shard_map(body, mesh=mesh, in_specs=in_specs, out_specs=out_specs, check_vma=False)
```

```python
import functools

import jax
import jax.numpy as jnp
from jax import lax
from jax.experimental import pallas as pl
from jax.experimental.pallas import tpu as pltpu
from jax.sharding import PartitionSpec as P

HEADS = 16
HEAD = 64
WINDOW = 2048
TILE = 512
LAG = 4
AHEAD = 5
MESH = pl.DeviceIdType.MESH
F32, BF16 = jnp.float32, jnp.bfloat16


def places():
    tower, blk, seq = lax.axis_index("tower"), lax.axis_index("blk"), lax.axis_index("seq")
    toward = 2 * seq - 1
    peers = dict(
        y=(tower, blk, 1 - seq),
        tower=(1 - tower, blk, seq),
        ahead=(tower, blk + toward, seq),
        behind=(tower, blk - toward, seq),
    )
    return tower, blk, seq, peers


def greet(has_ahead, has_behind, peers):
    barrier = pltpu.get_barrier_semaphore()
    for name in ("y", "tower"):
        pl.semaphore_signal(barrier, inc=1, device_id=peers[name], device_id_type=MESH)
    for name, present in (("ahead", has_ahead), ("behind", has_behind)):
        @pl.when(present)
        def _():
            pl.semaphore_signal(barrier, inc=1, device_id=peers[name], device_id_type=MESH)


def meet(has_ahead, has_behind):
    count = 2 + jnp.where(has_ahead, 1, 0) + jnp.where(has_behind, 1, 0)
    pl.semaphore_wait(pltpu.get_barrier_semaphore(), count)


def remote(src, dst, send, recv, device):
    return pltpu.make_async_remote_copy(
        src_ref=src, dst_ref=dst, send_sem=send, recv_sem=recv,
        device_id=device, device_id_type=MESH,
    )


def fused_kernel(
    blks, rows, cols,
    off_ref, q_ref, k_ref, v_ref, cq_ref, ck_ref, cv_ref, g_ref, m_ref,
    o_out, gq_out, gk_out, gv_out, gcq_out, gck_out, gcv_out,
    side, pair, halo, partner, far, mate, pick, mask_ext, bias,
    exps, dots, sums, stat, peer_stat,
    mine, y_stage, y_recv, core, x_stage, x_recv, own_stage, own_recv,
    part, mate_part, gpick, gfar,
    local_sem, mask_send, mask_recv, in_send, in_recv, halo_send, halo_recv,
    partner_send, partner_recv, far_send, far_recv, share_send, share_recv,
    stat_send, stat_recv, y_send, y_recv_sem, x_send, x_recv_sem, own_send, own_recv_sem,
    swap_send, swap_recv, gfar_send, gfar_recv, gshare_send, gshare_recv,
):
    tower, blk, seq, peers = places()
    half, wide = rows, 2 * HEAD
    groups = cols // wide
    scale = HEAD ** (-0.5)
    has_low, has_high = blk > 0, blk < blks - 1
    has_ahead = ((seq == 1) & has_high) | ((seq == 0) & has_low)
    has_behind = ((seq == 1) & has_low) | ((seq == 0) & has_high)
    outs = [o_out, gq_out, gcq_out]
    grads = [gk_out, gv_out, gck_out, gcv_out]

    off = off_ref[tower, blk]
    off_ahead = off_ref[tower, jnp.clip(blk + 2 * seq - 1, 0, blks - 1)]
    chosen = jnp.where(seq == 1, jnp.where(off_ahead > 0, 1, 0), jnp.where(off_ahead < 0, 1, 0))
    uses_far = jnp.where(seq == 0, jnp.where(off > 0, 1, 0), jnp.where(off < 0, 1, 0))
    far_from = jnp.where(seq == 0, 0, jnp.where(off < 0, half + off, half))
    far_to = jnp.where(seq == 0, jnp.maximum(off, 0), half)

    def strip(g):
        return pl.ds(pl.multiple_of(g * wide, wide), wide)

    def incoming(g):
        at = strip(g)
        return [
            remote(ref.at[:, at], side.at[i, 1, :, at], in_send.at[g, i], in_recv.at[g, i], peers["y"])
            for i, ref in enumerate((q_ref, cq_ref, g_ref))
        ]

    def haloed(g):
        at = strip(g)
        return [
            remote(
                ref.at[:, at], halo.at[i, :, at], halo_send.at[g, i], halo_recv.at[g, i],
                peers["ahead"],
            )
            for i, ref in enumerate((k_ref, v_ref))
        ]

    def afar(g):
        at = strip(g)
        return remote(
            pick.at[:, at], far.at[tower, :, at], far_send.at[g], far_recv.at[g], peers["ahead"]
        )

    def shared(g):
        at = strip(g)
        return remote(
            far.at[tower, :, at], far.at[tower, :, at], share_send.at[g], share_recv.at[g],
            peers["tower"],
        )

    partners = [
        remote(ref, partner.at[i], partner_send.at[i], partner_recv.at[i], peers["tower"])
        for i, ref in enumerate((ck_ref, cv_ref))
    ]
    mask_ahead = remote(m_ref, mask_ext.at[1], mask_send.at[0], mask_recv.at[0], peers["ahead"])

    def issue(g):
        for copy in incoming(g):
            copy.start()

    def issue_halo(g):
        @pl.when(has_ahead)
        def _():
            for copy in haloed(g):
                copy.start()

    def issue_far(g):
        @pl.when(has_ahead)
        def _():
            afar(g).start()

    greet(has_ahead, has_behind, peers)
    locals_ = [
        pltpu.make_async_copy(k_ref, pair.at[0], local_sem.at[0]),
        pltpu.make_async_copy(v_ref, pair.at[1], local_sem.at[1]),
        pltpu.make_async_copy(m_ref, mask_ext.at[0], local_sem.at[2]),
        pltpu.make_async_copy(q_ref, side.at[0, 0], local_sem.at[3]),
        pltpu.make_async_copy(cq_ref, side.at[1, 0], local_sem.at[4]),
        pltpu.make_async_copy(g_ref, side.at[2, 0], local_sem.at[5]),
    ]
    for copy in locals_:
        copy.start()
    for chain, ref in enumerate((ck_ref, cv_ref)):
        @pl.when(tower == chain)
        def _():
            pltpu.make_async_copy(ref, mate, local_sem.at[6]).start()

    @pl.when(jnp.logical_not(has_behind))
    def _():
        halo[...] = jnp.zeros(halo.shape, BF16)
        far[...] = jnp.zeros(far.shape, BF16)
        mask_ext[1] = jnp.zeros(mask_ext.shape[1:], jnp.int32)

    @pl.when(jnp.logical_not(has_ahead))
    def _():
        x_recv[...] = jnp.zeros(x_recv.shape, BF16)
        gfar[...] = jnp.zeros(gfar.shape, BF16)

    meet(has_ahead, has_behind)
    first = min(AHEAD, groups)
    issue(0)

    @pl.when(has_ahead)
    def _():
        mask_ahead.start()

    for copy in partners:
        copy.start()
    for g in range(1, first):
        issue(g)
    for g in range(min(2, groups)):
        issue_halo(g)
    for copy in locals_:
        copy.wait()
    for chain, ref in enumerate((ck_ref, cv_ref)):
        @pl.when(tower == chain)
        def _():
            pltpu.make_async_copy(ref, mate, local_sem.at[6]).wait()
    for copy in partners:
        copy.wait_recv()
    pick[...] = jnp.where(chosen == 1, mate[...], partner[tower])
    for g in range(groups):
        if g >= 2:
            issue_halo(g)
        issue_far(g)

    @pl.when(has_behind)
    def _():
        mask_ahead.wait_recv()

    def column(part_at, chain):
        row = jnp.where(
            chain == 0, mask_ext[part_at, 0:1, :].astype(F32), mask_ext[part_at, 1:2, :].astype(F32)
        )
        return jnp.transpose(jnp.broadcast_to(row, (half, half)))

    row_at = lax.broadcasted_iota(jnp.int32, (half, half), 0)
    col_at = lax.broadcasted_iota(jnp.int32, (half, half), 1)
    apart = (row_at - col_at) * jnp.where(seq == 0, 1, -1)
    from_far = (row_at >= far_from) & (row_at < far_to)
    own_valid, halo_valid = column(0, tower), column(1, tower)
    cross_valid = jnp.where(from_far, column(1, 1 - tower), column(0, 1 - tower))
    allowed = (
        own_valid > 0,
        (own_valid > 0) & (apart >= 0),
        (halo_valid > 0) & (apart <= 0),
        cross_valid > 0,
    )
    for i, near in enumerate(allowed):
        add = jnp.where(near, 0.0, -1e30)
        bias[i, :, :half] = add
        bias[i, :, half:] = add

    lanes = lax.broadcasted_iota(jnp.int32, (half, wide), 1)
    zero = jnp.zeros((half, wide), BF16)

    def split(tile):
        return jnp.concatenate(
            (jnp.where(lanes < HEAD, tile, zero), jnp.where(lanes < HEAD, zero, tile)), 0
        )

    def dot_t(a, b):
        return lax.dot_general(a, b, (((1,), (1,)), ((), ())), preferred_element_type=F32)

    def dot(a, b):
        return jnp.dot(a, b, preferred_element_type=F32)

    def own_heads(both):
        return jnp.concatenate((both[:HEAD, :half], both[HEAD:, half:]), 0)

    def turned(x):
        return jnp.transpose(x.astype(F32)).astype(BF16)

    def operands(g):
        at = strip(g)
        query = [split(side[0, i, :, at] * BF16(scale)) for i in range(2)]
        cross = [split(side[1, i, :, at] * BF16(scale)) for i in range(2)]
        cot = [split(side[2, i, :, at]) for i in range(2)]
        near = [pair[i, :, at] for i in range(2)]
        edge = [halo[i, :, at] for i in range(2)]
        band = [jnp.where(from_far, far[i, :, at], partner[i, :, at]) for i in range(2)]
        return query, cross, cot, near, edge, band

    spans = (slice(0, half), slice(half, 3 * half), slice(3 * half, 4 * half), slice(4 * half, 5 * half))

    def score(g):
        query, cross, cot, near, edge, band = operands(g)
        keys = (near, [jnp.concatenate((n, e), 0) for n, e in zip(near, edge)], band, band)
        asks = (query[0], query[1], cross[0], cross[1])
        adds = (bias[0], jnp.concatenate((bias[1], bias[2]), 0), bias[3], bias[3])
        for kind in range(4):
            key, value = keys[kind]
            scores = dot_t(key, asks[kind]) + adds[kind]
            products = dot_t(value, cot[kind % 2])
            top = jnp.max(scores, axis=0, keepdims=True)
            unnormed = jnp.exp(scores - top)
            total = jnp.sum(unnormed, axis=0, keepdims=True)
            exps[g, spans[kind], :] = unnormed
            dots[g, spans[kind], :] = products
            sums[g, kind : kind + 1, :] = total
            stat[g, 2 * kind : 2 * kind + 1, :] = top + jnp.log(total)
            stat[g, 2 * kind + 1 : 2 * kind + 2, :] = (
                jnp.sum(unnormed * products, axis=0, keepdims=True) / total
            )

    def exchange(g):
        return remote(
            stat.at[g], peer_stat.at[g], stat_send.at[g], stat_recv.at[g], peers["y"]
        )

    def weigh(g, kind):
        other = kind ^ 1
        here, there = stat[g, 2 * kind : 2 * kind + 1, :], peer_stat[g, 2 * other : 2 * other + 1, :]
        top = jnp.maximum(here, there)
        whole = top + jnp.log(jnp.exp(here - top) + jnp.exp(there - top))
        share_here, share_there = jnp.exp(here - whole), jnp.exp(there - whole)
        row_dot = (
            share_here * stat[g, 2 * kind + 1 : 2 * kind + 2, :]
            + share_there * peer_stat[g, 2 * other + 1 : 2 * other + 2, :]
        )
        weights = exps[g, spans[kind], :] * (share_here / sums[g, kind : kind + 1, :])
        grad_scores = weights * (dots[g, spans[kind], :] - row_dot)
        return weights.astype(BF16), grad_scores.astype(BF16)

    def settle(g, swap, relay):
        at = strip(g)
        query, cross, cot, near, edge, band = operands(g)
        band_t = [turned(x) for x in band]
        prob, slope = zip(*[weigh(g, kind) for kind in (2, 3)])
        cross_out = [own_heads(dot(band_t[1], prob[i])) for i in range(2)]
        cross_grad = [own_heads(dot(band_t[0], slope[i])) * scale for i in range(2)]
        band_grad = (
            dot(slope[0], cross[0]) + dot(slope[1], cross[1]),
            dot(prob[0], cot[0]) + dot(prob[1], cot[1]),
        )
        for i in range(2):
            part[i, :, at] = jnp.where(from_far, band_grad[i], 0.0).astype(BF16)
            own_stage[i, :, at] = jnp.where(from_far, 0.0, band_grad[i]).astype(BF16)
        swap()
        near_t = [turned(x) for x in near]
        both_t = [jnp.concatenate((n, turned(e)), 1) for n, e in zip(near_t, edge)]
        prob, slope = zip(*[weigh(g, kind) for kind in (0, 1)])
        self_out = [own_heads(dot(near_t[1], prob[0])), own_heads(dot(both_t[1], prob[1]))]
        self_grad = [own_heads(dot(near_t[0], slope[0])), own_heads(dot(both_t[0], slope[1]))]
        ours = (self_out[0] + cross_out[0], self_grad[0] * scale, cross_grad[0])
        theirs = (self_out[1] + cross_out[1], self_grad[1] * scale, cross_grad[1])
        for i in range(3):
            y_stage[i, :, at] = turned(theirs[i])
            mine[i, :, at] = jnp.transpose(ours[i])
        for i, (left, right, ask) in enumerate(
            ((slope[0], slope[1], query), (prob[0], prob[1], cot))
        ):
            core[i, :, at] = dot(left, ask[0]) + dot(right[:half], ask[1])
            x_stage[i, :, at] = dot(right[half:], ask[1]).astype(BF16)
        relay()

    def outgoing(g):
        at = strip(g)
        return [
            remote(
                y_stage.at[i, :, at], y_recv.at[i, :, at], y_send.at[g, i], y_recv_sem.at[g, i],
                peers["y"],
            )
            for i in range(3)
        ]

    def back(g):
        at = strip(g)
        return [
            remote(
                x_stage.at[i, :, at], x_recv.at[i, :, at], x_send.at[g, i], x_recv_sem.at[g, i],
                peers["behind"],
            )
            for i in range(2)
        ]

    def homeward(g):
        at = strip(g)
        return [
            remote(
                own_stage.at[i, :, at], own_recv.at[i, :, at],
                own_send.at[g, i], own_recv_sem.at[g, i], peers["tower"],
            )
            for i in range(2)
        ]

    def swapped_part(g):
        at = strip(g)
        return remote(
            part.at[1 - tower, :, at], mate_part.at[:, at], swap_send.at[g], swap_recv.at[g],
            peers["tower"],
        )

    def far_back(g):
        at = strip(g)
        return remote(
            gpick.at[:, at], gfar.at[tower, :, at], gfar_send.at[g], gfar_recv.at[g],
            peers["behind"],
        )

    def gshared(g):
        at = strip(g)
        return remote(
            gfar.at[tower, :, at], gfar.at[tower, :, at], gshare_send.at[g], gshare_recv.at[g],
            peers["tower"],
        )

    def share(g):
        @pl.when(has_behind)
        def _():
            afar(g).wait_recv()
            shared(g).start()

    def compute(g):
        def swap():
            swapped_part(g).start()
            for copy in homeward(g):
                copy.start()

        def relay():
            at = strip(g)
            for copy in outgoing(g):
                copy.start()
            swapped_part(g).wait_recv()
            gpick[:, at] = jnp.where(uses_far == 1, part[tower, :, at], mate_part[:, at])

            @pl.when(has_behind)
            def _():
                far_back(g).start()
                for copy in back(g):
                    copy.start()

        settle(g, swap, relay)

    def finish(g):
        at = strip(g)

        @pl.when(has_ahead)
        def _():
            far_back(g).wait_recv()
            gshared(g).start()
            for copy in back(g):
                copy.wait_recv()

        for i in range(2):
            grads[i][:, at] = (core[i, :, at] + x_recv[i, :, at].astype(F32)).astype(BF16)
        for i, copy in enumerate(outgoing(g)):
            copy.wait_recv()
            outs[i][:, at] = (mine[i, :, at] + y_recv[i, :, at].astype(F32)).astype(BF16)

        @pl.when(has_ahead)
        def _():
            gshared(g).wait_recv()

        for i, copy in enumerate(homeward(g)):
            copy.wait_recv()
            more = jnp.where(chosen == 1, gfar[i, :, at].astype(F32), 0.0)
            grads[2 + i][:, at] = (own_recv[i, :, at].astype(F32) + more).astype(BF16)

    def step(g, carry):
        @pl.when(g + AHEAD < groups)
        def _():
            issue(g + AHEAD)

        @pl.when(g < groups)
        def _():
            for copy in incoming(g):
                copy.wait_recv()

            @pl.when(has_behind)
            def _():
                for copy in haloed(g):
                    copy.wait_recv()
                shared(g).wait_recv()

            score(g)
            exchange(g).start()

        @pl.when(g + 1 < groups)
        def _():
            share(g + 1)

        @pl.when(g >= LAG)
        def _():
            exchange(g - LAG).wait_recv()
            compute(g - LAG)

        return carry

    share(0)
    lax.fori_loop(0, groups + LAG, step, 0)

    def end(g, carry):
        finish(g)
        for copy in incoming(g) + outgoing(g) + homeward(g):
            copy.wait_send()
        exchange(g).wait_send()
        swapped_part(g).wait_send()

        @pl.when(has_ahead)
        def _():
            for copy in haloed(g):
                copy.wait_send()
            afar(g).wait_send()
            gshared(g).wait_send()

        @pl.when(has_behind)
        def _():
            shared(g).wait_send()
            far_back(g).wait_send()
            for copy in back(g):
                copy.wait_send()

        return carry

    for copy in partners:
        copy.wait_send()

    @pl.when(has_ahead)
    def _():
        mask_ahead.wait_send()

    lax.fori_loop(0, groups, end, 0)


def copy_kernel(*refs):
    count = len(refs) // 2
    sem = refs[-1]
    copies = [
        pltpu.make_async_copy(src, dst, sem.at[i])
        for i, (src, dst) in enumerate(zip(refs[:count], refs[count:-1]))
    ]
    for copy in copies:
        copy.start()
    for copy in copies:
        copy.wait()


def paired(
    queries, key_rows, value_rows, cross_queries, cross_keys, cross_values, grad_out,
    offsets, key_valid,
):
    blks = lax.axis_size("blk")
    values = [
        value[0] for value in (
            queries, key_rows, value_rows, cross_queries, cross_keys, cross_values, grad_out
        )
    ]
    rows, cols = queries.shape[1:]
    groups, wide = cols // (2 * HEAD), 2 * rows
    dma = pltpu.SemaphoreType.DMA
    full = jax.ShapeDtypeStruct((rows, cols), BF16)
    narrow = pltpu.VMEM((2, rows, cols), BF16)
    single = pltpu.VMEM((rows, cols), BF16)
    scored = pltpu.VMEM((groups, 5 * rows, wide), F32)
    stats = pltpu.VMEM((groups, 8, wide), F32)
    pairs = (dma((groups, 2)),) * 2
    ones = (dma((groups,)),) * 2
    outs = pl.pallas_call(
        functools.partial(fused_kernel, blks, rows, cols),
        out_shape=(pltpu.VMEM((rows, cols), BF16),) * 7,
        in_specs=[pl.BlockSpec(memory_space=pltpu.SMEM)] + [pl.BlockSpec(memory_space=pl.ANY)] * 8,
        out_specs=(pl.BlockSpec(memory_space=pltpu.VMEM),) * 7,
        scratch_shapes=[
            pltpu.VMEM((3, 2, rows, cols), BF16),
            narrow, narrow, narrow, narrow, single, single,
            pltpu.VMEM((2,) + key_valid.shape, jnp.int32),
            pltpu.VMEM((4, rows, wide), F32),
            scored, scored, stats, stats, stats,
            pltpu.VMEM((3, rows, cols), F32),
            pltpu.VMEM((3, rows, cols), BF16), pltpu.VMEM((3, rows, cols), BF16),
            pltpu.VMEM((2, rows, cols), F32),
            narrow, narrow, narrow, narrow, narrow, single, single, narrow,
            dma((7,)), dma((1,)), dma((1,)),
            dma((groups, 3)), dma((groups, 3)), *pairs,
            dma((2,)), dma((2,)), *ones, *ones,
            *ones, dma((groups, 3)), dma((groups, 3)), *pairs, *pairs,
            *ones, *ones, *ones,
        ],
        compiler_params=pltpu.CompilerParams(collective_id=0, has_side_effects=True),
        name="attend_pairs",
    )(offsets, *values, key_valid)
    outs = pl.pallas_call(
        copy_kernel,
        out_shape=(full,) * 7,
        in_specs=[pl.BlockSpec(memory_space=pl.ANY)] * 7,
        out_specs=(pl.BlockSpec(memory_space=pl.ANY),) * 7,
        scratch_shapes=[dma((7,))],
        compiler_params=pltpu.CompilerParams(vmem_limit_bytes=1 << 20),
        name="hand_over",
    )(*outs)
    return tuple(piece[None] for piece in outs)


def extended(block, sides, width):
    for axis, dim in sides:
        count = lax.axis_size(axis)
        forward = [(i, i + 1) for i in range(count - 1)]
        backward = [(target, source) for source, target in forward]
        low = lax.ppermute(
            lax.slice_in_dim(block, block.shape[dim] - width, None, axis=dim), axis, forward
        )
        high = lax.ppermute(lax.slice_in_dim(block, 0, width, axis=dim), axis, backward)
        block = jnp.concatenate([low, block, high], axis=dim)
    return block


def swapped(value, axis, bit):
    mask = 2**bit
    pairs = [(source, source ^ mask) for source in range(lax.axis_size(axis))]
    return lax.ppermute(value, axis, pairs)


def passed_along(block, axis, distance):
    devices = range(lax.axis_size(axis))
    route = [(i - distance, i) for i in devices if i - distance in devices]
    return lax.ppermute(block, axis, route)


def attend(query_tile, grad_tile, key_block, value_block, allowed, heads_here):
    score_scale = HEAD ** (-0.5)
    rows_count = query_tile.shape[0]
    keys_count = key_block.shape[0]
    q_heads = query_tile.reshape(rows_count, heads_here, HEAD)
    g_heads = grad_tile.reshape(rows_count, heads_here, HEAD)
    k_heads = key_block.reshape(keys_count, heads_here, HEAD)
    v_heads = value_block.reshape(keys_count, heads_here, HEAD)
    scores = (
        jnp.einsum("qhe,khe->hqk", q_heads, k_heads, preferred_element_type=jnp.float32)
        * score_scale
    )
    scores = jnp.where(allowed[None], scores, -1e30)
    row_max = jnp.max(scores, axis=2)
    unnormed = jnp.exp(scores - row_max[:, :, None])
    row_sum = jnp.sum(unnormed, axis=2)
    weights = unnormed / row_sum[:, :, None]
    prob_bf = weights.astype(jnp.bfloat16)
    result = jnp.einsum(
        "hqk,khe->qhe", prob_bf, v_heads, preferred_element_type=jnp.float32
    ).reshape(rows_count, -1)
    grad_probs = jnp.einsum("qhe,khe->hqk", g_heads, v_heads, preferred_element_type=jnp.float32)
    row_dot = jnp.sum(weights * grad_probs, axis=2)
    grad_scores = (weights * (grad_probs - row_dot[:, :, None]) * score_scale).astype(jnp.bfloat16)
    grad_query = jnp.einsum(
        "hqk,khe->qhe", grad_scores, k_heads, preferred_element_type=jnp.float32
    ).reshape(rows_count, -1)
    grad_key = jnp.einsum(
        "hqk,qhe->khe", grad_scores, q_heads, preferred_element_type=jnp.float32
    ).reshape(keys_count, -1)
    grad_value = jnp.einsum(
        "hqk,qhe->khe", prob_bf, g_heads, preferred_element_type=jnp.float32
    ).reshape(keys_count, -1)
    return (result, grad_query, grad_key, grad_value, jnp.stack((row_max, row_sum, row_dot)))


def shards(
    queries,
    key_rows,
    value_rows,
    cross_queries,
    cross_keys,
    cross_values,
    grad_out,
    offsets,
    key_valid,
):
    seq_count = lax.axis_size("seq")
    heads_here = HEADS // seq_count
    local_rows = (
        queries[0],
        key_rows[0],
        value_rows[0],
        cross_queries[0],
        cross_keys[0],
        cross_values[0],
        grad_out[0],
    )
    query_here, key_here, value_here, cross_query, cross_key, cross_value, cotangent = (
        lax.all_to_all(local_rows[0], "seq", split_axis=1, concat_axis=0, tiled=True),
        lax.all_to_all(local_rows[1], "seq", split_axis=1, concat_axis=0, tiled=True),
        lax.all_to_all(local_rows[2], "seq", split_axis=1, concat_axis=0, tiled=True),
        lax.all_to_all(local_rows[3], "seq", split_axis=1, concat_axis=0, tiled=True),
        lax.all_to_all(local_rows[4], "seq", split_axis=1, concat_axis=0, tiled=True),
        lax.all_to_all(local_rows[5], "seq", split_axis=1, concat_axis=0, tiled=True),
        lax.all_to_all(local_rows[6], "seq", split_axis=1, concat_axis=0, tiled=True),
    )
    block_len = query_here.shape[0]
    columns = query_here.shape[1]
    half_width = min(WINDOW // 2, block_len // 2)
    tile_rows = min(TILE, block_len)
    tile_count = block_len // tile_rows
    window_span = tile_rows + 2 * half_width
    tower_id = lax.axis_index("tower")
    block_id = lax.axis_index("blk")
    block_mask = lax.all_gather(key_valid, "seq", axis=1, tiled=True)
    mask_ext = extended(block_mask, (("blk", 1),), half_width)
    self_valid = lax.dynamic_index_in_dim(mask_ext, tower_id, 0, keepdims=False)
    other_valid = lax.dynamic_index_in_dim(mask_ext, 1 - tower_id, 0, keepdims=False)
    pair_ext = extended(jnp.stack((key_here, value_here)), (("blk", 1),), half_width)
    partner = swapped(jnp.stack((cross_key, cross_value)), "tower", 0)
    partner_ext = extended(partner, (("blk", 1),), half_width)
    align_shift = offsets[tower_id, block_id]
    band_start = half_width + align_shift
    band = lax.dynamic_slice_in_dim(partner_ext, band_start, block_len, 1)
    band_valid = lax.dynamic_slice_in_dim(other_valid, band_start, block_len) > 0
    rows_local = jnp.arange(tile_rows)
    keys_local = jnp.arange(window_span)
    near = jnp.abs(rows_local[:, None] + half_width - keys_local[None, :]) <= half_width

    def self_step(carry, tile_index):
        grad_key_acc, grad_value_acc = carry
        tile_start = tile_index * tile_rows
        query_tile = lax.dynamic_slice_in_dim(query_here, tile_start, tile_rows, 0)
        grad_tile = lax.dynamic_slice_in_dim(cotangent, tile_start, tile_rows, 0)
        key_window = lax.dynamic_slice_in_dim(pair_ext[0], tile_start, window_span, 0)
        value_window = lax.dynamic_slice_in_dim(pair_ext[1], tile_start, window_span, 0)
        allowed = (
            near & (lax.dynamic_slice_in_dim(self_valid, tile_start, window_span) > 0)[None, :]
        )
        result, grad_query, grad_key, grad_value, stats = attend(
            query_tile, grad_tile, key_window, value_window, allowed, heads_here
        )
        grad_key_acc = lax.dynamic_update_slice_in_dim(
            grad_key_acc,
            lax.dynamic_slice_in_dim(grad_key_acc, tile_start, window_span, 0) + grad_key,
            tile_start,
            0,
        )
        grad_value_acc = lax.dynamic_update_slice_in_dim(
            grad_value_acc,
            lax.dynamic_slice_in_dim(grad_value_acc, tile_start, window_span, 0) + grad_value,
            tile_start,
            0,
        )
        return ((grad_key_acc, grad_value_acc), (result, grad_query, stats))

    def cross_step(carry, tile_index):
        grad_key_acc, grad_value_acc = carry
        tile_start = tile_index * tile_rows
        query_tile = lax.dynamic_slice_in_dim(cross_query, tile_start, tile_rows, 0)
        grad_tile = lax.dynamic_slice_in_dim(cotangent, tile_start, tile_rows, 0)
        result, grad_query, grad_key, grad_value, stats = attend(
            query_tile, grad_tile, band[0], band[1], band_valid[None, :], heads_here
        )
        return ((grad_key_acc + grad_key, grad_value_acc + grad_value), (result, grad_query))

    zeros_ext = jnp.zeros((block_len + 2 * half_width, columns), jnp.float32)
    zeros_band = jnp.zeros((block_len, columns), jnp.float32)
    tile_ids = jnp.arange(tile_count)
    (self_gk, self_gv), (self_out, self_gq, self_stats) = lax.scan(
        self_step, (zeros_ext, zeros_ext), tile_ids
    )
    (cross_gk, cross_gv), (cross_out, cross_gq) = lax.scan(
        cross_step, (zeros_band, zeros_band), tile_ids
    )
    self_out = self_out.reshape(block_len, columns)
    cross_out = cross_out.reshape(block_len, columns)
    self_stats = jnp.transpose(self_stats, (1, 2, 0, 3)).reshape(3, heads_here, block_len)
    attended = (self_out + cross_out).astype(jnp.bfloat16)
    cross_ext = jnp.zeros((2, block_len + 2 * half_width, columns), jnp.float32)
    cross_ext = lax.dynamic_update_slice_in_dim(
        cross_ext, jnp.stack((cross_gk, cross_gv)), band_start, 1
    )
    self_ext = jnp.stack((self_gk, self_gv))
    self_core = self_ext[:, half_width : half_width + block_len]
    cross_core = cross_ext[:, half_width : half_width + block_len]
    upper_cut = block_len - half_width
    lower_send = jnp.concatenate((self_ext[:, :half_width], cross_ext[:, :half_width]), 0)
    upper_send = jnp.concatenate(
        (self_ext[:, block_len + half_width :], cross_ext[:, block_len + half_width :]), 0
    )
    from_above = passed_along(lower_send.astype(jnp.bfloat16), "blk", -1).astype(lower_send.dtype)
    from_below = passed_along(upper_send.astype(jnp.bfloat16), "blk", 1).astype(upper_send.dtype)
    self_core = (
        self_core.at[:, upper_cut:].add(from_above[:2]).at[:, :half_width].add(from_below[:2])
    )
    cross_core = (
        cross_core.at[:, upper_cut:].add(from_above[2:]).at[:, :half_width].add(from_below[2:])
    )
    returned = swapped(cross_core.astype(jnp.bfloat16), "tower", 0)
    head_outs = (
        attended,
        self_gq.reshape(block_len, columns).astype(jnp.bfloat16),
        self_core[0].astype(jnp.bfloat16),
        self_core[1].astype(jnp.bfloat16),
        cross_gq.reshape(block_len, columns).astype(jnp.bfloat16),
        returned[0],
        returned[1],
    )
    token_outs = (
        lax.all_to_all(head_outs[0], "seq", split_axis=0, concat_axis=1, tiled=True),
        lax.all_to_all(head_outs[1], "seq", split_axis=0, concat_axis=1, tiled=True),
        lax.all_to_all(head_outs[2], "seq", split_axis=0, concat_axis=1, tiled=True),
        lax.all_to_all(head_outs[3], "seq", split_axis=0, concat_axis=1, tiled=True),
        lax.all_to_all(head_outs[4], "seq", split_axis=0, concat_axis=1, tiled=True),
        lax.all_to_all(head_outs[5], "seq", split_axis=0, concat_axis=1, tiled=True),
        lax.all_to_all(head_outs[6], "seq", split_axis=0, concat_axis=1, tiled=True),
    )
    return tuple((piece[None] for piece in token_outs))


def solution(mesh):
    in_specs = (
        P("tower", ("blk", "seq"), None),
        P("tower", ("blk", "seq"), None),
        P("tower", ("blk", "seq"), None),
        P("tower", ("blk", "seq"), None),
        P("tower", ("blk", "seq"), None),
        P("tower", ("blk", "seq"), None),
        P("tower", ("blk", "seq"), None),
        P(),
        P(None, ("blk", "seq")),
    )
    out_specs = (
        P("tower", ("blk", "seq"), None),
        P("tower", ("blk", "seq"), None),
        P("tower", ("blk", "seq"), None),
        P("tower", ("blk", "seq"), None),
        P("tower", ("blk", "seq"), None),
        P("tower", ("blk", "seq"), None),
        P("tower", ("blk", "seq"), None),
    )
    body = paired if mesh.shape["seq"] == 2 else shards
    return jax.shard_map(body, mesh=mesh, in_specs=in_specs, out_specs=out_specs, check_vma=False)
```

```python
import functools

import jax
import jax.numpy as jnp
from jax import lax
from jax.experimental import pallas as pl
from jax.experimental.pallas import tpu as pltpu
from jax.sharding import PartitionSpec as P

HEADS = 16
HEAD = 64
WINDOW = 2048
TILE = 512
LAG = 4
AHEAD = 5
MESH = pl.DeviceIdType.MESH
F32, BF16 = jnp.float32, jnp.bfloat16


def places():
    tower, blk, seq = lax.axis_index("tower"), lax.axis_index("blk"), lax.axis_index("seq")
    toward = 2 * seq - 1
    peers = dict(
        y=(tower, blk, 1 - seq),
        tower=(1 - tower, blk, seq),
        ahead=(tower, blk + toward, seq),
        behind=(tower, blk - toward, seq),
    )
    return tower, blk, seq, peers


def greet(has_ahead, has_behind, peers):
    barrier = pltpu.get_barrier_semaphore()
    for name in ("y", "tower"):
        pl.semaphore_signal(barrier, inc=1, device_id=peers[name], device_id_type=MESH)
    for name, present in (("ahead", has_ahead), ("behind", has_behind)):
        @pl.when(present)
        def _():
            pl.semaphore_signal(barrier, inc=1, device_id=peers[name], device_id_type=MESH)


def meet(has_ahead, has_behind):
    count = 2 + jnp.where(has_ahead, 1, 0) + jnp.where(has_behind, 1, 0)
    pl.semaphore_wait(pltpu.get_barrier_semaphore(), count)


def remote(src, dst, send, recv, device):
    return pltpu.make_async_remote_copy(
        src_ref=src, dst_ref=dst, send_sem=send, recv_sem=recv,
        device_id=device, device_id_type=MESH,
    )


def fused_kernel(
    blks, rows, cols,
    offsets_ref, q_ref, k_ref, v_ref, cq_ref, ck_ref, cv_ref, g_ref, m_ref,
    o_out, gq_out, gk_out, gv_out, gcq_out, gck_out, gcv_out,
    off_ref, side, pair, halo, partner, far, mate, pick, mask_ext, bias,
    exps, dots, sums, stat, peer_stat,
    mine, y_stage, y_recv, core, x_stage, x_recv, own_stage, own_recv,
    part, mate_part, gpick, gfar,
    local_sem, mask_send, mask_recv, in_send, in_recv, halo_send, halo_recv,
    partner_send, partner_recv, far_send, far_recv, share_send, share_recv,
    stat_send, stat_recv, y_send, y_recv_sem, x_send, x_recv_sem, own_send, own_recv_sem,
    swap_send, swap_recv, gfar_send, gfar_recv, gshare_send, gshare_recv,
):
    tower, blk, seq, peers = places()
    half, wide = rows, 2 * HEAD
    groups = cols // wide
    scale = HEAD ** (-0.5)
    has_low, has_high = blk > 0, blk < blks - 1
    has_ahead = ((seq == 1) & has_high) | ((seq == 0) & has_low)
    has_behind = ((seq == 1) & has_low) | ((seq == 0) & has_high)
    outs = [o_out, gq_out, gcq_out]
    grads = [gk_out, gv_out, gck_out, gcv_out]

    def strip(g):
        return pl.ds(pl.multiple_of(g * wide, wide), wide)

    def incoming(g):
        at = strip(g)
        return [
            remote(ref.at[:, at], side.at[i, 1, :, at], in_send.at[g, i], in_recv.at[g, i], peers["y"])
            for i, ref in enumerate((q_ref, cq_ref, g_ref))
        ]

    def haloed(g):
        at = strip(g)
        return [
            remote(
                ref.at[:, at], halo.at[i, :, at], halo_send.at[g, i], halo_recv.at[g, i],
                peers["ahead"],
            )
            for i, ref in enumerate((k_ref, v_ref))
        ]

    def afar(g):
        at = strip(g)
        return remote(
            pick.at[:, at], far.at[tower, :, at], far_send.at[g], far_recv.at[g], peers["ahead"]
        )

    def shared(g):
        at = strip(g)
        return remote(
            far.at[tower, :, at], far.at[tower, :, at], share_send.at[g], share_recv.at[g],
            peers["tower"],
        )

    partners = [
        remote(ref, partner.at[i], partner_send.at[i], partner_recv.at[i], peers["tower"])
        for i, ref in enumerate((ck_ref, cv_ref))
    ]
    mask_ahead = remote(m_ref, mask_ext.at[1], mask_send.at[0], mask_recv.at[0], peers["ahead"])

    def issue(g):
        for copy in incoming(g):
            copy.start()

    def issue_halo(g):
        @pl.when(has_ahead)
        def _():
            for copy in haloed(g):
                copy.start()

    def issue_far(g):
        @pl.when(has_ahead)
        def _():
            afar(g).start()

    greet(has_ahead, has_behind, peers)
    locals_ = [
        pltpu.make_async_copy(offsets_ref, off_ref, local_sem.at[7]),
        pltpu.make_async_copy(k_ref, pair.at[0], local_sem.at[0]),
        pltpu.make_async_copy(v_ref, pair.at[1], local_sem.at[1]),
        pltpu.make_async_copy(m_ref, mask_ext.at[0], local_sem.at[2]),
        pltpu.make_async_copy(q_ref, side.at[0, 0], local_sem.at[3]),
        pltpu.make_async_copy(cq_ref, side.at[1, 0], local_sem.at[4]),
        pltpu.make_async_copy(g_ref, side.at[2, 0], local_sem.at[5]),
    ]
    for copy in locals_:
        copy.start()
    for chain, ref in enumerate((ck_ref, cv_ref)):
        @pl.when(tower == chain)
        def _():
            pltpu.make_async_copy(ref, mate, local_sem.at[6]).start()

    @pl.when(jnp.logical_not(has_behind))
    def _():
        halo[...] = jnp.zeros(halo.shape, BF16)
        far[...] = jnp.zeros(far.shape, BF16)
        mask_ext[1] = jnp.zeros(mask_ext.shape[1:], jnp.int32)

    @pl.when(jnp.logical_not(has_ahead))
    def _():
        x_recv[...] = jnp.zeros(x_recv.shape, BF16)
        gfar[...] = jnp.zeros(gfar.shape, BF16)

    meet(has_ahead, has_behind)
    first = min(AHEAD, groups)
    issue(0)

    @pl.when(has_ahead)
    def _():
        mask_ahead.start()

    for copy in partners:
        copy.start()
    for g in range(1, first):
        issue(g)
    for g in range(min(2, groups)):
        issue_halo(g)
    for copy in locals_:
        copy.wait()
    for chain, ref in enumerate((ck_ref, cv_ref)):
        @pl.when(tower == chain)
        def _():
            pltpu.make_async_copy(ref, mate, local_sem.at[6]).wait()
    off = off_ref[tower, blk]
    off_ahead = off_ref[tower, jnp.clip(blk + 2 * seq - 1, 0, blks - 1)]
    chosen = jnp.where(seq == 1, jnp.where(off_ahead > 0, 1, 0), jnp.where(off_ahead < 0, 1, 0))
    uses_far = jnp.where(seq == 0, jnp.where(off > 0, 1, 0), jnp.where(off < 0, 1, 0))
    far_from = jnp.where(seq == 0, 0, jnp.where(off < 0, half + off, half))
    far_to = jnp.where(seq == 0, jnp.maximum(off, 0), half)

    for copy in partners:
        copy.wait_recv()
    pick[...] = jnp.where(chosen == 1, mate[...], partner[tower])
    for g in range(groups):
        if g >= 2:
            issue_halo(g)
        issue_far(g)

    @pl.when(has_behind)
    def _():
        mask_ahead.wait_recv()

    def column(part_at, chain):
        row = jnp.where(
            chain == 0, mask_ext[part_at, 0:1, :].astype(F32), mask_ext[part_at, 1:2, :].astype(F32)
        )
        return jnp.transpose(jnp.broadcast_to(row, (half, half)))

    row_at = lax.broadcasted_iota(jnp.int32, (half, half), 0)
    col_at = lax.broadcasted_iota(jnp.int32, (half, half), 1)
    apart = (row_at - col_at) * jnp.where(seq == 0, 1, -1)
    from_far = (row_at >= far_from) & (row_at < far_to)
    own_valid, halo_valid = column(0, tower), column(1, tower)
    cross_valid = jnp.where(from_far, column(1, 1 - tower), column(0, 1 - tower))
    allowed = (
        own_valid > 0,
        (own_valid > 0) & (apart >= 0),
        (halo_valid > 0) & (apart <= 0),
        cross_valid > 0,
    )
    for i, near in enumerate(allowed):
        add = jnp.where(near, 0.0, -1e30)
        bias[i, :, :half] = add
        bias[i, :, half:] = add

    lanes = lax.broadcasted_iota(jnp.int32, (half, wide), 1)
    zero = jnp.zeros((half, wide), BF16)

    def split(tile):
        return jnp.concatenate(
            (jnp.where(lanes < HEAD, tile, zero), jnp.where(lanes < HEAD, zero, tile)), 0
        )

    def dot_t(a, b):
        return lax.dot_general(a, b, (((1,), (1,)), ((), ())), preferred_element_type=F32)

    def dot(a, b):
        return jnp.dot(a, b, preferred_element_type=F32)

    def own_heads(both):
        return jnp.concatenate((both[:HEAD, :half], both[HEAD:, half:]), 0)

    def turned(x):
        return jnp.transpose(x.astype(F32)).astype(BF16)

    def operands(g):
        at = strip(g)
        query = [split(side[0, i, :, at] * BF16(scale)) for i in range(2)]
        cross = [split(side[1, i, :, at] * BF16(scale)) for i in range(2)]
        cot = [split(side[2, i, :, at]) for i in range(2)]
        near = [pair[i, :, at] for i in range(2)]
        edge = [halo[i, :, at] for i in range(2)]
        band = [jnp.where(from_far, far[i, :, at], partner[i, :, at]) for i in range(2)]
        return query, cross, cot, near, edge, band

    spans = (slice(0, half), slice(half, 3 * half), slice(3 * half, 4 * half), slice(4 * half, 5 * half))

    def score(g):
        query, cross, cot, near, edge, band = operands(g)
        keys = (near, [jnp.concatenate((n, e), 0) for n, e in zip(near, edge)], band, band)
        asks = (query[0], query[1], cross[0], cross[1])
        adds = (bias[0], jnp.concatenate((bias[1], bias[2]), 0), bias[3], bias[3])
        for kind in range(4):
            key, value = keys[kind]
            scores = dot_t(key, asks[kind]) + adds[kind]
            products = dot_t(value, cot[kind % 2])
            top = jnp.max(scores, axis=0, keepdims=True)
            unnormed = jnp.exp(scores - top)
            total = jnp.sum(unnormed, axis=0, keepdims=True)
            exps[g, spans[kind], :] = unnormed
            dots[g, spans[kind], :] = products
            sums[g, kind : kind + 1, :] = total
            stat[g, 2 * kind : 2 * kind + 1, :] = top + jnp.log(total)
            stat[g, 2 * kind + 1 : 2 * kind + 2, :] = (
                jnp.sum(unnormed * products, axis=0, keepdims=True) / total
            )

    def exchange(g):
        return remote(
            stat.at[g], peer_stat.at[g], stat_send.at[g], stat_recv.at[g], peers["y"]
        )

    def weigh(g, kind):
        other = kind ^ 1
        here, there = stat[g, 2 * kind : 2 * kind + 1, :], peer_stat[g, 2 * other : 2 * other + 1, :]
        top = jnp.maximum(here, there)
        whole = top + jnp.log(jnp.exp(here - top) + jnp.exp(there - top))
        share_here, share_there = jnp.exp(here - whole), jnp.exp(there - whole)
        row_dot = (
            share_here * stat[g, 2 * kind + 1 : 2 * kind + 2, :]
            + share_there * peer_stat[g, 2 * other + 1 : 2 * other + 2, :]
        )
        weights = exps[g, spans[kind], :] * (share_here / sums[g, kind : kind + 1, :])
        grad_scores = weights * (dots[g, spans[kind], :] - row_dot)
        return weights.astype(BF16), grad_scores.astype(BF16)

    def settle(g, swap, relay):
        at = strip(g)
        query, cross, cot, near, edge, band = operands(g)
        band_t = [turned(x) for x in band]
        prob, slope = zip(*[weigh(g, kind) for kind in (2, 3)])
        cross_out = [own_heads(dot(band_t[1], prob[i])) for i in range(2)]
        cross_grad = [own_heads(dot(band_t[0], slope[i])) * scale for i in range(2)]
        band_grad = (
            dot(slope[0], cross[0]) + dot(slope[1], cross[1]),
            dot(prob[0], cot[0]) + dot(prob[1], cot[1]),
        )
        for i in range(2):
            part[i, :, at] = jnp.where(from_far, band_grad[i], 0.0).astype(BF16)
            own_stage[i, :, at] = jnp.where(from_far, 0.0, band_grad[i]).astype(BF16)
        swap()
        near_t = [turned(x) for x in near]
        both_t = [jnp.concatenate((n, turned(e)), 1) for n, e in zip(near_t, edge)]
        prob, slope = zip(*[weigh(g, kind) for kind in (0, 1)])
        self_out = [own_heads(dot(near_t[1], prob[0])), own_heads(dot(both_t[1], prob[1]))]
        self_grad = [own_heads(dot(near_t[0], slope[0])), own_heads(dot(both_t[0], slope[1]))]
        ours = (self_out[0] + cross_out[0], self_grad[0] * scale, cross_grad[0])
        theirs = (self_out[1] + cross_out[1], self_grad[1] * scale, cross_grad[1])
        for i in range(3):
            y_stage[i, :, at] = turned(theirs[i])
            mine[i, :, at] = jnp.transpose(ours[i])
        for i, (left, right, ask) in enumerate(
            ((slope[0], slope[1], query), (prob[0], prob[1], cot))
        ):
            core[i, :, at] = dot(left, ask[0]) + dot(right[:half], ask[1])
            x_stage[i, :, at] = dot(right[half:], ask[1]).astype(BF16)
        relay()

    def outgoing(g):
        at = strip(g)
        return [
            remote(
                y_stage.at[i, :, at], y_recv.at[i, :, at], y_send.at[g, i], y_recv_sem.at[g, i],
                peers["y"],
            )
            for i in range(3)
        ]

    def back(g):
        at = strip(g)
        return [
            remote(
                x_stage.at[i, :, at], x_recv.at[i, :, at], x_send.at[g, i], x_recv_sem.at[g, i],
                peers["behind"],
            )
            for i in range(2)
        ]

    def homeward(g):
        at = strip(g)
        return [
            remote(
                own_stage.at[i, :, at], own_recv.at[i, :, at],
                own_send.at[g, i], own_recv_sem.at[g, i], peers["tower"],
            )
            for i in range(2)
        ]

    def swapped_part(g):
        at = strip(g)
        return remote(
            part.at[1 - tower, :, at], mate_part.at[:, at], swap_send.at[g], swap_recv.at[g],
            peers["tower"],
        )

    def far_back(g):
        at = strip(g)
        return remote(
            gpick.at[:, at], gfar.at[tower, :, at], gfar_send.at[g], gfar_recv.at[g],
            peers["behind"],
        )

    def gshared(g):
        at = strip(g)
        return remote(
            gfar.at[tower, :, at], gfar.at[tower, :, at], gshare_send.at[g], gshare_recv.at[g],
            peers["tower"],
        )

    def share(g):
        @pl.when(has_behind)
        def _():
            afar(g).wait_recv()
            shared(g).start()

    def compute(g):
        def swap():
            swapped_part(g).start()
            for copy in homeward(g):
                copy.start()

        def relay():
            at = strip(g)
            for copy in outgoing(g):
                copy.start()
            swapped_part(g).wait_recv()
            gpick[:, at] = jnp.where(uses_far == 1, part[tower, :, at], mate_part[:, at])

            @pl.when(has_behind)
            def _():
                far_back(g).start()
                for copy in back(g):
                    copy.start()

        settle(g, swap, relay)

    def finish(g):
        at = strip(g)

        @pl.when(has_ahead)
        def _():
            far_back(g).wait_recv()
            gshared(g).start()
            for copy in back(g):
                copy.wait_recv()

        for i in range(2):
            grads[i][:, at] = (core[i, :, at] + x_recv[i, :, at].astype(F32)).astype(BF16)
        for i, copy in enumerate(outgoing(g)):
            copy.wait_recv()
            outs[i][:, at] = (mine[i, :, at] + y_recv[i, :, at].astype(F32)).astype(BF16)

        @pl.when(has_ahead)
        def _():
            gshared(g).wait_recv()

        for i, copy in enumerate(homeward(g)):
            copy.wait_recv()
            more = jnp.where(chosen == 1, gfar[i, :, at].astype(F32), 0.0)
            grads[2 + i][:, at] = (own_recv[i, :, at].astype(F32) + more).astype(BF16)

    def step(g, carry):
        @pl.when(g + AHEAD < groups)
        def _():
            issue(g + AHEAD)

        @pl.when(g < groups)
        def _():
            for copy in incoming(g):
                copy.wait_recv()

            @pl.when(has_behind)
            def _():
                for copy in haloed(g):
                    copy.wait_recv()
                shared(g).wait_recv()

            score(g)
            exchange(g).start()

        @pl.when(g + 1 < groups)
        def _():
            share(g + 1)

        @pl.when(g >= LAG)
        def _():
            exchange(g - LAG).wait_recv()
            compute(g - LAG)

        return carry

    share(0)
    lax.fori_loop(0, groups + LAG, step, 0)

    def end(g, carry):
        finish(g)
        for copy in incoming(g) + outgoing(g) + homeward(g):
            copy.wait_send()
        exchange(g).wait_send()
        swapped_part(g).wait_send()

        @pl.when(has_ahead)
        def _():
            for copy in haloed(g):
                copy.wait_send()
            afar(g).wait_send()
            gshared(g).wait_send()

        @pl.when(has_behind)
        def _():
            shared(g).wait_send()
            far_back(g).wait_send()
            for copy in back(g):
                copy.wait_send()

        return carry

    for copy in partners:
        copy.wait_send()

    @pl.when(has_ahead)
    def _():
        mask_ahead.wait_send()

    lax.fori_loop(0, groups, end, 0)


def copy_kernel(*refs):
    count = len(refs) // 2
    sem = refs[-1]
    copies = [
        pltpu.make_async_copy(src, dst, sem.at[i])
        for i, (src, dst) in enumerate(zip(refs[:count], refs[count:-1]))
    ]
    for copy in copies:
        copy.start()
    for copy in copies:
        copy.wait()


def paired(
    queries, key_rows, value_rows, cross_queries, cross_keys, cross_values, grad_out,
    offsets, key_valid,
):
    blks = lax.axis_size("blk")
    values = [
        value[0] for value in (
            queries, key_rows, value_rows, cross_queries, cross_keys, cross_values, grad_out
        )
    ]
    rows, cols = queries.shape[1:]
    groups, wide = cols // (2 * HEAD), 2 * rows
    dma = pltpu.SemaphoreType.DMA
    full = jax.ShapeDtypeStruct((rows, cols), BF16)
    narrow = pltpu.VMEM((2, rows, cols), BF16)
    single = pltpu.VMEM((rows, cols), BF16)
    scored = pltpu.VMEM((groups, 5 * rows, wide), F32)
    stats = pltpu.VMEM((groups, 8, wide), F32)
    pairs = (dma((groups, 2)),) * 2
    ones = (dma((groups,)),) * 2
    outs = pl.pallas_call(
        functools.partial(fused_kernel, blks, rows, cols),
        out_shape=(pltpu.VMEM((rows, cols), BF16),) * 7,
        in_specs=[pl.BlockSpec(memory_space=pl.ANY)] * 9,
        out_specs=(pl.BlockSpec(memory_space=pltpu.VMEM),) * 7,
        scratch_shapes=[
            pltpu.SMEM(offsets.shape, jnp.int32),
            pltpu.VMEM((3, 2, rows, cols), BF16),
            narrow, narrow, narrow, narrow, single, single,
            pltpu.VMEM((2,) + key_valid.shape, jnp.int32),
            pltpu.VMEM((4, rows, wide), F32),
            scored, scored, stats, stats, stats,
            pltpu.VMEM((3, rows, cols), F32),
            pltpu.VMEM((3, rows, cols), BF16), pltpu.VMEM((3, rows, cols), BF16),
            pltpu.VMEM((2, rows, cols), F32),
            narrow, narrow, narrow, narrow, narrow, single, single, narrow,
            dma((8,)), dma((1,)), dma((1,)),
            dma((groups, 3)), dma((groups, 3)), *pairs,
            dma((2,)), dma((2,)), *ones, *ones,
            *ones, dma((groups, 3)), dma((groups, 3)), *pairs, *pairs,
            *ones, *ones, *ones,
        ],
        compiler_params=pltpu.CompilerParams(collective_id=0, has_side_effects=True),
        name="attend_pairs",
    )(offsets, *values, key_valid)
    outs = pl.pallas_call(
        copy_kernel,
        out_shape=(full,) * 7,
        in_specs=[pl.BlockSpec(memory_space=pl.ANY)] * 7,
        out_specs=(pl.BlockSpec(memory_space=pl.ANY),) * 7,
        scratch_shapes=[dma((7,))],
        compiler_params=pltpu.CompilerParams(vmem_limit_bytes=1 << 20),
        name="hand_over",
    )(*outs)
    return tuple(piece[None] for piece in outs)


def extended(block, sides, width):
    for axis, dim in sides:
        count = lax.axis_size(axis)
        forward = [(i, i + 1) for i in range(count - 1)]
        backward = [(target, source) for source, target in forward]
        low = lax.ppermute(
            lax.slice_in_dim(block, block.shape[dim] - width, None, axis=dim), axis, forward
        )
        high = lax.ppermute(lax.slice_in_dim(block, 0, width, axis=dim), axis, backward)
        block = jnp.concatenate([low, block, high], axis=dim)
    return block


def swapped(value, axis, bit):
    mask = 2**bit
    pairs = [(source, source ^ mask) for source in range(lax.axis_size(axis))]
    return lax.ppermute(value, axis, pairs)


def passed_along(block, axis, distance):
    devices = range(lax.axis_size(axis))
    route = [(i - distance, i) for i in devices if i - distance in devices]
    return lax.ppermute(block, axis, route)


def attend(query_tile, grad_tile, key_block, value_block, allowed, heads_here):
    score_scale = HEAD ** (-0.5)
    rows_count = query_tile.shape[0]
    keys_count = key_block.shape[0]
    q_heads = query_tile.reshape(rows_count, heads_here, HEAD)
    g_heads = grad_tile.reshape(rows_count, heads_here, HEAD)
    k_heads = key_block.reshape(keys_count, heads_here, HEAD)
    v_heads = value_block.reshape(keys_count, heads_here, HEAD)
    scores = (
        jnp.einsum("qhe,khe->hqk", q_heads, k_heads, preferred_element_type=jnp.float32)
        * score_scale
    )
    scores = jnp.where(allowed[None], scores, -1e30)
    row_max = jnp.max(scores, axis=2)
    unnormed = jnp.exp(scores - row_max[:, :, None])
    row_sum = jnp.sum(unnormed, axis=2)
    weights = unnormed / row_sum[:, :, None]
    prob_bf = weights.astype(jnp.bfloat16)
    result = jnp.einsum(
        "hqk,khe->qhe", prob_bf, v_heads, preferred_element_type=jnp.float32
    ).reshape(rows_count, -1)
    grad_probs = jnp.einsum("qhe,khe->hqk", g_heads, v_heads, preferred_element_type=jnp.float32)
    row_dot = jnp.sum(weights * grad_probs, axis=2)
    grad_scores = (weights * (grad_probs - row_dot[:, :, None]) * score_scale).astype(jnp.bfloat16)
    grad_query = jnp.einsum(
        "hqk,khe->qhe", grad_scores, k_heads, preferred_element_type=jnp.float32
    ).reshape(rows_count, -1)
    grad_key = jnp.einsum(
        "hqk,qhe->khe", grad_scores, q_heads, preferred_element_type=jnp.float32
    ).reshape(keys_count, -1)
    grad_value = jnp.einsum(
        "hqk,qhe->khe", prob_bf, g_heads, preferred_element_type=jnp.float32
    ).reshape(keys_count, -1)
    return (result, grad_query, grad_key, grad_value, jnp.stack((row_max, row_sum, row_dot)))


def shards(
    queries,
    key_rows,
    value_rows,
    cross_queries,
    cross_keys,
    cross_values,
    grad_out,
    offsets,
    key_valid,
):
    seq_count = lax.axis_size("seq")
    heads_here = HEADS // seq_count
    local_rows = (
        queries[0],
        key_rows[0],
        value_rows[0],
        cross_queries[0],
        cross_keys[0],
        cross_values[0],
        grad_out[0],
    )
    query_here, key_here, value_here, cross_query, cross_key, cross_value, cotangent = (
        lax.all_to_all(local_rows[0], "seq", split_axis=1, concat_axis=0, tiled=True),
        lax.all_to_all(local_rows[1], "seq", split_axis=1, concat_axis=0, tiled=True),
        lax.all_to_all(local_rows[2], "seq", split_axis=1, concat_axis=0, tiled=True),
        lax.all_to_all(local_rows[3], "seq", split_axis=1, concat_axis=0, tiled=True),
        lax.all_to_all(local_rows[4], "seq", split_axis=1, concat_axis=0, tiled=True),
        lax.all_to_all(local_rows[5], "seq", split_axis=1, concat_axis=0, tiled=True),
        lax.all_to_all(local_rows[6], "seq", split_axis=1, concat_axis=0, tiled=True),
    )
    block_len = query_here.shape[0]
    columns = query_here.shape[1]
    half_width = min(WINDOW // 2, block_len // 2)
    tile_rows = min(TILE, block_len)
    tile_count = block_len // tile_rows
    window_span = tile_rows + 2 * half_width
    tower_id = lax.axis_index("tower")
    block_id = lax.axis_index("blk")
    block_mask = lax.all_gather(key_valid, "seq", axis=1, tiled=True)
    mask_ext = extended(block_mask, (("blk", 1),), half_width)
    self_valid = lax.dynamic_index_in_dim(mask_ext, tower_id, 0, keepdims=False)
    other_valid = lax.dynamic_index_in_dim(mask_ext, 1 - tower_id, 0, keepdims=False)
    pair_ext = extended(jnp.stack((key_here, value_here)), (("blk", 1),), half_width)
    partner = swapped(jnp.stack((cross_key, cross_value)), "tower", 0)
    partner_ext = extended(partner, (("blk", 1),), half_width)
    align_shift = offsets[tower_id, block_id]
    band_start = half_width + align_shift
    band = lax.dynamic_slice_in_dim(partner_ext, band_start, block_len, 1)
    band_valid = lax.dynamic_slice_in_dim(other_valid, band_start, block_len) > 0
    rows_local = jnp.arange(tile_rows)
    keys_local = jnp.arange(window_span)
    near = jnp.abs(rows_local[:, None] + half_width - keys_local[None, :]) <= half_width

    def self_step(carry, tile_index):
        grad_key_acc, grad_value_acc = carry
        tile_start = tile_index * tile_rows
        query_tile = lax.dynamic_slice_in_dim(query_here, tile_start, tile_rows, 0)
        grad_tile = lax.dynamic_slice_in_dim(cotangent, tile_start, tile_rows, 0)
        key_window = lax.dynamic_slice_in_dim(pair_ext[0], tile_start, window_span, 0)
        value_window = lax.dynamic_slice_in_dim(pair_ext[1], tile_start, window_span, 0)
        allowed = (
            near & (lax.dynamic_slice_in_dim(self_valid, tile_start, window_span) > 0)[None, :]
        )
        result, grad_query, grad_key, grad_value, stats = attend(
            query_tile, grad_tile, key_window, value_window, allowed, heads_here
        )
        grad_key_acc = lax.dynamic_update_slice_in_dim(
            grad_key_acc,
            lax.dynamic_slice_in_dim(grad_key_acc, tile_start, window_span, 0) + grad_key,
            tile_start,
            0,
        )
        grad_value_acc = lax.dynamic_update_slice_in_dim(
            grad_value_acc,
            lax.dynamic_slice_in_dim(grad_value_acc, tile_start, window_span, 0) + grad_value,
            tile_start,
            0,
        )
        return ((grad_key_acc, grad_value_acc), (result, grad_query, stats))

    def cross_step(carry, tile_index):
        grad_key_acc, grad_value_acc = carry
        tile_start = tile_index * tile_rows
        query_tile = lax.dynamic_slice_in_dim(cross_query, tile_start, tile_rows, 0)
        grad_tile = lax.dynamic_slice_in_dim(cotangent, tile_start, tile_rows, 0)
        result, grad_query, grad_key, grad_value, stats = attend(
            query_tile, grad_tile, band[0], band[1], band_valid[None, :], heads_here
        )
        return ((grad_key_acc + grad_key, grad_value_acc + grad_value), (result, grad_query))

    zeros_ext = jnp.zeros((block_len + 2 * half_width, columns), jnp.float32)
    zeros_band = jnp.zeros((block_len, columns), jnp.float32)
    tile_ids = jnp.arange(tile_count)
    (self_gk, self_gv), (self_out, self_gq, self_stats) = lax.scan(
        self_step, (zeros_ext, zeros_ext), tile_ids
    )
    (cross_gk, cross_gv), (cross_out, cross_gq) = lax.scan(
        cross_step, (zeros_band, zeros_band), tile_ids
    )
    self_out = self_out.reshape(block_len, columns)
    cross_out = cross_out.reshape(block_len, columns)
    self_stats = jnp.transpose(self_stats, (1, 2, 0, 3)).reshape(3, heads_here, block_len)
    attended = (self_out + cross_out).astype(jnp.bfloat16)
    cross_ext = jnp.zeros((2, block_len + 2 * half_width, columns), jnp.float32)
    cross_ext = lax.dynamic_update_slice_in_dim(
        cross_ext, jnp.stack((cross_gk, cross_gv)), band_start, 1
    )
    self_ext = jnp.stack((self_gk, self_gv))
    self_core = self_ext[:, half_width : half_width + block_len]
    cross_core = cross_ext[:, half_width : half_width + block_len]
    upper_cut = block_len - half_width
    lower_send = jnp.concatenate((self_ext[:, :half_width], cross_ext[:, :half_width]), 0)
    upper_send = jnp.concatenate(
        (self_ext[:, block_len + half_width :], cross_ext[:, block_len + half_width :]), 0
    )
    from_above = passed_along(lower_send.astype(jnp.bfloat16), "blk", -1).astype(lower_send.dtype)
    from_below = passed_along(upper_send.astype(jnp.bfloat16), "blk", 1).astype(upper_send.dtype)
    self_core = (
        self_core.at[:, upper_cut:].add(from_above[:2]).at[:, :half_width].add(from_below[:2])
    )
    cross_core = (
        cross_core.at[:, upper_cut:].add(from_above[2:]).at[:, :half_width].add(from_below[2:])
    )
    returned = swapped(cross_core.astype(jnp.bfloat16), "tower", 0)
    head_outs = (
        attended,
        self_gq.reshape(block_len, columns).astype(jnp.bfloat16),
        self_core[0].astype(jnp.bfloat16),
        self_core[1].astype(jnp.bfloat16),
        cross_gq.reshape(block_len, columns).astype(jnp.bfloat16),
        returned[0],
        returned[1],
    )
    token_outs = (
        lax.all_to_all(head_outs[0], "seq", split_axis=0, concat_axis=1, tiled=True),
        lax.all_to_all(head_outs[1], "seq", split_axis=0, concat_axis=1, tiled=True),
        lax.all_to_all(head_outs[2], "seq", split_axis=0, concat_axis=1, tiled=True),
        lax.all_to_all(head_outs[3], "seq", split_axis=0, concat_axis=1, tiled=True),
        lax.all_to_all(head_outs[4], "seq", split_axis=0, concat_axis=1, tiled=True),
        lax.all_to_all(head_outs[5], "seq", split_axis=0, concat_axis=1, tiled=True),
        lax.all_to_all(head_outs[6], "seq", split_axis=0, concat_axis=1, tiled=True),
    )
    return tuple((piece[None] for piece in token_outs))


def solution(mesh):
    in_specs = (
        P("tower", ("blk", "seq"), None),
        P("tower", ("blk", "seq"), None),
        P("tower", ("blk", "seq"), None),
        P("tower", ("blk", "seq"), None),
        P("tower", ("blk", "seq"), None),
        P("tower", ("blk", "seq"), None),
        P("tower", ("blk", "seq"), None),
        P(),
        P(None, ("blk", "seq")),
    )
    out_specs = (
        P("tower", ("blk", "seq"), None),
        P("tower", ("blk", "seq"), None),
        P("tower", ("blk", "seq"), None),
        P("tower", ("blk", "seq"), None),
        P("tower", ("blk", "seq"), None),
        P("tower", ("blk", "seq"), None),
        P("tower", ("blk", "seq"), None),
    )
    body = paired if mesh.shape["seq"] == 2 else shards
    return jax.shard_map(body, mesh=mesh, in_specs=in_specs, out_specs=out_specs, check_vma=False)
```

```python
import functools

import jax
import jax.numpy as jnp
from jax import lax
from jax.experimental import pallas as pl
from jax.experimental.pallas import tpu as pltpu
from jax.sharding import PartitionSpec as P

HEADS = 16
HEAD = 64
WINDOW = 2048
TILE = 512
LAG = 4
AHEAD = 5
MESH = pl.DeviceIdType.MESH
F32, BF16 = jnp.float32, jnp.bfloat16


def places():
    tower, blk, seq = lax.axis_index("tower"), lax.axis_index("blk"), lax.axis_index("seq")
    toward = 2 * seq - 1
    peers = dict(
        y=(tower, blk, 1 - seq),
        tower=(1 - tower, blk, seq),
        ahead=(tower, blk + toward, seq),
        behind=(tower, blk - toward, seq),
    )
    return tower, blk, seq, peers


def greet(has_ahead, has_behind, peers):
    barrier = pltpu.get_barrier_semaphore()
    for name in ("y", "tower"):
        pl.semaphore_signal(barrier, inc=1, device_id=peers[name], device_id_type=MESH)
    for name, present in (("ahead", has_ahead), ("behind", has_behind)):
        @pl.when(present)
        def _():
            pl.semaphore_signal(barrier, inc=1, device_id=peers[name], device_id_type=MESH)


def meet(has_ahead, has_behind):
    count = 2 + jnp.where(has_ahead, 1, 0) + jnp.where(has_behind, 1, 0)
    pl.semaphore_wait(pltpu.get_barrier_semaphore(), count)


def remote(src, dst, send, recv, device):
    return pltpu.make_async_remote_copy(
        src_ref=src, dst_ref=dst, send_sem=send, recv_sem=recv,
        device_id=device, device_id_type=MESH,
    )


def fused_kernel(
    blks, rows, cols,
    offsets_ref, q_ref, k_ref, v_ref, cq_ref, ck_ref, cv_ref, g_ref, m_ref,
    o_out, gq_out, gk_out, gv_out, gcq_out, gck_out, gcv_out,
    off_ref, side, pair, halo, partner, far, mate, pick, mask_ext, bias,
    exps, dots, sums, stat, flat, packed, peer_packed,
    mine, y_stage, y_recv, core, x_stage, x_recv, own_stage, own_recv,
    part, mate_part, gpick, gfar,
    local_sem, mask_send, mask_recv, in_send, in_recv, halo_send, halo_recv,
    partner_send, partner_recv, far_send, far_recv, share_send, share_recv,
    stat_send, stat_recv, y_send, y_recv_sem, x_send, x_recv_sem, own_send, own_recv_sem,
    swap_send, swap_recv, gfar_send, gfar_recv, gshare_send, gshare_recv,
):
    tower, blk, seq, peers = places()
    half, wide = rows, 2 * HEAD
    groups = cols // wide
    scale = HEAD ** (-0.5)
    has_low, has_high = blk > 0, blk < blks - 1
    has_ahead = ((seq == 1) & has_high) | ((seq == 0) & has_low)
    has_behind = ((seq == 1) & has_low) | ((seq == 0) & has_high)
    outs = [o_out, gq_out, gcq_out]
    grads = [gk_out, gv_out, gck_out, gcv_out]

    def strip(g):
        return pl.ds(pl.multiple_of(g * wide, wide), wide)

    def incoming(g):
        at = strip(g)
        return [
            remote(ref.at[:, at], side.at[i, 1, :, at], in_send.at[g, i], in_recv.at[g, i], peers["y"])
            for i, ref in enumerate((q_ref, cq_ref, g_ref))
        ]

    def haloed(g):
        at = strip(g)
        return [
            remote(
                ref.at[:, at], halo.at[i, :, at], halo_send.at[g, i], halo_recv.at[g, i],
                peers["ahead"],
            )
            for i, ref in enumerate((k_ref, v_ref))
        ]

    def afar(g):
        at = strip(g)
        return remote(
            pick.at[:, at], far.at[tower, :, at], far_send.at[g], far_recv.at[g], peers["ahead"]
        )

    def shared(g):
        at = strip(g)
        return remote(
            far.at[tower, :, at], far.at[tower, :, at], share_send.at[g], share_recv.at[g],
            peers["tower"],
        )

    partners = [
        remote(ref, partner.at[i], partner_send.at[i], partner_recv.at[i], peers["tower"])
        for i, ref in enumerate((ck_ref, cv_ref))
    ]
    mask_ahead = remote(m_ref, mask_ext.at[1], mask_send.at[0], mask_recv.at[0], peers["ahead"])

    def issue(g):
        for copy in incoming(g):
            copy.start()

    def issue_halo(g):
        @pl.when(has_ahead)
        def _():
            for copy in haloed(g):
                copy.start()

    def issue_far(g):
        @pl.when(has_ahead)
        def _():
            afar(g).start()

    greet(has_ahead, has_behind, peers)
    locals_ = [
        pltpu.make_async_copy(offsets_ref, off_ref, local_sem.at[7]),
        pltpu.make_async_copy(k_ref, pair.at[0], local_sem.at[0]),
        pltpu.make_async_copy(v_ref, pair.at[1], local_sem.at[1]),
        pltpu.make_async_copy(m_ref, mask_ext.at[0], local_sem.at[2]),
        pltpu.make_async_copy(q_ref, side.at[0, 0], local_sem.at[3]),
        pltpu.make_async_copy(cq_ref, side.at[1, 0], local_sem.at[4]),
        pltpu.make_async_copy(g_ref, side.at[2, 0], local_sem.at[5]),
    ]
    for copy in locals_:
        copy.start()
    for chain, ref in enumerate((ck_ref, cv_ref)):
        @pl.when(tower == chain)
        def _():
            pltpu.make_async_copy(ref, mate, local_sem.at[6]).start()

    @pl.when(jnp.logical_not(has_behind))
    def _():
        halo[...] = jnp.zeros(halo.shape, BF16)
        far[...] = jnp.zeros(far.shape, BF16)
        mask_ext[1] = jnp.zeros(mask_ext.shape[1:], jnp.int32)

    @pl.when(jnp.logical_not(has_ahead))
    def _():
        x_recv[...] = jnp.zeros(x_recv.shape, BF16)
        gfar[...] = jnp.zeros(gfar.shape, BF16)

    meet(has_ahead, has_behind)
    first = min(AHEAD, groups)
    issue(0)

    @pl.when(has_ahead)
    def _():
        mask_ahead.start()

    for copy in partners:
        copy.start()
    for g in range(1, first):
        issue(g)
    for g in range(min(2, groups)):
        issue_halo(g)
    for copy in locals_:
        copy.wait()
    for chain, ref in enumerate((ck_ref, cv_ref)):
        @pl.when(tower == chain)
        def _():
            pltpu.make_async_copy(ref, mate, local_sem.at[6]).wait()
    off = off_ref[tower, blk]
    off_ahead = off_ref[tower, jnp.clip(blk + 2 * seq - 1, 0, blks - 1)]
    chosen = jnp.where(seq == 1, jnp.where(off_ahead > 0, 1, 0), jnp.where(off_ahead < 0, 1, 0))
    uses_far = jnp.where(seq == 0, jnp.where(off > 0, 1, 0), jnp.where(off < 0, 1, 0))
    far_from = jnp.where(seq == 0, 0, jnp.where(off < 0, half + off, half))
    far_to = jnp.where(seq == 0, jnp.maximum(off, 0), half)

    for copy in partners:
        copy.wait_recv()
    pick[...] = jnp.where(chosen == 1, mate[...], partner[tower])
    for g in range(groups):
        if g >= 2:
            issue_halo(g)
        issue_far(g)

    @pl.when(has_behind)
    def _():
        mask_ahead.wait_recv()

    def column(part_at, chain):
        row = jnp.where(
            chain == 0, mask_ext[part_at, 0:1, :].astype(F32), mask_ext[part_at, 1:2, :].astype(F32)
        )
        return jnp.transpose(jnp.broadcast_to(row, (half, half)))

    row_at = lax.broadcasted_iota(jnp.int32, (half, half), 0)
    col_at = lax.broadcasted_iota(jnp.int32, (half, half), 1)
    apart = (row_at - col_at) * jnp.where(seq == 0, 1, -1)
    from_far = (row_at >= far_from) & (row_at < far_to)
    own_valid, halo_valid = column(0, tower), column(1, tower)
    cross_valid = jnp.where(from_far, column(1, 1 - tower), column(0, 1 - tower))
    allowed = (
        own_valid > 0,
        (own_valid > 0) & (apart >= 0),
        (halo_valid > 0) & (apart <= 0),
        cross_valid > 0,
    )
    for i, near in enumerate(allowed):
        add = jnp.where(near, 0.0, -1e30)
        bias[i, :, :half] = add
        bias[i, :, half:] = add

    lanes = lax.broadcasted_iota(jnp.int32, (half, wide), 1)
    zero = jnp.zeros((half, wide), BF16)

    def split(tile):
        return jnp.concatenate(
            (jnp.where(lanes < HEAD, tile, zero), jnp.where(lanes < HEAD, zero, tile)), 0
        )

    def dot_t(a, b):
        return lax.dot_general(a, b, (((1,), (1,)), ((), ())), preferred_element_type=F32)

    def dot(a, b):
        return jnp.dot(a, b, preferred_element_type=F32)

    def own_heads(both):
        return jnp.concatenate((both[:HEAD, :half], both[HEAD:, half:]), 0)

    def turned(x):
        return jnp.transpose(x.astype(F32)).astype(BF16)

    def operands(g):
        at = strip(g)
        query = [split(side[0, i, :, at] * BF16(scale)) for i in range(2)]
        cross = [split(side[1, i, :, at] * BF16(scale)) for i in range(2)]
        cot = [split(side[2, i, :, at]) for i in range(2)]
        near = [pair[i, :, at] for i in range(2)]
        edge = [halo[i, :, at] for i in range(2)]
        band = [jnp.where(from_far, far[i, :, at], partner[i, :, at]) for i in range(2)]
        return query, cross, cot, near, edge, band

    spans = (slice(0, half), slice(half, 3 * half), slice(3 * half, 4 * half), slice(4 * half, 5 * half))

    def score(g):
        query, cross, cot, near, edge, band = operands(g)
        keys = (near, [jnp.concatenate((n, e), 0) for n, e in zip(near, edge)], band, band)
        asks = (query[0], query[1], cross[0], cross[1])
        adds = (bias[0], jnp.concatenate((bias[1], bias[2]), 0), bias[3], bias[3])
        for kind in range(4):
            key, value = keys[kind]
            scores = dot_t(key, asks[kind]) + adds[kind]
            products = dot_t(value, cot[kind % 2])
            top = jnp.max(scores, axis=0, keepdims=True)
            unnormed = jnp.exp(scores - top)
            total = jnp.sum(unnormed, axis=0, keepdims=True)
            exps[g, spans[kind], :] = unnormed
            dots[g, spans[kind], :] = products
            sums[g, kind : kind + 1, :] = total
            merged = top + jnp.log(total)
            row_dot = jnp.sum(unnormed * products, axis=0, keepdims=True) / total
            stat[g, 2 * kind : 2 * kind + 1, :] = merged
            stat[g, 2 * kind + 1 : 2 * kind + 2, :] = row_dot
            for head in range(2):
                lane = slice(head * half, (head + 1) * half)
                at = 2 * kind + head
                flat[0, at : at + 1, :] = merged[:, lane]
                flat[1, at : at + 1, :] = row_dot[:, lane]
        high = flat[0].astype(BF16)
        low = (flat[0] - high.astype(F32)).astype(BF16)
        packed[g] = jnp.concatenate((high, low, flat[1].astype(BF16)), 1)

    def exchange(g):
        return remote(
            packed.at[g], peer_packed.at[g], stat_send.at[g], stat_recv.at[g], peers["y"]
        )

    def weigh(g, kind):
        peer = peer_packed[g].astype(F32)
        at = 2 * (kind ^ 1)

        def joined(rows_of):
            return jnp.concatenate((rows_of[at : at + 1], rows_of[at + 1 : at + 2]), 1)

        here, there = (
            stat[g, 2 * kind : 2 * kind + 1, :],
            joined(peer[:, :half] + peer[:, half : 2 * half]),
        )
        top = jnp.maximum(here, there)
        whole = top + jnp.log(jnp.exp(here - top) + jnp.exp(there - top))
        share_here, share_there = jnp.exp(here - whole), jnp.exp(there - whole)
        row_dot = (
            share_here * stat[g, 2 * kind + 1 : 2 * kind + 2, :]
            + share_there * joined(peer[:, 2 * half :])
        )
        weights = exps[g, spans[kind], :] * (share_here / sums[g, kind : kind + 1, :])
        grad_scores = weights * (dots[g, spans[kind], :] - row_dot)
        return weights.astype(BF16), grad_scores.astype(BF16)

    def settle(g, swap, relay):
        at = strip(g)
        query, cross, cot, near, edge, band = operands(g)
        band_t = [turned(x) for x in band]
        prob, slope = zip(*[weigh(g, kind) for kind in (2, 3)])
        cross_out = [own_heads(dot(band_t[1], prob[i])) for i in range(2)]
        cross_grad = [own_heads(dot(band_t[0], slope[i])) * scale for i in range(2)]
        band_grad = (
            dot(slope[0], cross[0]) + dot(slope[1], cross[1]),
            dot(prob[0], cot[0]) + dot(prob[1], cot[1]),
        )
        for i in range(2):
            part[i, :, at] = jnp.where(from_far, band_grad[i], 0.0).astype(BF16)
            own_stage[i, :, at] = jnp.where(from_far, 0.0, band_grad[i]).astype(BF16)
        swap()
        near_t = [turned(x) for x in near]
        both_t = [jnp.concatenate((n, turned(e)), 1) for n, e in zip(near_t, edge)]
        prob, slope = zip(*[weigh(g, kind) for kind in (0, 1)])
        self_out = [own_heads(dot(near_t[1], prob[0])), own_heads(dot(both_t[1], prob[1]))]
        self_grad = [own_heads(dot(near_t[0], slope[0])), own_heads(dot(both_t[0], slope[1]))]
        ours = (self_out[0] + cross_out[0], self_grad[0] * scale, cross_grad[0])
        theirs = (self_out[1] + cross_out[1], self_grad[1] * scale, cross_grad[1])
        for i in range(3):
            y_stage[i, :, at] = turned(theirs[i])
            mine[i, :, at] = jnp.transpose(ours[i])
        for i, (left, right, ask) in enumerate(
            ((slope[0], slope[1], query), (prob[0], prob[1], cot))
        ):
            core[i, :, at] = dot(left, ask[0]) + dot(right[:half], ask[1])
            x_stage[i, :, at] = dot(right[half:], ask[1]).astype(BF16)
        relay()

    def outgoing(g):
        at = strip(g)
        return [
            remote(
                y_stage.at[i, :, at], y_recv.at[i, :, at], y_send.at[g, i], y_recv_sem.at[g, i],
                peers["y"],
            )
            for i in range(3)
        ]

    def back(g):
        at = strip(g)
        return [
            remote(
                x_stage.at[i, :, at], x_recv.at[i, :, at], x_send.at[g, i], x_recv_sem.at[g, i],
                peers["behind"],
            )
            for i in range(2)
        ]

    def homeward(g):
        at = strip(g)
        return [
            remote(
                own_stage.at[i, :, at], own_recv.at[i, :, at],
                own_send.at[g, i], own_recv_sem.at[g, i], peers["tower"],
            )
            for i in range(2)
        ]

    def swapped_part(g):
        at = strip(g)
        return remote(
            part.at[1 - tower, :, at], mate_part.at[:, at], swap_send.at[g], swap_recv.at[g],
            peers["tower"],
        )

    def far_back(g):
        at = strip(g)
        return remote(
            gpick.at[:, at], gfar.at[tower, :, at], gfar_send.at[g], gfar_recv.at[g],
            peers["behind"],
        )

    def gshared(g):
        at = strip(g)
        return remote(
            gfar.at[tower, :, at], gfar.at[tower, :, at], gshare_send.at[g], gshare_recv.at[g],
            peers["tower"],
        )

    def share(g):
        @pl.when(has_behind)
        def _():
            afar(g).wait_recv()
            shared(g).start()

    def compute(g):
        def swap():
            swapped_part(g).start()
            for copy in homeward(g):
                copy.start()

        def relay():
            at = strip(g)
            for copy in outgoing(g):
                copy.start()
            swapped_part(g).wait_recv()
            gpick[:, at] = jnp.where(uses_far == 1, part[tower, :, at], mate_part[:, at])

            @pl.when(has_behind)
            def _():
                far_back(g).start()
                for copy in back(g):
                    copy.start()

        settle(g, swap, relay)

    def finish(g):
        at = strip(g)

        @pl.when(has_ahead)
        def _():
            far_back(g).wait_recv()
            gshared(g).start()
            for copy in back(g):
                copy.wait_recv()

        for i in range(2):
            grads[i][:, at] = (core[i, :, at] + x_recv[i, :, at].astype(F32)).astype(BF16)
        for i, copy in enumerate(outgoing(g)):
            copy.wait_recv()
            outs[i][:, at] = (mine[i, :, at] + y_recv[i, :, at].astype(F32)).astype(BF16)

        @pl.when(has_ahead)
        def _():
            gshared(g).wait_recv()

        for i, copy in enumerate(homeward(g)):
            copy.wait_recv()
            more = jnp.where(chosen == 1, gfar[i, :, at].astype(F32), 0.0)
            grads[2 + i][:, at] = (own_recv[i, :, at].astype(F32) + more).astype(BF16)

    def step(g, carry):
        @pl.when(g + AHEAD < groups)
        def _():
            issue(g + AHEAD)

        @pl.when(g < groups)
        def _():
            for copy in incoming(g):
                copy.wait_recv()

            @pl.when(has_behind)
            def _():
                for copy in haloed(g):
                    copy.wait_recv()
                shared(g).wait_recv()

            score(g)
            exchange(g).start()

        @pl.when(g + 1 < groups)
        def _():
            share(g + 1)

        @pl.when(g >= LAG)
        def _():
            exchange(g - LAG).wait_recv()
            compute(g - LAG)

        return carry

    share(0)
    lax.fori_loop(0, groups + LAG, step, 0)

    def end(g, carry):
        finish(g)
        for copy in incoming(g) + outgoing(g) + homeward(g):
            copy.wait_send()
        exchange(g).wait_send()
        swapped_part(g).wait_send()

        @pl.when(has_ahead)
        def _():
            for copy in haloed(g):
                copy.wait_send()
            afar(g).wait_send()
            gshared(g).wait_send()

        @pl.when(has_behind)
        def _():
            shared(g).wait_send()
            far_back(g).wait_send()
            for copy in back(g):
                copy.wait_send()

        return carry

    for copy in partners:
        copy.wait_send()

    @pl.when(has_ahead)
    def _():
        mask_ahead.wait_send()

    lax.fori_loop(0, groups, end, 0)


def copy_kernel(*refs):
    count = len(refs) // 2
    sem = refs[-1]
    copies = [
        pltpu.make_async_copy(src, dst, sem.at[i])
        for i, (src, dst) in enumerate(zip(refs[:count], refs[count:-1]))
    ]
    for copy in copies:
        copy.start()
    for copy in copies:
        copy.wait()


def paired(
    queries, key_rows, value_rows, cross_queries, cross_keys, cross_values, grad_out,
    offsets, key_valid,
):
    blks = lax.axis_size("blk")
    values = [
        value[0] for value in (
            queries, key_rows, value_rows, cross_queries, cross_keys, cross_values, grad_out
        )
    ]
    rows, cols = queries.shape[1:]
    groups, wide = cols // (2 * HEAD), 2 * rows
    dma = pltpu.SemaphoreType.DMA
    full = jax.ShapeDtypeStruct((rows, cols), BF16)
    narrow = pltpu.VMEM((2, rows, cols), BF16)
    single = pltpu.VMEM((rows, cols), BF16)
    scored = pltpu.VMEM((groups, 5 * rows, wide), F32)
    stats = pltpu.VMEM((groups, 8, wide), F32)
    bits = pltpu.VMEM((groups, 8, 3 * rows), BF16)
    pairs = (dma((groups, 2)),) * 2
    ones = (dma((groups,)),) * 2
    outs = pl.pallas_call(
        functools.partial(fused_kernel, blks, rows, cols),
        out_shape=(pltpu.VMEM((rows, cols), BF16),) * 7,
        in_specs=[pl.BlockSpec(memory_space=pl.ANY)] * 9,
        out_specs=(pl.BlockSpec(memory_space=pltpu.VMEM),) * 7,
        scratch_shapes=[
            pltpu.SMEM(offsets.shape, jnp.int32),
            pltpu.VMEM((3, 2, rows, cols), BF16),
            narrow, narrow, narrow, narrow, single, single,
            pltpu.VMEM((2,) + key_valid.shape, jnp.int32),
            pltpu.VMEM((4, rows, wide), F32),
            scored, scored, stats, stats,
            pltpu.VMEM((2, 8, rows), F32), bits, bits,
            pltpu.VMEM((3, rows, cols), F32),
            pltpu.VMEM((3, rows, cols), BF16), pltpu.VMEM((3, rows, cols), BF16),
            pltpu.VMEM((2, rows, cols), F32),
            narrow, narrow, narrow, narrow, narrow, single, single, narrow,
            dma((8,)), dma((1,)), dma((1,)),
            dma((groups, 3)), dma((groups, 3)), *pairs,
            dma((2,)), dma((2,)), *ones, *ones,
            *ones, dma((groups, 3)), dma((groups, 3)), *pairs, *pairs,
            *ones, *ones, *ones,
        ],
        compiler_params=pltpu.CompilerParams(collective_id=0, has_side_effects=True),
        name="attend_pairs",
    )(offsets, *values, key_valid)
    outs = pl.pallas_call(
        copy_kernel,
        out_shape=(full,) * 7,
        in_specs=[pl.BlockSpec(memory_space=pl.ANY)] * 7,
        out_specs=(pl.BlockSpec(memory_space=pl.ANY),) * 7,
        scratch_shapes=[dma((7,))],
        compiler_params=pltpu.CompilerParams(vmem_limit_bytes=1 << 20),
        name="hand_over",
    )(*outs)
    return tuple(piece[None] for piece in outs)


def extended(block, sides, width):
    for axis, dim in sides:
        count = lax.axis_size(axis)
        forward = [(i, i + 1) for i in range(count - 1)]
        backward = [(target, source) for source, target in forward]
        low = lax.ppermute(
            lax.slice_in_dim(block, block.shape[dim] - width, None, axis=dim), axis, forward
        )
        high = lax.ppermute(lax.slice_in_dim(block, 0, width, axis=dim), axis, backward)
        block = jnp.concatenate([low, block, high], axis=dim)
    return block


def swapped(value, axis, bit):
    mask = 2**bit
    pairs = [(source, source ^ mask) for source in range(lax.axis_size(axis))]
    return lax.ppermute(value, axis, pairs)


def passed_along(block, axis, distance):
    devices = range(lax.axis_size(axis))
    route = [(i - distance, i) for i in devices if i - distance in devices]
    return lax.ppermute(block, axis, route)


def attend(query_tile, grad_tile, key_block, value_block, allowed, heads_here):
    score_scale = HEAD ** (-0.5)
    rows_count = query_tile.shape[0]
    keys_count = key_block.shape[0]
    q_heads = query_tile.reshape(rows_count, heads_here, HEAD)
    g_heads = grad_tile.reshape(rows_count, heads_here, HEAD)
    k_heads = key_block.reshape(keys_count, heads_here, HEAD)
    v_heads = value_block.reshape(keys_count, heads_here, HEAD)
    scores = (
        jnp.einsum("qhe,khe->hqk", q_heads, k_heads, preferred_element_type=jnp.float32)
        * score_scale
    )
    scores = jnp.where(allowed[None], scores, -1e30)
    row_max = jnp.max(scores, axis=2)
    unnormed = jnp.exp(scores - row_max[:, :, None])
    row_sum = jnp.sum(unnormed, axis=2)
    weights = unnormed / row_sum[:, :, None]
    prob_bf = weights.astype(jnp.bfloat16)
    result = jnp.einsum(
        "hqk,khe->qhe", prob_bf, v_heads, preferred_element_type=jnp.float32
    ).reshape(rows_count, -1)
    grad_probs = jnp.einsum("qhe,khe->hqk", g_heads, v_heads, preferred_element_type=jnp.float32)
    row_dot = jnp.sum(weights * grad_probs, axis=2)
    grad_scores = (weights * (grad_probs - row_dot[:, :, None]) * score_scale).astype(jnp.bfloat16)
    grad_query = jnp.einsum(
        "hqk,khe->qhe", grad_scores, k_heads, preferred_element_type=jnp.float32
    ).reshape(rows_count, -1)
    grad_key = jnp.einsum(
        "hqk,qhe->khe", grad_scores, q_heads, preferred_element_type=jnp.float32
    ).reshape(keys_count, -1)
    grad_value = jnp.einsum(
        "hqk,qhe->khe", prob_bf, g_heads, preferred_element_type=jnp.float32
    ).reshape(keys_count, -1)
    return (result, grad_query, grad_key, grad_value, jnp.stack((row_max, row_sum, row_dot)))


def shards(
    queries,
    key_rows,
    value_rows,
    cross_queries,
    cross_keys,
    cross_values,
    grad_out,
    offsets,
    key_valid,
):
    seq_count = lax.axis_size("seq")
    heads_here = HEADS // seq_count
    local_rows = (
        queries[0],
        key_rows[0],
        value_rows[0],
        cross_queries[0],
        cross_keys[0],
        cross_values[0],
        grad_out[0],
    )
    query_here, key_here, value_here, cross_query, cross_key, cross_value, cotangent = (
        lax.all_to_all(local_rows[0], "seq", split_axis=1, concat_axis=0, tiled=True),
        lax.all_to_all(local_rows[1], "seq", split_axis=1, concat_axis=0, tiled=True),
        lax.all_to_all(local_rows[2], "seq", split_axis=1, concat_axis=0, tiled=True),
        lax.all_to_all(local_rows[3], "seq", split_axis=1, concat_axis=0, tiled=True),
        lax.all_to_all(local_rows[4], "seq", split_axis=1, concat_axis=0, tiled=True),
        lax.all_to_all(local_rows[5], "seq", split_axis=1, concat_axis=0, tiled=True),
        lax.all_to_all(local_rows[6], "seq", split_axis=1, concat_axis=0, tiled=True),
    )
    block_len = query_here.shape[0]
    columns = query_here.shape[1]
    half_width = min(WINDOW // 2, block_len // 2)
    tile_rows = min(TILE, block_len)
    tile_count = block_len // tile_rows
    window_span = tile_rows + 2 * half_width
    tower_id = lax.axis_index("tower")
    block_id = lax.axis_index("blk")
    block_mask = lax.all_gather(key_valid, "seq", axis=1, tiled=True)
    mask_ext = extended(block_mask, (("blk", 1),), half_width)
    self_valid = lax.dynamic_index_in_dim(mask_ext, tower_id, 0, keepdims=False)
    other_valid = lax.dynamic_index_in_dim(mask_ext, 1 - tower_id, 0, keepdims=False)
    pair_ext = extended(jnp.stack((key_here, value_here)), (("blk", 1),), half_width)
    partner = swapped(jnp.stack((cross_key, cross_value)), "tower", 0)
    partner_ext = extended(partner, (("blk", 1),), half_width)
    align_shift = offsets[tower_id, block_id]
    band_start = half_width + align_shift
    band = lax.dynamic_slice_in_dim(partner_ext, band_start, block_len, 1)
    band_valid = lax.dynamic_slice_in_dim(other_valid, band_start, block_len) > 0
    rows_local = jnp.arange(tile_rows)
    keys_local = jnp.arange(window_span)
    near = jnp.abs(rows_local[:, None] + half_width - keys_local[None, :]) <= half_width

    def self_step(carry, tile_index):
        grad_key_acc, grad_value_acc = carry
        tile_start = tile_index * tile_rows
        query_tile = lax.dynamic_slice_in_dim(query_here, tile_start, tile_rows, 0)
        grad_tile = lax.dynamic_slice_in_dim(cotangent, tile_start, tile_rows, 0)
        key_window = lax.dynamic_slice_in_dim(pair_ext[0], tile_start, window_span, 0)
        value_window = lax.dynamic_slice_in_dim(pair_ext[1], tile_start, window_span, 0)
        allowed = (
            near & (lax.dynamic_slice_in_dim(self_valid, tile_start, window_span) > 0)[None, :]
        )
        result, grad_query, grad_key, grad_value, stats = attend(
            query_tile, grad_tile, key_window, value_window, allowed, heads_here
        )
        grad_key_acc = lax.dynamic_update_slice_in_dim(
            grad_key_acc,
            lax.dynamic_slice_in_dim(grad_key_acc, tile_start, window_span, 0) + grad_key,
            tile_start,
            0,
        )
        grad_value_acc = lax.dynamic_update_slice_in_dim(
            grad_value_acc,
            lax.dynamic_slice_in_dim(grad_value_acc, tile_start, window_span, 0) + grad_value,
            tile_start,
            0,
        )
        return ((grad_key_acc, grad_value_acc), (result, grad_query, stats))

    def cross_step(carry, tile_index):
        grad_key_acc, grad_value_acc = carry
        tile_start = tile_index * tile_rows
        query_tile = lax.dynamic_slice_in_dim(cross_query, tile_start, tile_rows, 0)
        grad_tile = lax.dynamic_slice_in_dim(cotangent, tile_start, tile_rows, 0)
        result, grad_query, grad_key, grad_value, stats = attend(
            query_tile, grad_tile, band[0], band[1], band_valid[None, :], heads_here
        )
        return ((grad_key_acc + grad_key, grad_value_acc + grad_value), (result, grad_query))

    zeros_ext = jnp.zeros((block_len + 2 * half_width, columns), jnp.float32)
    zeros_band = jnp.zeros((block_len, columns), jnp.float32)
    tile_ids = jnp.arange(tile_count)
    (self_gk, self_gv), (self_out, self_gq, self_stats) = lax.scan(
        self_step, (zeros_ext, zeros_ext), tile_ids
    )
    (cross_gk, cross_gv), (cross_out, cross_gq) = lax.scan(
        cross_step, (zeros_band, zeros_band), tile_ids
    )
    self_out = self_out.reshape(block_len, columns)
    cross_out = cross_out.reshape(block_len, columns)
    self_stats = jnp.transpose(self_stats, (1, 2, 0, 3)).reshape(3, heads_here, block_len)
    attended = (self_out + cross_out).astype(jnp.bfloat16)
    cross_ext = jnp.zeros((2, block_len + 2 * half_width, columns), jnp.float32)
    cross_ext = lax.dynamic_update_slice_in_dim(
        cross_ext, jnp.stack((cross_gk, cross_gv)), band_start, 1
    )
    self_ext = jnp.stack((self_gk, self_gv))
    self_core = self_ext[:, half_width : half_width + block_len]
    cross_core = cross_ext[:, half_width : half_width + block_len]
    upper_cut = block_len - half_width
    lower_send = jnp.concatenate((self_ext[:, :half_width], cross_ext[:, :half_width]), 0)
    upper_send = jnp.concatenate(
        (self_ext[:, block_len + half_width :], cross_ext[:, block_len + half_width :]), 0
    )
    from_above = passed_along(lower_send.astype(jnp.bfloat16), "blk", -1).astype(lower_send.dtype)
    from_below = passed_along(upper_send.astype(jnp.bfloat16), "blk", 1).astype(upper_send.dtype)
    self_core = (
        self_core.at[:, upper_cut:].add(from_above[:2]).at[:, :half_width].add(from_below[:2])
    )
    cross_core = (
        cross_core.at[:, upper_cut:].add(from_above[2:]).at[:, :half_width].add(from_below[2:])
    )
    returned = swapped(cross_core.astype(jnp.bfloat16), "tower", 0)
    head_outs = (
        attended,
        self_gq.reshape(block_len, columns).astype(jnp.bfloat16),
        self_core[0].astype(jnp.bfloat16),
        self_core[1].astype(jnp.bfloat16),
        cross_gq.reshape(block_len, columns).astype(jnp.bfloat16),
        returned[0],
        returned[1],
    )
    token_outs = (
        lax.all_to_all(head_outs[0], "seq", split_axis=0, concat_axis=1, tiled=True),
        lax.all_to_all(head_outs[1], "seq", split_axis=0, concat_axis=1, tiled=True),
        lax.all_to_all(head_outs[2], "seq", split_axis=0, concat_axis=1, tiled=True),
        lax.all_to_all(head_outs[3], "seq", split_axis=0, concat_axis=1, tiled=True),
        lax.all_to_all(head_outs[4], "seq", split_axis=0, concat_axis=1, tiled=True),
        lax.all_to_all(head_outs[5], "seq", split_axis=0, concat_axis=1, tiled=True),
        lax.all_to_all(head_outs[6], "seq", split_axis=0, concat_axis=1, tiled=True),
    )
    return tuple((piece[None] for piece in token_outs))


def solution(mesh):
    in_specs = (
        P("tower", ("blk", "seq"), None),
        P("tower", ("blk", "seq"), None),
        P("tower", ("blk", "seq"), None),
        P("tower", ("blk", "seq"), None),
        P("tower", ("blk", "seq"), None),
        P("tower", ("blk", "seq"), None),
        P("tower", ("blk", "seq"), None),
        P(),
        P(None, ("blk", "seq")),
    )
    out_specs = (
        P("tower", ("blk", "seq"), None),
        P("tower", ("blk", "seq"), None),
        P("tower", ("blk", "seq"), None),
        P("tower", ("blk", "seq"), None),
        P("tower", ("blk", "seq"), None),
        P("tower", ("blk", "seq"), None),
        P("tower", ("blk", "seq"), None),
    )
    body = paired if mesh.shape["seq"] == 2 else shards
    return jax.shard_map(body, mesh=mesh, in_specs=in_specs, out_specs=out_specs, check_vma=False)
```

```python
import functools

import jax
import jax.numpy as jnp
from jax import lax
from jax.experimental import pallas as pl
from jax.experimental.pallas import tpu as pltpu
from jax.sharding import PartitionSpec as P

HEADS = 16
HEAD = 64
WINDOW = 2048
TILE = 512
LAG = 4
AHEAD = 5
MESH = pl.DeviceIdType.MESH
F32, BF16 = jnp.float32, jnp.bfloat16


def places():
    tower, blk, seq = lax.axis_index("tower"), lax.axis_index("blk"), lax.axis_index("seq")
    toward = 2 * seq - 1
    peers = dict(
        y=(tower, blk, 1 - seq),
        tower=(1 - tower, blk, seq),
        ahead=(tower, blk + toward, seq),
        behind=(tower, blk - toward, seq),
    )
    return tower, blk, seq, peers


def greet(has_ahead, has_behind, peers):
    barrier = pltpu.get_barrier_semaphore()
    for name in ("y", "tower"):
        pl.semaphore_signal(barrier, inc=1, device_id=peers[name], device_id_type=MESH)
    for name, present in (("ahead", has_ahead), ("behind", has_behind)):
        @pl.when(present)
        def _():
            pl.semaphore_signal(barrier, inc=1, device_id=peers[name], device_id_type=MESH)


def meet(has_ahead, has_behind):
    count = 2 + jnp.where(has_ahead, 1, 0) + jnp.where(has_behind, 1, 0)
    pl.semaphore_wait(pltpu.get_barrier_semaphore(), count)


def remote(src, dst, send, recv, device):
    return pltpu.make_async_remote_copy(
        src_ref=src, dst_ref=dst, send_sem=send, recv_sem=recv,
        device_id=device, device_id_type=MESH,
    )


def fused_kernel(
    blks, rows, cols,
    offsets_ref, q_ref, k_ref, v_ref, cq_ref, ck_ref, cv_ref, g_ref, m_ref,
    o_out, gq_out, gk_out, gv_out, gcq_out, gck_out, gcv_out,
    off_ref, side, pair, halo, partner, far, mate, pick, mask_ext, bias,
    exps, dots, sums, stat, flat, packed, peer_packed,
    mine, y_stage, y_recv, core, x_stage, x_recv, own_stage, own_recv,
    part, mate_part, gpick, gfar,
    local_sem, mask_send, mask_recv, in_send, in_recv, halo_send, halo_recv,
    partner_send, partner_recv, far_send, far_recv, share_send, share_recv,
    stat_send, stat_recv, y_send, y_recv_sem, x_send, x_recv_sem, own_send, own_recv_sem,
    swap_send, swap_recv, gfar_send, gfar_recv, gshare_send, gshare_recv,
):
    tower, blk, seq, peers = places()
    half, wide = rows, 2 * HEAD
    groups = cols // wide
    scale = HEAD ** (-0.5)
    has_low, has_high = blk > 0, blk < blks - 1
    has_ahead = ((seq == 1) & has_high) | ((seq == 0) & has_low)
    has_behind = ((seq == 1) & has_low) | ((seq == 0) & has_high)
    outs = [o_out, gq_out, gcq_out]
    grads = [gk_out, gv_out, gck_out, gcv_out]

    def strip(g):
        return pl.ds(pl.multiple_of(g * wide, wide), wide)

    def incoming(g):
        at = strip(g)
        return [
            remote(ref.at[:, at], side.at[i, 1, :, at], in_send.at[g, i], in_recv.at[g, i], peers["y"])
            for i, ref in enumerate((q_ref, cq_ref, g_ref))
        ]

    def haloed(g):
        at = strip(g)
        return [
            remote(
                ref.at[:, at], halo.at[i, :, at], halo_send.at[g, i], halo_recv.at[g, i],
                peers["ahead"],
            )
            for i, ref in enumerate((k_ref, v_ref))
        ]

    def afar(g):
        at = strip(g)
        return remote(
            pick.at[:, at], far.at[tower, :, at], far_send.at[g], far_recv.at[g], peers["ahead"]
        )

    def shared(g):
        at = strip(g)
        return remote(
            far.at[tower, :, at], far.at[tower, :, at], share_send.at[g], share_recv.at[g],
            peers["tower"],
        )

    partners = [
        remote(ref, partner.at[i], partner_send.at[i], partner_recv.at[i], peers["tower"])
        for i, ref in enumerate((ck_ref, cv_ref))
    ]
    mask_ahead = remote(m_ref, mask_ext.at[1], mask_send.at[0], mask_recv.at[0], peers["ahead"])

    def issue(g):
        for copy in incoming(g):
            copy.start()

    def issue_halo(g):
        @pl.when(has_ahead)
        def _():
            for copy in haloed(g):
                copy.start()

    def issue_far(g):
        @pl.when(has_ahead)
        def _():
            afar(g).start()

    greet(has_ahead, has_behind, peers)
    locals_ = [
        pltpu.make_async_copy(offsets_ref, off_ref, local_sem.at[7]),
        pltpu.make_async_copy(k_ref, pair.at[0], local_sem.at[0]),
        pltpu.make_async_copy(v_ref, pair.at[1], local_sem.at[1]),
        pltpu.make_async_copy(m_ref, mask_ext.at[0], local_sem.at[2]),
        pltpu.make_async_copy(q_ref, side.at[0, 0], local_sem.at[3]),
        pltpu.make_async_copy(cq_ref, side.at[1, 0], local_sem.at[4]),
        pltpu.make_async_copy(g_ref, side.at[2, 0], local_sem.at[5]),
    ]
    meet(has_ahead, has_behind)
    first = min(AHEAD, groups)
    issue(0)
    for copy in locals_:
        copy.start()
    for chain, ref in enumerate((ck_ref, cv_ref)):
        @pl.when(tower == chain)
        def _():
            pltpu.make_async_copy(ref, mate, local_sem.at[6]).start()


    @pl.when(has_ahead)
    def _():
        mask_ahead.start()

    for copy in partners:
        copy.start()
    for g in range(1, first):
        issue(g)
    for g in range(min(2, groups)):
        issue_halo(g)

    @pl.when(jnp.logical_not(has_behind))
    def _():
        halo[...] = jnp.zeros(halo.shape, BF16)
        far[...] = jnp.zeros(far.shape, BF16)
        mask_ext[1] = jnp.zeros(mask_ext.shape[1:], jnp.int32)

    @pl.when(jnp.logical_not(has_ahead))
    def _():
        x_recv[...] = jnp.zeros(x_recv.shape, BF16)
        gfar[...] = jnp.zeros(gfar.shape, BF16)

    for copy in locals_:
        copy.wait()
    for chain, ref in enumerate((ck_ref, cv_ref)):
        @pl.when(tower == chain)
        def _():
            pltpu.make_async_copy(ref, mate, local_sem.at[6]).wait()
    off = off_ref[tower, blk]
    off_ahead = off_ref[tower, jnp.clip(blk + 2 * seq - 1, 0, blks - 1)]
    chosen = jnp.where(seq == 1, jnp.where(off_ahead > 0, 1, 0), jnp.where(off_ahead < 0, 1, 0))
    uses_far = jnp.where(seq == 0, jnp.where(off > 0, 1, 0), jnp.where(off < 0, 1, 0))
    far_from = jnp.where(seq == 0, 0, jnp.where(off < 0, half + off, half))
    far_to = jnp.where(seq == 0, jnp.maximum(off, 0), half)

    for copy in partners:
        copy.wait_recv()
    pick[...] = jnp.where(chosen == 1, mate[...], partner[tower])
    for g in range(groups):
        if g >= 2:
            issue_halo(g)
        issue_far(g)

    @pl.when(has_behind)
    def _():
        mask_ahead.wait_recv()

    def column(part_at, chain):
        row = jnp.where(
            chain == 0, mask_ext[part_at, 0:1, :].astype(F32), mask_ext[part_at, 1:2, :].astype(F32)
        )
        return jnp.transpose(jnp.broadcast_to(row, (half, half)))

    row_at = lax.broadcasted_iota(jnp.int32, (half, half), 0)
    col_at = lax.broadcasted_iota(jnp.int32, (half, half), 1)
    apart = (row_at - col_at) * jnp.where(seq == 0, 1, -1)
    from_far = (row_at >= far_from) & (row_at < far_to)
    own_valid, halo_valid = column(0, tower), column(1, tower)
    cross_valid = jnp.where(from_far, column(1, 1 - tower), column(0, 1 - tower))
    allowed = (
        own_valid > 0,
        (own_valid > 0) & (apart >= 0),
        (halo_valid > 0) & (apart <= 0),
        cross_valid > 0,
    )
    for i, near in enumerate(allowed):
        add = jnp.where(near, 0.0, -1e30)
        bias[i, :, :half] = add
        bias[i, :, half:] = add

    lanes = lax.broadcasted_iota(jnp.int32, (half, wide), 1)
    zero = jnp.zeros((half, wide), BF16)

    def split(tile):
        return jnp.concatenate(
            (jnp.where(lanes < HEAD, tile, zero), jnp.where(lanes < HEAD, zero, tile)), 0
        )

    def dot_t(a, b):
        return lax.dot_general(a, b, (((1,), (1,)), ((), ())), preferred_element_type=F32)

    def dot(a, b):
        return jnp.dot(a, b, preferred_element_type=F32)

    def own_heads(both):
        return jnp.concatenate((both[:HEAD, :half], both[HEAD:, half:]), 0)

    def turned(x):
        return jnp.transpose(x.astype(F32)).astype(BF16)

    def operands(g):
        at = strip(g)
        query = [split(side[0, i, :, at] * BF16(scale)) for i in range(2)]
        cross = [split(side[1, i, :, at] * BF16(scale)) for i in range(2)]
        cot = [split(side[2, i, :, at]) for i in range(2)]
        near = [pair[i, :, at] for i in range(2)]
        edge = [halo[i, :, at] for i in range(2)]
        band = [jnp.where(from_far, far[i, :, at], partner[i, :, at]) for i in range(2)]
        return query, cross, cot, near, edge, band

    spans = (slice(0, half), slice(half, 3 * half), slice(3 * half, 4 * half), slice(4 * half, 5 * half))

    def score(g):
        query, cross, cot, near, edge, band = operands(g)
        keys = (near, [jnp.concatenate((n, e), 0) for n, e in zip(near, edge)], band, band)
        asks = (query[0], query[1], cross[0], cross[1])
        adds = (bias[0], jnp.concatenate((bias[1], bias[2]), 0), bias[3], bias[3])
        for kind in range(4):
            key, value = keys[kind]
            scores = dot_t(key, asks[kind]) + adds[kind]
            products = dot_t(value, cot[kind % 2])
            top = jnp.max(scores, axis=0, keepdims=True)
            unnormed = jnp.exp(scores - top)
            total = jnp.sum(unnormed, axis=0, keepdims=True)
            exps[g, spans[kind], :] = unnormed
            dots[g, spans[kind], :] = products
            sums[g, kind : kind + 1, :] = total
            merged = top + jnp.log(total)
            row_dot = jnp.sum(unnormed * products, axis=0, keepdims=True) / total
            stat[g, 2 * kind : 2 * kind + 1, :] = merged
            stat[g, 2 * kind + 1 : 2 * kind + 2, :] = row_dot
            for head in range(2):
                lane = slice(head * half, (head + 1) * half)
                at = 2 * kind + head
                flat[0, at : at + 1, :] = merged[:, lane]
                flat[1, at : at + 1, :] = row_dot[:, lane]
        high = flat[0].astype(BF16)
        low = (flat[0] - high.astype(F32)).astype(BF16)
        packed[g] = jnp.concatenate((high, low, flat[1].astype(BF16)), 1)

    def exchange(g):
        return remote(
            packed.at[g], peer_packed.at[g], stat_send.at[g], stat_recv.at[g], peers["y"]
        )

    def weigh(g, kind):
        peer = peer_packed[g].astype(F32)
        at = 2 * (kind ^ 1)

        def joined(rows_of):
            return jnp.concatenate((rows_of[at : at + 1], rows_of[at + 1 : at + 2]), 1)

        here, there = (
            stat[g, 2 * kind : 2 * kind + 1, :],
            joined(peer[:, :half] + peer[:, half : 2 * half]),
        )
        top = jnp.maximum(here, there)
        whole = top + jnp.log(jnp.exp(here - top) + jnp.exp(there - top))
        share_here, share_there = jnp.exp(here - whole), jnp.exp(there - whole)
        row_dot = (
            share_here * stat[g, 2 * kind + 1 : 2 * kind + 2, :]
            + share_there * joined(peer[:, 2 * half :])
        )
        weights = exps[g, spans[kind], :] * (share_here / sums[g, kind : kind + 1, :])
        grad_scores = weights * (dots[g, spans[kind], :] - row_dot)
        return weights.astype(BF16), grad_scores.astype(BF16)

    def settle(g, swap, relay):
        at = strip(g)
        query, cross, cot, near, edge, band = operands(g)
        band_t = [turned(x) for x in band]
        prob, slope = zip(*[weigh(g, kind) for kind in (2, 3)])
        cross_out = [own_heads(dot(band_t[1], prob[i])) for i in range(2)]
        cross_grad = [own_heads(dot(band_t[0], slope[i])) * scale for i in range(2)]
        band_grad = (
            dot(slope[0], cross[0]) + dot(slope[1], cross[1]),
            dot(prob[0], cot[0]) + dot(prob[1], cot[1]),
        )
        for i in range(2):
            part[i, :, at] = jnp.where(from_far, band_grad[i], 0.0).astype(BF16)
            own_stage[i, :, at] = jnp.where(from_far, 0.0, band_grad[i]).astype(BF16)
        swap()
        near_t = [turned(x) for x in near]
        both_t = [jnp.concatenate((n, turned(e)), 1) for n, e in zip(near_t, edge)]
        prob, slope = zip(*[weigh(g, kind) for kind in (0, 1)])
        self_out = [own_heads(dot(near_t[1], prob[0])), own_heads(dot(both_t[1], prob[1]))]
        self_grad = [own_heads(dot(near_t[0], slope[0])), own_heads(dot(both_t[0], slope[1]))]
        ours = (self_out[0] + cross_out[0], self_grad[0] * scale, cross_grad[0])
        theirs = (self_out[1] + cross_out[1], self_grad[1] * scale, cross_grad[1])
        for i in range(3):
            y_stage[i, :, at] = turned(theirs[i])
            mine[i, :, at] = jnp.transpose(ours[i])
        for i, (left, right, ask) in enumerate(
            ((slope[0], slope[1], query), (prob[0], prob[1], cot))
        ):
            core[i, :, at] = dot(left, ask[0]) + dot(right[:half], ask[1])
            x_stage[i, :, at] = dot(right[half:], ask[1]).astype(BF16)
        relay()

    def outgoing(g):
        at = strip(g)
        return [
            remote(
                y_stage.at[i, :, at], y_recv.at[i, :, at], y_send.at[g, i], y_recv_sem.at[g, i],
                peers["y"],
            )
            for i in range(3)
        ]

    def back(g):
        at = strip(g)
        return [
            remote(
                x_stage.at[i, :, at], x_recv.at[i, :, at], x_send.at[g, i], x_recv_sem.at[g, i],
                peers["behind"],
            )
            for i in range(2)
        ]

    def homeward(g):
        at = strip(g)
        return [
            remote(
                own_stage.at[i, :, at], own_recv.at[i, :, at],
                own_send.at[g, i], own_recv_sem.at[g, i], peers["tower"],
            )
            for i in range(2)
        ]

    def swapped_part(g):
        at = strip(g)
        return remote(
            part.at[1 - tower, :, at], mate_part.at[:, at], swap_send.at[g], swap_recv.at[g],
            peers["tower"],
        )

    def far_back(g):
        at = strip(g)
        return remote(
            gpick.at[:, at], gfar.at[tower, :, at], gfar_send.at[g], gfar_recv.at[g],
            peers["behind"],
        )

    def gshared(g):
        at = strip(g)
        return remote(
            gfar.at[tower, :, at], gfar.at[tower, :, at], gshare_send.at[g], gshare_recv.at[g],
            peers["tower"],
        )

    def share(g):
        @pl.when(has_behind)
        def _():
            afar(g).wait_recv()
            shared(g).start()

    def compute(g):
        def swap():
            swapped_part(g).start()
            for copy in homeward(g):
                copy.start()

        def relay():
            at = strip(g)
            for copy in outgoing(g):
                copy.start()
            swapped_part(g).wait_recv()
            gpick[:, at] = jnp.where(uses_far == 1, part[tower, :, at], mate_part[:, at])

            @pl.when(has_behind)
            def _():
                far_back(g).start()
                for copy in back(g):
                    copy.start()

        settle(g, swap, relay)

    def finish(g):
        at = strip(g)

        @pl.when(has_ahead)
        def _():
            far_back(g).wait_recv()
            gshared(g).start()
            for copy in back(g):
                copy.wait_recv()

        for i in range(2):
            grads[i][:, at] = (core[i, :, at] + x_recv[i, :, at].astype(F32)).astype(BF16)
        for i, copy in enumerate(outgoing(g)):
            copy.wait_recv()
            outs[i][:, at] = (mine[i, :, at] + y_recv[i, :, at].astype(F32)).astype(BF16)

        @pl.when(has_ahead)
        def _():
            gshared(g).wait_recv()

        for i, copy in enumerate(homeward(g)):
            copy.wait_recv()
            more = jnp.where(chosen == 1, gfar[i, :, at].astype(F32), 0.0)
            grads[2 + i][:, at] = (own_recv[i, :, at].astype(F32) + more).astype(BF16)

    def step(g, carry):
        @pl.when(g + AHEAD < groups)
        def _():
            issue(g + AHEAD)

        @pl.when(g < groups)
        def _():
            for copy in incoming(g):
                copy.wait_recv()

            @pl.when(has_behind)
            def _():
                for copy in haloed(g):
                    copy.wait_recv()
                shared(g).wait_recv()

            score(g)
            exchange(g).start()

        @pl.when(g + 1 < groups)
        def _():
            share(g + 1)

        @pl.when(g >= LAG)
        def _():
            exchange(g - LAG).wait_recv()
            compute(g - LAG)

        return carry

    share(0)
    lax.fori_loop(0, groups + LAG, step, 0)

    def end(g, carry):
        finish(g)
        for copy in incoming(g) + outgoing(g) + homeward(g):
            copy.wait_send()
        exchange(g).wait_send()
        swapped_part(g).wait_send()

        @pl.when(has_ahead)
        def _():
            for copy in haloed(g):
                copy.wait_send()
            afar(g).wait_send()
            gshared(g).wait_send()

        @pl.when(has_behind)
        def _():
            shared(g).wait_send()
            far_back(g).wait_send()
            for copy in back(g):
                copy.wait_send()

        return carry

    for copy in partners:
        copy.wait_send()

    @pl.when(has_ahead)
    def _():
        mask_ahead.wait_send()

    lax.fori_loop(0, groups, end, 0)


def copy_kernel(*refs):
    count = len(refs) // 2
    sem = refs[-1]
    copies = [
        pltpu.make_async_copy(src, dst, sem.at[i])
        for i, (src, dst) in enumerate(zip(refs[:count], refs[count:-1]))
    ]
    for copy in copies:
        copy.start()
    for copy in copies:
        copy.wait()


def paired(
    queries, key_rows, value_rows, cross_queries, cross_keys, cross_values, grad_out,
    offsets, key_valid,
):
    blks = lax.axis_size("blk")
    values = [
        value[0] for value in (
            queries, key_rows, value_rows, cross_queries, cross_keys, cross_values, grad_out
        )
    ]
    rows, cols = queries.shape[1:]
    groups, wide = cols // (2 * HEAD), 2 * rows
    dma = pltpu.SemaphoreType.DMA
    full = jax.ShapeDtypeStruct((rows, cols), BF16)
    narrow = pltpu.VMEM((2, rows, cols), BF16)
    single = pltpu.VMEM((rows, cols), BF16)
    scored = pltpu.VMEM((groups, 5 * rows, wide), F32)
    stats = pltpu.VMEM((groups, 8, wide), F32)
    bits = pltpu.VMEM((groups, 8, 3 * rows), BF16)
    pairs = (dma((groups, 2)),) * 2
    ones = (dma((groups,)),) * 2
    outs = pl.pallas_call(
        functools.partial(fused_kernel, blks, rows, cols),
        out_shape=(pltpu.VMEM((rows, cols), BF16),) * 7,
        in_specs=[pl.BlockSpec(memory_space=pl.ANY)] * 9,
        out_specs=(pl.BlockSpec(memory_space=pltpu.VMEM),) * 7,
        scratch_shapes=[
            pltpu.SMEM(offsets.shape, jnp.int32),
            pltpu.VMEM((3, 2, rows, cols), BF16),
            narrow, narrow, narrow, narrow, single, single,
            pltpu.VMEM((2,) + key_valid.shape, jnp.int32),
            pltpu.VMEM((4, rows, wide), F32),
            scored, scored, stats, stats,
            pltpu.VMEM((2, 8, rows), F32), bits, bits,
            pltpu.VMEM((3, rows, cols), F32),
            pltpu.VMEM((3, rows, cols), BF16), pltpu.VMEM((3, rows, cols), BF16),
            pltpu.VMEM((2, rows, cols), F32),
            narrow, narrow, narrow, narrow, narrow, single, single, narrow,
            dma((8,)), dma((1,)), dma((1,)),
            dma((groups, 3)), dma((groups, 3)), *pairs,
            dma((2,)), dma((2,)), *ones, *ones,
            *ones, dma((groups, 3)), dma((groups, 3)), *pairs, *pairs,
            *ones, *ones, *ones,
        ],
        compiler_params=pltpu.CompilerParams(collective_id=0, has_side_effects=True),
        name="attend_pairs",
    )(offsets, *values, key_valid)
    outs = pl.pallas_call(
        copy_kernel,
        out_shape=(full,) * 7,
        in_specs=[pl.BlockSpec(memory_space=pl.ANY)] * 7,
        out_specs=(pl.BlockSpec(memory_space=pl.ANY),) * 7,
        scratch_shapes=[dma((7,))],
        compiler_params=pltpu.CompilerParams(vmem_limit_bytes=1 << 20),
        name="hand_over",
    )(*outs)
    return tuple(piece[None] for piece in outs)


def extended(block, sides, width):
    for axis, dim in sides:
        count = lax.axis_size(axis)
        forward = [(i, i + 1) for i in range(count - 1)]
        backward = [(target, source) for source, target in forward]
        low = lax.ppermute(
            lax.slice_in_dim(block, block.shape[dim] - width, None, axis=dim), axis, forward
        )
        high = lax.ppermute(lax.slice_in_dim(block, 0, width, axis=dim), axis, backward)
        block = jnp.concatenate([low, block, high], axis=dim)
    return block


def swapped(value, axis, bit):
    mask = 2**bit
    pairs = [(source, source ^ mask) for source in range(lax.axis_size(axis))]
    return lax.ppermute(value, axis, pairs)


def passed_along(block, axis, distance):
    devices = range(lax.axis_size(axis))
    route = [(i - distance, i) for i in devices if i - distance in devices]
    return lax.ppermute(block, axis, route)


def attend(query_tile, grad_tile, key_block, value_block, allowed, heads_here):
    score_scale = HEAD ** (-0.5)
    rows_count = query_tile.shape[0]
    keys_count = key_block.shape[0]
    q_heads = query_tile.reshape(rows_count, heads_here, HEAD)
    g_heads = grad_tile.reshape(rows_count, heads_here, HEAD)
    k_heads = key_block.reshape(keys_count, heads_here, HEAD)
    v_heads = value_block.reshape(keys_count, heads_here, HEAD)
    scores = (
        jnp.einsum("qhe,khe->hqk", q_heads, k_heads, preferred_element_type=jnp.float32)
        * score_scale
    )
    scores = jnp.where(allowed[None], scores, -1e30)
    row_max = jnp.max(scores, axis=2)
    unnormed = jnp.exp(scores - row_max[:, :, None])
    row_sum = jnp.sum(unnormed, axis=2)
    weights = unnormed / row_sum[:, :, None]
    prob_bf = weights.astype(jnp.bfloat16)
    result = jnp.einsum(
        "hqk,khe->qhe", prob_bf, v_heads, preferred_element_type=jnp.float32
    ).reshape(rows_count, -1)
    grad_probs = jnp.einsum("qhe,khe->hqk", g_heads, v_heads, preferred_element_type=jnp.float32)
    row_dot = jnp.sum(weights * grad_probs, axis=2)
    grad_scores = (weights * (grad_probs - row_dot[:, :, None]) * score_scale).astype(jnp.bfloat16)
    grad_query = jnp.einsum(
        "hqk,khe->qhe", grad_scores, k_heads, preferred_element_type=jnp.float32
    ).reshape(rows_count, -1)
    grad_key = jnp.einsum(
        "hqk,qhe->khe", grad_scores, q_heads, preferred_element_type=jnp.float32
    ).reshape(keys_count, -1)
    grad_value = jnp.einsum(
        "hqk,qhe->khe", prob_bf, g_heads, preferred_element_type=jnp.float32
    ).reshape(keys_count, -1)
    return (result, grad_query, grad_key, grad_value, jnp.stack((row_max, row_sum, row_dot)))


def shards(
    queries,
    key_rows,
    value_rows,
    cross_queries,
    cross_keys,
    cross_values,
    grad_out,
    offsets,
    key_valid,
):
    seq_count = lax.axis_size("seq")
    heads_here = HEADS // seq_count
    local_rows = (
        queries[0],
        key_rows[0],
        value_rows[0],
        cross_queries[0],
        cross_keys[0],
        cross_values[0],
        grad_out[0],
    )
    query_here, key_here, value_here, cross_query, cross_key, cross_value, cotangent = (
        lax.all_to_all(local_rows[0], "seq", split_axis=1, concat_axis=0, tiled=True),
        lax.all_to_all(local_rows[1], "seq", split_axis=1, concat_axis=0, tiled=True),
        lax.all_to_all(local_rows[2], "seq", split_axis=1, concat_axis=0, tiled=True),
        lax.all_to_all(local_rows[3], "seq", split_axis=1, concat_axis=0, tiled=True),
        lax.all_to_all(local_rows[4], "seq", split_axis=1, concat_axis=0, tiled=True),
        lax.all_to_all(local_rows[5], "seq", split_axis=1, concat_axis=0, tiled=True),
        lax.all_to_all(local_rows[6], "seq", split_axis=1, concat_axis=0, tiled=True),
    )
    block_len = query_here.shape[0]
    columns = query_here.shape[1]
    half_width = min(WINDOW // 2, block_len // 2)
    tile_rows = min(TILE, block_len)
    tile_count = block_len // tile_rows
    window_span = tile_rows + 2 * half_width
    tower_id = lax.axis_index("tower")
    block_id = lax.axis_index("blk")
    block_mask = lax.all_gather(key_valid, "seq", axis=1, tiled=True)
    mask_ext = extended(block_mask, (("blk", 1),), half_width)
    self_valid = lax.dynamic_index_in_dim(mask_ext, tower_id, 0, keepdims=False)
    other_valid = lax.dynamic_index_in_dim(mask_ext, 1 - tower_id, 0, keepdims=False)
    pair_ext = extended(jnp.stack((key_here, value_here)), (("blk", 1),), half_width)
    partner = swapped(jnp.stack((cross_key, cross_value)), "tower", 0)
    partner_ext = extended(partner, (("blk", 1),), half_width)
    align_shift = offsets[tower_id, block_id]
    band_start = half_width + align_shift
    band = lax.dynamic_slice_in_dim(partner_ext, band_start, block_len, 1)
    band_valid = lax.dynamic_slice_in_dim(other_valid, band_start, block_len) > 0
    rows_local = jnp.arange(tile_rows)
    keys_local = jnp.arange(window_span)
    near = jnp.abs(rows_local[:, None] + half_width - keys_local[None, :]) <= half_width

    def self_step(carry, tile_index):
        grad_key_acc, grad_value_acc = carry
        tile_start = tile_index * tile_rows
        query_tile = lax.dynamic_slice_in_dim(query_here, tile_start, tile_rows, 0)
        grad_tile = lax.dynamic_slice_in_dim(cotangent, tile_start, tile_rows, 0)
        key_window = lax.dynamic_slice_in_dim(pair_ext[0], tile_start, window_span, 0)
        value_window = lax.dynamic_slice_in_dim(pair_ext[1], tile_start, window_span, 0)
        allowed = (
            near & (lax.dynamic_slice_in_dim(self_valid, tile_start, window_span) > 0)[None, :]
        )
        result, grad_query, grad_key, grad_value, stats = attend(
            query_tile, grad_tile, key_window, value_window, allowed, heads_here
        )
        grad_key_acc = lax.dynamic_update_slice_in_dim(
            grad_key_acc,
            lax.dynamic_slice_in_dim(grad_key_acc, tile_start, window_span, 0) + grad_key,
            tile_start,
            0,
        )
        grad_value_acc = lax.dynamic_update_slice_in_dim(
            grad_value_acc,
            lax.dynamic_slice_in_dim(grad_value_acc, tile_start, window_span, 0) + grad_value,
            tile_start,
            0,
        )
        return ((grad_key_acc, grad_value_acc), (result, grad_query, stats))

    def cross_step(carry, tile_index):
        grad_key_acc, grad_value_acc = carry
        tile_start = tile_index * tile_rows
        query_tile = lax.dynamic_slice_in_dim(cross_query, tile_start, tile_rows, 0)
        grad_tile = lax.dynamic_slice_in_dim(cotangent, tile_start, tile_rows, 0)
        result, grad_query, grad_key, grad_value, stats = attend(
            query_tile, grad_tile, band[0], band[1], band_valid[None, :], heads_here
        )
        return ((grad_key_acc + grad_key, grad_value_acc + grad_value), (result, grad_query))

    zeros_ext = jnp.zeros((block_len + 2 * half_width, columns), jnp.float32)
    zeros_band = jnp.zeros((block_len, columns), jnp.float32)
    tile_ids = jnp.arange(tile_count)
    (self_gk, self_gv), (self_out, self_gq, self_stats) = lax.scan(
        self_step, (zeros_ext, zeros_ext), tile_ids
    )
    (cross_gk, cross_gv), (cross_out, cross_gq) = lax.scan(
        cross_step, (zeros_band, zeros_band), tile_ids
    )
    self_out = self_out.reshape(block_len, columns)
    cross_out = cross_out.reshape(block_len, columns)
    self_stats = jnp.transpose(self_stats, (1, 2, 0, 3)).reshape(3, heads_here, block_len)
    attended = (self_out + cross_out).astype(jnp.bfloat16)
    cross_ext = jnp.zeros((2, block_len + 2 * half_width, columns), jnp.float32)
    cross_ext = lax.dynamic_update_slice_in_dim(
        cross_ext, jnp.stack((cross_gk, cross_gv)), band_start, 1
    )
    self_ext = jnp.stack((self_gk, self_gv))
    self_core = self_ext[:, half_width : half_width + block_len]
    cross_core = cross_ext[:, half_width : half_width + block_len]
    upper_cut = block_len - half_width
    lower_send = jnp.concatenate((self_ext[:, :half_width], cross_ext[:, :half_width]), 0)
    upper_send = jnp.concatenate(
        (self_ext[:, block_len + half_width :], cross_ext[:, block_len + half_width :]), 0
    )
    from_above = passed_along(lower_send.astype(jnp.bfloat16), "blk", -1).astype(lower_send.dtype)
    from_below = passed_along(upper_send.astype(jnp.bfloat16), "blk", 1).astype(upper_send.dtype)
    self_core = (
        self_core.at[:, upper_cut:].add(from_above[:2]).at[:, :half_width].add(from_below[:2])
    )
    cross_core = (
        cross_core.at[:, upper_cut:].add(from_above[2:]).at[:, :half_width].add(from_below[2:])
    )
    returned = swapped(cross_core.astype(jnp.bfloat16), "tower", 0)
    head_outs = (
        attended,
        self_gq.reshape(block_len, columns).astype(jnp.bfloat16),
        self_core[0].astype(jnp.bfloat16),
        self_core[1].astype(jnp.bfloat16),
        cross_gq.reshape(block_len, columns).astype(jnp.bfloat16),
        returned[0],
        returned[1],
    )
    token_outs = (
        lax.all_to_all(head_outs[0], "seq", split_axis=0, concat_axis=1, tiled=True),
        lax.all_to_all(head_outs[1], "seq", split_axis=0, concat_axis=1, tiled=True),
        lax.all_to_all(head_outs[2], "seq", split_axis=0, concat_axis=1, tiled=True),
        lax.all_to_all(head_outs[3], "seq", split_axis=0, concat_axis=1, tiled=True),
        lax.all_to_all(head_outs[4], "seq", split_axis=0, concat_axis=1, tiled=True),
        lax.all_to_all(head_outs[5], "seq", split_axis=0, concat_axis=1, tiled=True),
        lax.all_to_all(head_outs[6], "seq", split_axis=0, concat_axis=1, tiled=True),
    )
    return tuple((piece[None] for piece in token_outs))


def solution(mesh):
    in_specs = (
        P("tower", ("blk", "seq"), None),
        P("tower", ("blk", "seq"), None),
        P("tower", ("blk", "seq"), None),
        P("tower", ("blk", "seq"), None),
        P("tower", ("blk", "seq"), None),
        P("tower", ("blk", "seq"), None),
        P("tower", ("blk", "seq"), None),
        P(),
        P(None, ("blk", "seq")),
    )
    out_specs = (
        P("tower", ("blk", "seq"), None),
        P("tower", ("blk", "seq"), None),
        P("tower", ("blk", "seq"), None),
        P("tower", ("blk", "seq"), None),
        P("tower", ("blk", "seq"), None),
        P("tower", ("blk", "seq"), None),
        P("tower", ("blk", "seq"), None),
    )
    body = paired if mesh.shape["seq"] == 2 else shards
    return jax.shard_map(body, mesh=mesh, in_specs=in_specs, out_specs=out_specs, check_vma=False)
```

```python
import functools

import jax
import jax.numpy as jnp
from jax import lax
from jax.experimental import pallas as pl
from jax.experimental.pallas import tpu as pltpu
from jax.sharding import PartitionSpec as P

HEADS = 16
HEAD = 64
WINDOW = 2048
TILE = 512
LAG = 4
AHEAD = 4
MESH = pl.DeviceIdType.MESH
F32, BF16 = jnp.float32, jnp.bfloat16


def places():
    tower, blk, seq = lax.axis_index("tower"), lax.axis_index("blk"), lax.axis_index("seq")
    toward = 2 * seq - 1
    peers = dict(
        y=(tower, blk, 1 - seq),
        tower=(1 - tower, blk, seq),
        ahead=(tower, blk + toward, seq),
        behind=(tower, blk - toward, seq),
    )
    return tower, blk, seq, peers


def greet(has_ahead, has_behind, peers):
    barrier = pltpu.get_barrier_semaphore()
    for name in ("y", "tower"):
        pl.semaphore_signal(barrier, inc=1, device_id=peers[name], device_id_type=MESH)
    for name, present in (("ahead", has_ahead), ("behind", has_behind)):
        @pl.when(present)
        def _():
            pl.semaphore_signal(barrier, inc=1, device_id=peers[name], device_id_type=MESH)


def meet(has_ahead, has_behind):
    count = 2 + jnp.where(has_ahead, 1, 0) + jnp.where(has_behind, 1, 0)
    pl.semaphore_wait(pltpu.get_barrier_semaphore(), count)


def remote(src, dst, send, recv, device):
    return pltpu.make_async_remote_copy(
        src_ref=src, dst_ref=dst, send_sem=send, recv_sem=recv,
        device_id=device, device_id_type=MESH,
    )


def fused_kernel(
    blks, rows, cols,
    offsets_ref, q_ref, k_ref, v_ref, cq_ref, ck_ref, cv_ref, g_ref, m_ref,
    o_out, gq_out, gk_out, gv_out, gcq_out, gck_out, gcv_out,
    off_ref, side, pair, halo, partner, far, mate, pick, mask_ext, bias,
    exps, dots, sums, stat, flat, packed, peer_packed,
    mine, y_stage, y_recv, core, x_stage, x_recv, own_stage, own_recv,
    part, mate_part, gpick, gfar,
    local_sem, mask_send, mask_recv, in_send, in_recv, halo_send, halo_recv,
    partner_send, partner_recv, far_send, far_recv, share_send, share_recv,
    stat_send, stat_recv, y_send, y_recv_sem, x_send, x_recv_sem, own_send, own_recv_sem,
    swap_send, swap_recv, gfar_send, gfar_recv, gshare_send, gshare_recv,
):
    tower, blk, seq, peers = places()
    half, wide = rows, 2 * HEAD
    groups = cols // wide
    scale = HEAD ** (-0.5)
    has_low, has_high = blk > 0, blk < blks - 1
    has_ahead = ((seq == 1) & has_high) | ((seq == 0) & has_low)
    has_behind = ((seq == 1) & has_low) | ((seq == 0) & has_high)
    outs = [o_out, gq_out, gcq_out]
    grads = [gk_out, gv_out, gck_out, gcv_out]

    def strip(g):
        return pl.ds(pl.multiple_of(g * wide, wide), wide)

    def incoming(g):
        at = strip(g)
        return [
            remote(ref.at[:, at], side.at[i, 1, :, at], in_send.at[g, i], in_recv.at[g, i], peers["y"])
            for i, ref in enumerate((q_ref, cq_ref, g_ref))
        ]

    def haloed(g):
        at = strip(g)
        return [
            remote(
                ref.at[:, at], halo.at[i, :, at], halo_send.at[g, i], halo_recv.at[g, i],
                peers["ahead"],
            )
            for i, ref in enumerate((k_ref, v_ref))
        ]

    def afar(g):
        at = strip(g)
        return remote(
            pick.at[:, at], far.at[tower, :, at], far_send.at[g], far_recv.at[g], peers["ahead"]
        )

    def shared(g):
        at = strip(g)
        return remote(
            far.at[tower, :, at], far.at[tower, :, at], share_send.at[g], share_recv.at[g],
            peers["tower"],
        )

    partners = [
        remote(ref, partner.at[i], partner_send.at[i], partner_recv.at[i], peers["tower"])
        for i, ref in enumerate((ck_ref, cv_ref))
    ]
    mask_ahead = remote(m_ref, mask_ext.at[1], mask_send.at[0], mask_recv.at[0], peers["ahead"])

    def issue(g):
        for copy in incoming(g):
            copy.start()

    def issue_halo(g):
        @pl.when(has_ahead)
        def _():
            for copy in haloed(g):
                copy.start()

    def issue_far(g):
        @pl.when(has_ahead)
        def _():
            afar(g).start()

    greet(has_ahead, has_behind, peers)
    locals_ = [
        pltpu.make_async_copy(offsets_ref, off_ref, local_sem.at[7]),
        pltpu.make_async_copy(k_ref, pair.at[0], local_sem.at[0]),
        pltpu.make_async_copy(v_ref, pair.at[1], local_sem.at[1]),
        pltpu.make_async_copy(m_ref, mask_ext.at[0], local_sem.at[2]),
        pltpu.make_async_copy(q_ref, side.at[0, 0], local_sem.at[3]),
        pltpu.make_async_copy(cq_ref, side.at[1, 0], local_sem.at[4]),
        pltpu.make_async_copy(g_ref, side.at[2, 0], local_sem.at[5]),
    ]
    for copy in locals_:
        copy.start()
    for chain, ref in enumerate((ck_ref, cv_ref)):
        @pl.when(tower == chain)
        def _():
            pltpu.make_async_copy(ref, mate, local_sem.at[6]).start()

    @pl.when(jnp.logical_not(has_behind))
    def _():
        halo[...] = jnp.zeros(halo.shape, BF16)
        far[...] = jnp.zeros(far.shape, BF16)
        mask_ext[1] = jnp.zeros(mask_ext.shape[1:], jnp.int32)

    @pl.when(jnp.logical_not(has_ahead))
    def _():
        x_recv[...] = jnp.zeros(x_recv.shape, BF16)
        gfar[...] = jnp.zeros(gfar.shape, BF16)

    meet(has_ahead, has_behind)
    first = min(AHEAD, groups)
    issue(0)

    @pl.when(has_ahead)
    def _():
        mask_ahead.start()

    for copy in partners:
        copy.start()
    for g in range(1, first):
        issue(g)
    for g in range(min(2, groups)):
        issue_halo(g)
    for copy in locals_:
        copy.wait()
    for chain, ref in enumerate((ck_ref, cv_ref)):
        @pl.when(tower == chain)
        def _():
            pltpu.make_async_copy(ref, mate, local_sem.at[6]).wait()
    off = off_ref[tower, blk]
    off_ahead = off_ref[tower, jnp.clip(blk + 2 * seq - 1, 0, blks - 1)]
    chosen = jnp.where(seq == 1, jnp.where(off_ahead > 0, 1, 0), jnp.where(off_ahead < 0, 1, 0))
    uses_far = jnp.where(seq == 0, jnp.where(off > 0, 1, 0), jnp.where(off < 0, 1, 0))
    far_from = jnp.where(seq == 0, 0, jnp.where(off < 0, half + off, half))
    far_to = jnp.where(seq == 0, jnp.maximum(off, 0), half)

    for copy in partners:
        copy.wait_recv()
    pick[...] = jnp.where(chosen == 1, mate[...], partner[tower])
    for g in range(groups):
        if g >= 2:
            issue_halo(g)
        issue_far(g)

    @pl.when(has_behind)
    def _():
        mask_ahead.wait_recv()

    def column(part_at, chain):
        row = jnp.where(
            chain == 0, mask_ext[part_at, 0:1, :].astype(F32), mask_ext[part_at, 1:2, :].astype(F32)
        )
        return jnp.transpose(jnp.broadcast_to(row, (half, half)))

    row_at = lax.broadcasted_iota(jnp.int32, (half, half), 0)
    col_at = lax.broadcasted_iota(jnp.int32, (half, half), 1)
    apart = (row_at - col_at) * jnp.where(seq == 0, 1, -1)
    from_far = (row_at >= far_from) & (row_at < far_to)
    own_valid, halo_valid = column(0, tower), column(1, tower)
    cross_valid = jnp.where(from_far, column(1, 1 - tower), column(0, 1 - tower))
    allowed = (
        own_valid > 0,
        (own_valid > 0) & (apart >= 0),
        (halo_valid > 0) & (apart <= 0),
        cross_valid > 0,
    )
    for i, near in enumerate(allowed):
        add = jnp.where(near, 0.0, -1e30)
        bias[i, :, :half] = add
        bias[i, :, half:] = add

    lanes = lax.broadcasted_iota(jnp.int32, (half, wide), 1)
    zero = jnp.zeros((half, wide), BF16)

    def split(tile):
        return jnp.concatenate(
            (jnp.where(lanes < HEAD, tile, zero), jnp.where(lanes < HEAD, zero, tile)), 0
        )

    def dot_t(a, b):
        return lax.dot_general(a, b, (((1,), (1,)), ((), ())), preferred_element_type=F32)

    def dot(a, b):
        return jnp.dot(a, b, preferred_element_type=F32)

    def own_heads(both):
        return jnp.concatenate((both[:HEAD, :half], both[HEAD:, half:]), 0)

    def turned(x):
        return jnp.transpose(x.astype(F32)).astype(BF16)

    def operands(g):
        at = strip(g)
        query = [split(side[0, i, :, at] * BF16(scale)) for i in range(2)]
        cross = [split(side[1, i, :, at] * BF16(scale)) for i in range(2)]
        cot = [split(side[2, i, :, at]) for i in range(2)]
        near = [pair[i, :, at] for i in range(2)]
        edge = [halo[i, :, at] for i in range(2)]
        band = [jnp.where(from_far, far[i, :, at], partner[i, :, at]) for i in range(2)]
        return query, cross, cot, near, edge, band

    spans = (slice(0, half), slice(half, 3 * half), slice(3 * half, 4 * half), slice(4 * half, 5 * half))

    def score(g):
        query, cross, cot, near, edge, band = operands(g)
        keys = (near, [jnp.concatenate((n, e), 0) for n, e in zip(near, edge)], band, band)
        asks = (query[0], query[1], cross[0], cross[1])
        adds = (bias[0], jnp.concatenate((bias[1], bias[2]), 0), bias[3], bias[3])
        for kind in range(4):
            key, value = keys[kind]
            scores = dot_t(key, asks[kind]) + adds[kind]
            products = dot_t(value, cot[kind % 2])
            top = jnp.max(scores, axis=0, keepdims=True)
            unnormed = jnp.exp(scores - top)
            total = jnp.sum(unnormed, axis=0, keepdims=True)
            exps[g, spans[kind], :] = unnormed
            dots[g, spans[kind], :] = products
            sums[g, kind : kind + 1, :] = total
            merged = top + jnp.log(total)
            row_dot = jnp.sum(unnormed * products, axis=0, keepdims=True) / total
            stat[g, 2 * kind : 2 * kind + 1, :] = merged
            stat[g, 2 * kind + 1 : 2 * kind + 2, :] = row_dot
            for head in range(2):
                lane = slice(head * half, (head + 1) * half)
                at = 2 * kind + head
                flat[0, at : at + 1, :] = merged[:, lane]
                flat[1, at : at + 1, :] = row_dot[:, lane]
        high = flat[0].astype(BF16)
        low = (flat[0] - high.astype(F32)).astype(BF16)
        packed[g] = jnp.concatenate((high, low, flat[1].astype(BF16)), 1)

    def exchange(g):
        return remote(
            packed.at[g], peer_packed.at[g], stat_send.at[g], stat_recv.at[g], peers["y"]
        )

    def weigh(g, kind):
        peer = peer_packed[g].astype(F32)
        at = 2 * (kind ^ 1)

        def joined(rows_of):
            return jnp.concatenate((rows_of[at : at + 1], rows_of[at + 1 : at + 2]), 1)

        here, there = (
            stat[g, 2 * kind : 2 * kind + 1, :],
            joined(peer[:, :half] + peer[:, half : 2 * half]),
        )
        top = jnp.maximum(here, there)
        whole = top + jnp.log(jnp.exp(here - top) + jnp.exp(there - top))
        share_here, share_there = jnp.exp(here - whole), jnp.exp(there - whole)
        row_dot = (
            share_here * stat[g, 2 * kind + 1 : 2 * kind + 2, :]
            + share_there * joined(peer[:, 2 * half :])
        )
        weights = exps[g, spans[kind], :] * (share_here / sums[g, kind : kind + 1, :])
        grad_scores = weights * (dots[g, spans[kind], :] - row_dot)
        return weights.astype(BF16), grad_scores.astype(BF16)

    def settle(g, swap, relay):
        at = strip(g)
        query, cross, cot, near, edge, band = operands(g)
        band_t = [turned(x) for x in band]
        prob, slope = zip(*[weigh(g, kind) for kind in (2, 3)])
        cross_out = [own_heads(dot(band_t[1], prob[i])) for i in range(2)]
        cross_grad = [own_heads(dot(band_t[0], slope[i])) * scale for i in range(2)]
        band_grad = (
            dot(slope[0], cross[0]) + dot(slope[1], cross[1]),
            dot(prob[0], cot[0]) + dot(prob[1], cot[1]),
        )
        for i in range(2):
            part[i, :, at] = jnp.where(from_far, band_grad[i], 0.0).astype(BF16)
            own_stage[i, :, at] = jnp.where(from_far, 0.0, band_grad[i]).astype(BF16)
        swap()
        near_t = [turned(x) for x in near]
        both_t = [jnp.concatenate((n, turned(e)), 1) for n, e in zip(near_t, edge)]
        prob, slope = zip(*[weigh(g, kind) for kind in (0, 1)])
        self_out = [own_heads(dot(near_t[1], prob[0])), own_heads(dot(both_t[1], prob[1]))]
        self_grad = [own_heads(dot(near_t[0], slope[0])), own_heads(dot(both_t[0], slope[1]))]
        ours = (self_out[0] + cross_out[0], self_grad[0] * scale, cross_grad[0])
        theirs = (self_out[1] + cross_out[1], self_grad[1] * scale, cross_grad[1])
        for i in range(3):
            y_stage[i, :, at] = turned(theirs[i])
            mine[i, :, at] = jnp.transpose(ours[i])
        for i, (left, right, ask) in enumerate(
            ((slope[0], slope[1], query), (prob[0], prob[1], cot))
        ):
            core[i, :, at] = dot(left, ask[0]) + dot(right[:half], ask[1])
            x_stage[i, :, at] = dot(right[half:], ask[1]).astype(BF16)
        relay()

    def outgoing(g):
        at = strip(g)
        return [
            remote(
                y_stage.at[i, :, at], y_recv.at[i, :, at], y_send.at[g, i], y_recv_sem.at[g, i],
                peers["y"],
            )
            for i in range(3)
        ]

    def back(g):
        at = strip(g)
        return [
            remote(
                x_stage.at[i, :, at], x_recv.at[i, :, at], x_send.at[g, i], x_recv_sem.at[g, i],
                peers["behind"],
            )
            for i in range(2)
        ]

    def homeward(g):
        at = strip(g)
        return [
            remote(
                own_stage.at[i, :, at], own_recv.at[i, :, at],
                own_send.at[g, i], own_recv_sem.at[g, i], peers["tower"],
            )
            for i in range(2)
        ]

    def swapped_part(g):
        at = strip(g)
        return remote(
            part.at[1 - tower, :, at], mate_part.at[:, at], swap_send.at[g], swap_recv.at[g],
            peers["tower"],
        )

    def far_back(g):
        at = strip(g)
        return remote(
            gpick.at[:, at], gfar.at[tower, :, at], gfar_send.at[g], gfar_recv.at[g],
            peers["behind"],
        )

    def gshared(g):
        at = strip(g)
        return remote(
            gfar.at[tower, :, at], gfar.at[tower, :, at], gshare_send.at[g], gshare_recv.at[g],
            peers["tower"],
        )

    def share(g):
        @pl.when(has_behind)
        def _():
            afar(g).wait_recv()
            shared(g).start()

    def compute(g):
        def swap():
            swapped_part(g).start()
            for copy in homeward(g):
                copy.start()

        def relay():
            at = strip(g)
            for copy in outgoing(g):
                copy.start()
            swapped_part(g).wait_recv()
            gpick[:, at] = jnp.where(uses_far == 1, part[tower, :, at], mate_part[:, at])

            @pl.when(has_behind)
            def _():
                far_back(g).start()
                for copy in back(g):
                    copy.start()

        settle(g, swap, relay)

    def finish(g):
        at = strip(g)

        @pl.when(has_ahead)
        def _():
            far_back(g).wait_recv()
            gshared(g).start()
            for copy in back(g):
                copy.wait_recv()

        for i in range(2):
            grads[i][:, at] = (core[i, :, at] + x_recv[i, :, at].astype(F32)).astype(BF16)
        for i, copy in enumerate(outgoing(g)):
            copy.wait_recv()
            outs[i][:, at] = (mine[i, :, at] + y_recv[i, :, at].astype(F32)).astype(BF16)

        @pl.when(has_ahead)
        def _():
            gshared(g).wait_recv()

        for i, copy in enumerate(homeward(g)):
            copy.wait_recv()
            more = jnp.where(chosen == 1, gfar[i, :, at].astype(F32), 0.0)
            grads[2 + i][:, at] = (own_recv[i, :, at].astype(F32) + more).astype(BF16)

    def step(g, carry):
        @pl.when(g + AHEAD < groups)
        def _():
            issue(g + AHEAD)

        @pl.when(g < groups)
        def _():
            for copy in incoming(g):
                copy.wait_recv()

            @pl.when(has_behind)
            def _():
                for copy in haloed(g):
                    copy.wait_recv()
                shared(g).wait_recv()

            score(g)
            exchange(g).start()

        @pl.when(g + 1 < groups)
        def _():
            share(g + 1)

        @pl.when(g >= LAG)
        def _():
            exchange(g - LAG).wait_recv()
            compute(g - LAG)

        return carry

    share(0)
    lax.fori_loop(0, groups + LAG, step, 0)

    def end(g, carry):
        finish(g)
        for copy in incoming(g) + outgoing(g) + homeward(g):
            copy.wait_send()
        exchange(g).wait_send()
        swapped_part(g).wait_send()

        @pl.when(has_ahead)
        def _():
            for copy in haloed(g):
                copy.wait_send()
            afar(g).wait_send()
            gshared(g).wait_send()

        @pl.when(has_behind)
        def _():
            shared(g).wait_send()
            far_back(g).wait_send()
            for copy in back(g):
                copy.wait_send()

        return carry

    for copy in partners:
        copy.wait_send()

    @pl.when(has_ahead)
    def _():
        mask_ahead.wait_send()

    lax.fori_loop(0, groups, end, 0)


def copy_kernel(*refs):
    count = len(refs) // 2
    sem = refs[-1]
    copies = [
        pltpu.make_async_copy(src, dst, sem.at[i])
        for i, (src, dst) in enumerate(zip(refs[:count], refs[count:-1]))
    ]
    for copy in copies:
        copy.start()
    for copy in copies:
        copy.wait()


def paired(
    queries, key_rows, value_rows, cross_queries, cross_keys, cross_values, grad_out,
    offsets, key_valid,
):
    blks = lax.axis_size("blk")
    values = [
        value[0] for value in (
            queries, key_rows, value_rows, cross_queries, cross_keys, cross_values, grad_out
        )
    ]
    rows, cols = queries.shape[1:]
    groups, wide = cols // (2 * HEAD), 2 * rows
    dma = pltpu.SemaphoreType.DMA
    full = jax.ShapeDtypeStruct((rows, cols), BF16)
    narrow = pltpu.VMEM((2, rows, cols), BF16)
    single = pltpu.VMEM((rows, cols), BF16)
    scored = pltpu.VMEM((groups, 5 * rows, wide), F32)
    stats = pltpu.VMEM((groups, 8, wide), F32)
    bits = pltpu.VMEM((groups, 8, 3 * rows), BF16)
    pairs = (dma((groups, 2)),) * 2
    ones = (dma((groups,)),) * 2
    outs = pl.pallas_call(
        functools.partial(fused_kernel, blks, rows, cols),
        out_shape=(pltpu.VMEM((rows, cols), BF16),) * 7,
        in_specs=[pl.BlockSpec(memory_space=pl.ANY)] * 9,
        out_specs=(pl.BlockSpec(memory_space=pltpu.VMEM),) * 7,
        scratch_shapes=[
            pltpu.SMEM(offsets.shape, jnp.int32),
            pltpu.VMEM((3, 2, rows, cols), BF16),
            narrow, narrow, narrow, narrow, single, single,
            pltpu.VMEM((2,) + key_valid.shape, jnp.int32),
            pltpu.VMEM((4, rows, wide), F32),
            scored, scored, stats, stats,
            pltpu.VMEM((2, 8, rows), F32), bits, bits,
            pltpu.VMEM((3, rows, cols), F32),
            pltpu.VMEM((3, rows, cols), BF16), pltpu.VMEM((3, rows, cols), BF16),
            pltpu.VMEM((2, rows, cols), F32),
            narrow, narrow, narrow, narrow, narrow, single, single, narrow,
            dma((8,)), dma((1,)), dma((1,)),
            dma((groups, 3)), dma((groups, 3)), *pairs,
            dma((2,)), dma((2,)), *ones, *ones,
            *ones, dma((groups, 3)), dma((groups, 3)), *pairs, *pairs,
            *ones, *ones, *ones,
        ],
        compiler_params=pltpu.CompilerParams(collective_id=0, has_side_effects=True),
        name="attend_pairs",
    )(offsets, *values, key_valid)
    outs = pl.pallas_call(
        copy_kernel,
        out_shape=(full,) * 7,
        in_specs=[pl.BlockSpec(memory_space=pl.ANY)] * 7,
        out_specs=(pl.BlockSpec(memory_space=pl.ANY),) * 7,
        scratch_shapes=[dma((7,))],
        compiler_params=pltpu.CompilerParams(vmem_limit_bytes=1 << 20),
        name="hand_over",
    )(*outs)
    return tuple(piece[None] for piece in outs)


def extended(block, sides, width):
    for axis, dim in sides:
        count = lax.axis_size(axis)
        forward = [(i, i + 1) for i in range(count - 1)]
        backward = [(target, source) for source, target in forward]
        low = lax.ppermute(
            lax.slice_in_dim(block, block.shape[dim] - width, None, axis=dim), axis, forward
        )
        high = lax.ppermute(lax.slice_in_dim(block, 0, width, axis=dim), axis, backward)
        block = jnp.concatenate([low, block, high], axis=dim)
    return block


def swapped(value, axis, bit):
    mask = 2**bit
    pairs = [(source, source ^ mask) for source in range(lax.axis_size(axis))]
    return lax.ppermute(value, axis, pairs)


def passed_along(block, axis, distance):
    devices = range(lax.axis_size(axis))
    route = [(i - distance, i) for i in devices if i - distance in devices]
    return lax.ppermute(block, axis, route)


def attend(query_tile, grad_tile, key_block, value_block, allowed, heads_here):
    score_scale = HEAD ** (-0.5)
    rows_count = query_tile.shape[0]
    keys_count = key_block.shape[0]
    q_heads = query_tile.reshape(rows_count, heads_here, HEAD)
    g_heads = grad_tile.reshape(rows_count, heads_here, HEAD)
    k_heads = key_block.reshape(keys_count, heads_here, HEAD)
    v_heads = value_block.reshape(keys_count, heads_here, HEAD)
    scores = (
        jnp.einsum("qhe,khe->hqk", q_heads, k_heads, preferred_element_type=jnp.float32)
        * score_scale
    )
    scores = jnp.where(allowed[None], scores, -1e30)
    row_max = jnp.max(scores, axis=2)
    unnormed = jnp.exp(scores - row_max[:, :, None])
    row_sum = jnp.sum(unnormed, axis=2)
    weights = unnormed / row_sum[:, :, None]
    prob_bf = weights.astype(jnp.bfloat16)
    result = jnp.einsum(
        "hqk,khe->qhe", prob_bf, v_heads, preferred_element_type=jnp.float32
    ).reshape(rows_count, -1)
    grad_probs = jnp.einsum("qhe,khe->hqk", g_heads, v_heads, preferred_element_type=jnp.float32)
    row_dot = jnp.sum(weights * grad_probs, axis=2)
    grad_scores = (weights * (grad_probs - row_dot[:, :, None]) * score_scale).astype(jnp.bfloat16)
    grad_query = jnp.einsum(
        "hqk,khe->qhe", grad_scores, k_heads, preferred_element_type=jnp.float32
    ).reshape(rows_count, -1)
    grad_key = jnp.einsum(
        "hqk,qhe->khe", grad_scores, q_heads, preferred_element_type=jnp.float32
    ).reshape(keys_count, -1)
    grad_value = jnp.einsum(
        "hqk,qhe->khe", prob_bf, g_heads, preferred_element_type=jnp.float32
    ).reshape(keys_count, -1)
    return (result, grad_query, grad_key, grad_value, jnp.stack((row_max, row_sum, row_dot)))


def shards(
    queries,
    key_rows,
    value_rows,
    cross_queries,
    cross_keys,
    cross_values,
    grad_out,
    offsets,
    key_valid,
):
    seq_count = lax.axis_size("seq")
    heads_here = HEADS // seq_count
    local_rows = (
        queries[0],
        key_rows[0],
        value_rows[0],
        cross_queries[0],
        cross_keys[0],
        cross_values[0],
        grad_out[0],
    )
    query_here, key_here, value_here, cross_query, cross_key, cross_value, cotangent = (
        lax.all_to_all(local_rows[0], "seq", split_axis=1, concat_axis=0, tiled=True),
        lax.all_to_all(local_rows[1], "seq", split_axis=1, concat_axis=0, tiled=True),
        lax.all_to_all(local_rows[2], "seq", split_axis=1, concat_axis=0, tiled=True),
        lax.all_to_all(local_rows[3], "seq", split_axis=1, concat_axis=0, tiled=True),
        lax.all_to_all(local_rows[4], "seq", split_axis=1, concat_axis=0, tiled=True),
        lax.all_to_all(local_rows[5], "seq", split_axis=1, concat_axis=0, tiled=True),
        lax.all_to_all(local_rows[6], "seq", split_axis=1, concat_axis=0, tiled=True),
    )
    block_len = query_here.shape[0]
    columns = query_here.shape[1]
    half_width = min(WINDOW // 2, block_len // 2)
    tile_rows = min(TILE, block_len)
    tile_count = block_len // tile_rows
    window_span = tile_rows + 2 * half_width
    tower_id = lax.axis_index("tower")
    block_id = lax.axis_index("blk")
    block_mask = lax.all_gather(key_valid, "seq", axis=1, tiled=True)
    mask_ext = extended(block_mask, (("blk", 1),), half_width)
    self_valid = lax.dynamic_index_in_dim(mask_ext, tower_id, 0, keepdims=False)
    other_valid = lax.dynamic_index_in_dim(mask_ext, 1 - tower_id, 0, keepdims=False)
    pair_ext = extended(jnp.stack((key_here, value_here)), (("blk", 1),), half_width)
    partner = swapped(jnp.stack((cross_key, cross_value)), "tower", 0)
    partner_ext = extended(partner, (("blk", 1),), half_width)
    align_shift = offsets[tower_id, block_id]
    band_start = half_width + align_shift
    band = lax.dynamic_slice_in_dim(partner_ext, band_start, block_len, 1)
    band_valid = lax.dynamic_slice_in_dim(other_valid, band_start, block_len) > 0
    rows_local = jnp.arange(tile_rows)
    keys_local = jnp.arange(window_span)
    near = jnp.abs(rows_local[:, None] + half_width - keys_local[None, :]) <= half_width

    def self_step(carry, tile_index):
        grad_key_acc, grad_value_acc = carry
        tile_start = tile_index * tile_rows
        query_tile = lax.dynamic_slice_in_dim(query_here, tile_start, tile_rows, 0)
        grad_tile = lax.dynamic_slice_in_dim(cotangent, tile_start, tile_rows, 0)
        key_window = lax.dynamic_slice_in_dim(pair_ext[0], tile_start, window_span, 0)
        value_window = lax.dynamic_slice_in_dim(pair_ext[1], tile_start, window_span, 0)
        allowed = (
            near & (lax.dynamic_slice_in_dim(self_valid, tile_start, window_span) > 0)[None, :]
        )
        result, grad_query, grad_key, grad_value, stats = attend(
            query_tile, grad_tile, key_window, value_window, allowed, heads_here
        )
        grad_key_acc = lax.dynamic_update_slice_in_dim(
            grad_key_acc,
            lax.dynamic_slice_in_dim(grad_key_acc, tile_start, window_span, 0) + grad_key,
            tile_start,
            0,
        )
        grad_value_acc = lax.dynamic_update_slice_in_dim(
            grad_value_acc,
            lax.dynamic_slice_in_dim(grad_value_acc, tile_start, window_span, 0) + grad_value,
            tile_start,
            0,
        )
        return ((grad_key_acc, grad_value_acc), (result, grad_query, stats))

    def cross_step(carry, tile_index):
        grad_key_acc, grad_value_acc = carry
        tile_start = tile_index * tile_rows
        query_tile = lax.dynamic_slice_in_dim(cross_query, tile_start, tile_rows, 0)
        grad_tile = lax.dynamic_slice_in_dim(cotangent, tile_start, tile_rows, 0)
        result, grad_query, grad_key, grad_value, stats = attend(
            query_tile, grad_tile, band[0], band[1], band_valid[None, :], heads_here
        )
        return ((grad_key_acc + grad_key, grad_value_acc + grad_value), (result, grad_query))

    zeros_ext = jnp.zeros((block_len + 2 * half_width, columns), jnp.float32)
    zeros_band = jnp.zeros((block_len, columns), jnp.float32)
    tile_ids = jnp.arange(tile_count)
    (self_gk, self_gv), (self_out, self_gq, self_stats) = lax.scan(
        self_step, (zeros_ext, zeros_ext), tile_ids
    )
    (cross_gk, cross_gv), (cross_out, cross_gq) = lax.scan(
        cross_step, (zeros_band, zeros_band), tile_ids
    )
    self_out = self_out.reshape(block_len, columns)
    cross_out = cross_out.reshape(block_len, columns)
    self_stats = jnp.transpose(self_stats, (1, 2, 0, 3)).reshape(3, heads_here, block_len)
    attended = (self_out + cross_out).astype(jnp.bfloat16)
    cross_ext = jnp.zeros((2, block_len + 2 * half_width, columns), jnp.float32)
    cross_ext = lax.dynamic_update_slice_in_dim(
        cross_ext, jnp.stack((cross_gk, cross_gv)), band_start, 1
    )
    self_ext = jnp.stack((self_gk, self_gv))
    self_core = self_ext[:, half_width : half_width + block_len]
    cross_core = cross_ext[:, half_width : half_width + block_len]
    upper_cut = block_len - half_width
    lower_send = jnp.concatenate((self_ext[:, :half_width], cross_ext[:, :half_width]), 0)
    upper_send = jnp.concatenate(
        (self_ext[:, block_len + half_width :], cross_ext[:, block_len + half_width :]), 0
    )
    from_above = passed_along(lower_send.astype(jnp.bfloat16), "blk", -1).astype(lower_send.dtype)
    from_below = passed_along(upper_send.astype(jnp.bfloat16), "blk", 1).astype(upper_send.dtype)
    self_core = (
        self_core.at[:, upper_cut:].add(from_above[:2]).at[:, :half_width].add(from_below[:2])
    )
    cross_core = (
        cross_core.at[:, upper_cut:].add(from_above[2:]).at[:, :half_width].add(from_below[2:])
    )
    returned = swapped(cross_core.astype(jnp.bfloat16), "tower", 0)
    head_outs = (
        attended,
        self_gq.reshape(block_len, columns).astype(jnp.bfloat16),
        self_core[0].astype(jnp.bfloat16),
        self_core[1].astype(jnp.bfloat16),
        cross_gq.reshape(block_len, columns).astype(jnp.bfloat16),
        returned[0],
        returned[1],
    )
    token_outs = (
        lax.all_to_all(head_outs[0], "seq", split_axis=0, concat_axis=1, tiled=True),
        lax.all_to_all(head_outs[1], "seq", split_axis=0, concat_axis=1, tiled=True),
        lax.all_to_all(head_outs[2], "seq", split_axis=0, concat_axis=1, tiled=True),
        lax.all_to_all(head_outs[3], "seq", split_axis=0, concat_axis=1, tiled=True),
        lax.all_to_all(head_outs[4], "seq", split_axis=0, concat_axis=1, tiled=True),
        lax.all_to_all(head_outs[5], "seq", split_axis=0, concat_axis=1, tiled=True),
        lax.all_to_all(head_outs[6], "seq", split_axis=0, concat_axis=1, tiled=True),
    )
    return tuple((piece[None] for piece in token_outs))


def solution(mesh):
    in_specs = (
        P("tower", ("blk", "seq"), None),
        P("tower", ("blk", "seq"), None),
        P("tower", ("blk", "seq"), None),
        P("tower", ("blk", "seq"), None),
        P("tower", ("blk", "seq"), None),
        P("tower", ("blk", "seq"), None),
        P("tower", ("blk", "seq"), None),
        P(),
        P(None, ("blk", "seq")),
    )
    out_specs = (
        P("tower", ("blk", "seq"), None),
        P("tower", ("blk", "seq"), None),
        P("tower", ("blk", "seq"), None),
        P("tower", ("blk", "seq"), None),
        P("tower", ("blk", "seq"), None),
        P("tower", ("blk", "seq"), None),
        P("tower", ("blk", "seq"), None),
    )
    body = paired if mesh.shape["seq"] == 2 else shards
    return jax.shard_map(body, mesh=mesh, in_specs=in_specs, out_specs=out_specs, check_vma=False)
```
